256 devices in a mesh: sta: 64 (over z, y, x_hi), seg: 4 (over x_lo, core).
Axes of the slice: x: 4 (x_hi: 2, x_lo: 2; x = x_hi * 2 + x_lo), y: 4, z: 8, core: 2. Of those that a mesh axis runs over, the one named last changes fastest.
Arguments:
- records: float32 [1024, 16, 2048], P('sta', 'seg'), as said below
- plan: int32 [4, 64], replicated, may hold values from 0 to 63, as said below
Outputs:
- correlations: float32 [2048, 4, 16384], P('seg', None, 'sta')
The draws below stay inside these ranges and needn't reach their ends.
Inputs may be any that keep to these rules, and one draw needn't show every extreme that they name: Row r pairs the 64 blocks: plan[r, plan[r, b]] = b and plan[r, b] != b; no two rows pair the same two blocks. `records`: raw ground-motion samples.
All inputs are finite; a program needn't handle non-finite values.
Results may differ from the reference program's by a relative error of at most 0.0075.
Values may be sent and summed in bfloat16 or wider, within the bound.
A program may use at most 128 MiB of HBM per device.

```python
import math
import jax
import jax.numpy as jnp
from jax import lax

S = 16
NWIN = 4
WLEN = 2048
NBIN = 1024
HALF = 64
ROUNDS = 4
NB = 64
STATIONS = 1024
WINS = 16
LAGS = 2048
N_SEG = 4


def draw_records(key, part):
    subkeys = jax.random.split(key, 7)
    noise_part = jax.random.normal(subkeys[0], (STATIONS, WINS, WLEN), jnp.float32)
    top_env = 10.0
    common_weight = 0.1
    envelope = jnp.exp(jax.random.uniform(subkeys[1], (STATIONS, WINS, WLEN // 128), jnp.float32, 0.0, math.log(top_env)))
    envelope = jnp.repeat(envelope, 128, axis=2)
    delay_reach = WLEN // 2
    source = jax.random.normal(subkeys[2], (WINS, WLEN + delay_reach), jnp.float32)
    delays = jax.random.randint(subkeys[3], (STATIONS,), 0, delay_reach).astype(jnp.int32)
    position = jnp.arange(WLEN, dtype=jnp.int32)
    shared = source[:, position[None, :] + delays[:, None]]
    shared = jnp.transpose(shared, (1, 0, 2))
    loudness = jnp.exp(jax.random.uniform(subkeys[4], (STATIONS, 1, 1), jnp.float32, 0.0, math.log(5.0)))
    frequency = jax.random.uniform(subkeys[5], (STATIONS, 1, 1), jnp.float32, 0.5, 3.0)
    offset = jax.random.uniform(subkeys[6], (STATIONS, WINS, 1), jnp.float32, -math.pi, math.pi)
    tone_part = loudness * jnp.sin(2.0 * math.pi * frequency * position.astype(jnp.float32)[None, None, :] / 40.0 + offset)
    return envelope * (noise_part + common_weight * shared) + tone_part


def draw_plan(key, part):
    first_key, second_key = jax.random.split(key)
    labels = jax.random.permutation(first_key, NB).astype(jnp.int32)
    picked = jax.random.permutation(second_key, NB - 1)[:ROUNDS].astype(jnp.int32)
    slot_index = jnp.arange(NB, dtype=jnp.int32)

    def one_round(round_pivot):
        mirror = jnp.mod(2 * round_pivot - slot_index, NB - 1)
        partner = jnp.where(slot_index == NB - 1, round_pivot, jnp.where(slot_index == round_pivot, NB - 1, mirror))
        return jnp.zeros((NB,), jnp.int32).at[labels].set(labels[partner])
    return jax.vmap(one_round)(picked).astype(jnp.int32)


def setup_inputs(seed: int = 0) -> dict:
    arg_keys = jax.random.split(jax.random.key(seed), 3)
    return {
        "records": draw_records(jax.random.fold_in(arg_keys[2], 71), 0),
        "plan": draw_plan(jax.random.fold_in(arg_keys[2], 71), 0),
    }


def band_mean(values, half_width):
    row_count, length = values.shape
    block_width = 2 * half_width
    blocks_count = length // block_width
    inside = jnp.arange(block_width, dtype=jnp.int32)
    source = inside[:, None]
    target = inside[None, :]
    inner_band = (jnp.abs(source - target) <= half_width).astype(jnp.bfloat16)
    before = (target + block_width - source <= half_width).astype(jnp.bfloat16)
    after_band = (source + block_width - target <= half_width).astype(jnp.bfloat16)
    blocks = values.reshape(row_count, blocks_count, block_width)
    earlier = jnp.pad(blocks[:, :-1], ((0, 0), (1, 0), (0, 0)))
    following = jnp.pad(blocks[:, 1:], ((0, 0), (0, 1), (0, 0)))
    flat_shape = (row_count * blocks_count, block_width)
    running = jnp.dot(blocks.reshape(flat_shape), inner_band, preferred_element_type=jnp.float32)
    running = running + jnp.dot(earlier.reshape(flat_shape), before, preferred_element_type=jnp.float32)
    running = running + jnp.dot(following.reshape(flat_shape), after_band, preferred_element_type=jnp.float32)
    position = jnp.arange(length, dtype=jnp.int32)
    counted = (jnp.minimum(position, half_width) + jnp.minimum(length - 1 - position, half_width) + 1).astype(jnp.float32)
    return running.reshape(row_count, length) / counted

def forward_table(first_bin, bin_count, length, transform):
    samples = jnp.arange(length, dtype=jnp.int32)
    bin_index = first_bin + jnp.arange(bin_count, dtype=jnp.int32)
    phase_int = samples[:, None] * bin_index[None, :] % transform
    angles = phase_int.astype(jnp.float32) * (2.0 * math.pi / transform)
    return jnp.concatenate([jnp.cos(angles), -jnp.sin(angles)], axis=1).astype(jnp.bfloat16)

def lag_table(first_lag, lag_count, bin_total, transform):
    lag_index = first_lag + jnp.arange(lag_count, dtype=jnp.int32)
    bin_index = jnp.arange(bin_total, dtype=jnp.int32)
    phase_int = lag_index[:, None] * bin_index[None, :] % transform
    angles = phase_int.astype(jnp.float32) * (2.0 * math.pi / transform)
    weight = jnp.where(bin_index == 0, 1.0, 2.0).astype(jnp.float32)[None, :]
    paired = jnp.stack([weight * jnp.cos(angles), -weight * jnp.sin(angles)], axis=2)
    return paired.reshape(lag_count, 2 * bin_total).astype(jnp.bfloat16)

def reference(records, plan):
    fourier = forward_table(0, NBIN, WLEN, 2 * WLEN)

    def prepare(block):
        signal = block.reshape(S * WINS, WLEN)
        mean_level = band_mean(jnp.abs(signal).astype(jnp.bfloat16), HALF)
        flattened = (signal / (mean_level + 1e-05)).astype(jnp.bfloat16)
        product = jnp.dot(flattened, fourier, preferred_element_type=jnp.float32)
        spec_real = product[:, :NBIN]
        spec_imag = product[:, NBIN:]
        magnitude = jnp.sqrt(spec_real * spec_real + spec_imag * spec_imag).astype(jnp.bfloat16)
        smooth = band_mean(magnitude, HALF)
        whitened = jnp.stack([spec_real / (smooth + 1e-06), spec_imag / (smooth + 1e-06)], axis=1).astype(jnp.bfloat16)
        return whitened.reshape(S, WINS, 2, NBIN)
    whitened = lax.map(prepare, records.reshape(NB, S, WINS, WLEN))
    inverse = lax.optimization_barrier(lag_table(0, LAGS, NBIN, 2 * WLEN)).astype(jnp.float32)
    scaling = 1.0 / math.sqrt(4.0 * NBIN * WINS)

    def round_corr(partners):

        def pair_block(block_index):
            own_block = whitened[block_index].astype(jnp.float32).reshape(S, N_SEG, NWIN, 2, NBIN)
            partner = whitened[partners[block_index]].astype(jnp.float32).reshape(S, N_SEG, NWIN, 2, NBIN)
            turned = jnp.stack([-partner[:, :, :, 1], partner[:, :, :, 0]], axis=3)
            real_cross = jnp.einsum('sgwck,tgwck->gkst', own_block, partner, precision=lax.Precision.HIGHEST)
            imag_cross = jnp.einsum('sgwck,tgwck->gkst', own_block, turned, precision=lax.Precision.HIGHEST)
            crossed = jnp.stack([real_cross, imag_cross], axis=2).astype(jnp.bfloat16)
            crossed = lax.optimization_barrier(crossed).astype(jnp.float32)
            return lax.optimization_barrier(jnp.sum(crossed, axis=0)).reshape(2 * NBIN, S * S)
        blocks = lax.map(pair_block, jnp.arange(NB, dtype=jnp.int32))
        operand = jnp.transpose(blocks, (1, 0, 2)).reshape(2 * NBIN, NB * S * S)
        return jnp.dot(inverse, operand, precision=lax.Precision.HIGHEST, preferred_element_type=jnp.float32) * scaling
    lagged = lax.map(round_corr, plan)
    return jnp.transpose(lagged, (1, 0, 2))
```

```python
import math

import jax
import jax.numpy as jnp
from jax import lax
from jax.sharding import PartitionSpec as P

WLEN = 2048
NBIN = 1024
HALF = 64
ROUNDS = 4
LAGS = 2048


def band_mean(values, half_width):
    row_count, length = values.shape
    block_width = 2 * half_width
    blocks_count = length // block_width
    inside = jnp.arange(block_width, dtype=jnp.int32)
    source = inside[:, None]
    target = inside[None, :]
    inner_band = (jnp.abs(source - target) <= half_width).astype(jnp.bfloat16)
    before = (target + block_width - source <= half_width).astype(jnp.bfloat16)
    after_band = (source + block_width - target <= half_width).astype(jnp.bfloat16)
    blocks = values.reshape(row_count, blocks_count, block_width)
    earlier = jnp.pad(blocks[:, :-1], ((0, 0), (1, 0), (0, 0)))
    following = jnp.pad(blocks[:, 1:], ((0, 0), (0, 1), (0, 0)))
    flat_shape = (row_count * blocks_count, block_width)
    running = jnp.dot(blocks.reshape(flat_shape), inner_band, preferred_element_type=jnp.float32)
    running = running + jnp.dot(
        earlier.reshape(flat_shape), before, preferred_element_type=jnp.float32
    )
    running = running + jnp.dot(
        following.reshape(flat_shape), after_band, preferred_element_type=jnp.float32
    )
    position = jnp.arange(length, dtype=jnp.int32)
    counted = (
        jnp.minimum(position, half_width) + jnp.minimum(length - 1 - position, half_width) + 1
    ).astype(jnp.float32)
    return running.reshape(row_count, length) / counted


def angles_of(rows, step, bins, transform):
    phase_int = (rows[:, None] * step) * bins[None, :] % transform
    return phase_int.astype(jnp.float32) * (2.0 * math.pi / transform)


def fourier_table(length, bin_count, transform):
    low_count = 64
    high_count = length // low_count
    bins = jnp.arange(bin_count, dtype=jnp.int32)
    high = angles_of(jnp.arange(high_count, dtype=jnp.int32), low_count, bins, transform)
    low = angles_of(jnp.arange(low_count, dtype=jnp.int32), 1, bins, transform)
    hc, hs = jnp.cos(high)[:, None], jnp.sin(high)[:, None]
    lc, ls = jnp.cos(low)[None], jnp.sin(low)[None]
    cos_part = hc * lc - hs * ls
    sin_part = hs * lc + hc * ls
    table = jnp.stack([cos_part, -sin_part], axis=2).astype(jnp.bfloat16)
    return table.reshape(length, 2 * bin_count)


def per_device(records, plan):
    stations_dev, windows, length = records.shape
    sta_devices = lax.axis_size("sta")
    seg_devices = lax.axis_size("seg")
    transform = 2 * length
    row_count = stations_dev * windows
    table = fourier_table(length, NBIN, transform)
    signal = records.reshape(row_count, length)
    mean_level = band_mean(jnp.abs(signal).astype(jnp.bfloat16), HALF)
    flattened = (signal / (mean_level + 1e-05)).astype(jnp.bfloat16)
    product = jnp.dot(flattened, table, preferred_element_type=jnp.float32)
    spec_real = product[:, :NBIN]
    spec_imag = product[:, NBIN:]
    magnitude = jnp.sqrt(spec_real * spec_real + spec_imag * spec_imag).astype(jnp.bfloat16)
    smooth = band_mean(magnitude, HALF)
    whitened = jnp.stack(
        [spec_real / (smooth + 1e-06), spec_imag / (smooth + 1e-06)], axis=0
    ).astype(jnp.bfloat16)
    whitened = whitened.reshape(2, stations_dev, windows, NBIN)
    quarter = NBIN // seg_devices
    own = lax.all_to_all(whitened, "seg", split_axis=3, concat_axis=2, tiled=True)
    all_windows = windows * seg_devices
    chunk = quarter // sta_devices
    own_chunks = own.reshape(2, stations_dev, all_windows, sta_devices, chunk)
    own_chunks = jnp.transpose(own_chunks, (3, 0, 1, 2, 4))
    spread = lax.all_to_all(own_chunks, "sta", split_axis=0, concat_axis=0, tiled=True)
    partners = jnp.stack([jnp.take(spread, plan[number], axis=0) for number in range(ROUNDS)], axis=1)
    partner = lax.all_to_all(partners, "sta", split_axis=0, concat_axis=0, tiled=True)
    partner = jnp.transpose(partner, (1, 2, 3, 4, 0, 5)).reshape(
        ROUNDS, 2, stations_dev, all_windows, quarter
    )
    own_f = own.astype(jnp.float32)
    other = partner.astype(jnp.float32)
    own_real = own_f[0][None, :, None]
    own_imag = own_f[1][None, :, None]
    other_real = other[:, 0][:, None]
    other_imag = other[:, 1][:, None]
    real_cross = jnp.sum(own_real * other_real + own_imag * other_imag, axis=3)
    imag_cross = jnp.sum(own_imag * other_real - own_real * other_imag, axis=3)
    square = stations_dev * stations_dev
    crossed = jnp.stack([real_cross, imag_cross], axis=1).astype(jnp.bfloat16)
    crossed = crossed.reshape(ROUNDS, 2, square, quarter)
    mine = lax.all_to_all(crossed, "seg", split_axis=0, concat_axis=3, tiled=True)
    mine = mine.reshape(2, square, NBIN)
    weight = jnp.where(jnp.arange(NBIN) == 0, 1.0, 2.0).astype(jnp.bfloat16)
    mine = mine * weight
    scaling = 1.0 / math.sqrt(4.0 * NBIN * all_windows)
    lagged = lax.dot_general(
        table.reshape(LAGS, 2, NBIN), mine, (((1, 2), (0, 2)), ((), ())),
        preferred_element_type=jnp.float32,
    ) * scaling
    lagged = lagged.reshape(LAGS, 1, square)
    return lax.all_to_all(lagged, "seg", split_axis=0, concat_axis=1, tiled=True)


def solution(mesh):
    in_specs = (P("sta", "seg", None), P())
    out_specs = P("seg", None, "sta")
    return jax.shard_map(
        per_device, mesh=mesh, in_specs=in_specs, out_specs=out_specs, check_vma=False
    )
```

```python
import math

import jax
import jax.numpy as jnp
from jax import lax
from jax.experimental import pallas as pl
from jax.sharding import PartitionSpec as P

WLEN = 2048
NBIN = 1024
HALF = 64
ROUNDS = 4
LAGS = 2048


def band_mean(values, half_width):
    row_count, length = values.shape
    block_width = 2 * half_width
    blocks_count = length // block_width
    inside = jnp.arange(block_width, dtype=jnp.int32)
    source = inside[:, None]
    target = inside[None, :]
    inner_band = (jnp.abs(source - target) <= half_width).astype(jnp.bfloat16)
    before = (target + block_width - source <= half_width).astype(jnp.bfloat16)
    after_band = (source + block_width - target <= half_width).astype(jnp.bfloat16)
    blocks = values.reshape(row_count, blocks_count, block_width)
    earlier = jnp.pad(blocks[:, :-1], ((0, 0), (1, 0), (0, 0)))
    following = jnp.pad(blocks[:, 1:], ((0, 0), (0, 1), (0, 0)))
    flat_shape = (row_count * blocks_count, block_width)
    running = jnp.dot(blocks.reshape(flat_shape), inner_band, preferred_element_type=jnp.float32)
    running = running + jnp.dot(
        earlier.reshape(flat_shape), before, preferred_element_type=jnp.float32
    )
    running = running + jnp.dot(
        following.reshape(flat_shape), after_band, preferred_element_type=jnp.float32
    )
    position = jnp.arange(length, dtype=jnp.int32)
    counted = (
        jnp.minimum(position, half_width) + jnp.minimum(length - 1 - position, half_width) + 1
    ).astype(jnp.float32)
    return running.reshape(row_count, length) / counted


def angles_of(rows, step, bins, transform):
    phase_int = (rows[:, None] * step) * bins[None, :] % transform
    return phase_int.astype(jnp.float32) * (2.0 * math.pi / transform)


def fourier_tables(length, bin_count, transform):
    low_count = 64
    high_count = length // low_count
    bins = jnp.arange(bin_count, dtype=jnp.int32)
    high = angles_of(jnp.arange(high_count, dtype=jnp.int32), low_count, bins, transform)
    low = angles_of(jnp.arange(low_count, dtype=jnp.int32), 1, bins, transform)
    hc, hs = jnp.cos(high)[:, None], jnp.sin(high)[:, None]
    lc, ls = jnp.cos(low)[None], jnp.sin(low)[None]
    cos_part = (hc * lc - hs * ls).astype(jnp.bfloat16).reshape(length, bin_count)
    sin_part = (-(hs * lc + hc * ls)).astype(jnp.bfloat16).reshape(length, bin_count)
    return cos_part, sin_part


def cross_kernel(weight_ref, own_ref, other_ref, out_ref):
    windows = own_ref.shape[1]
    stations = own_ref.shape[2]
    group = 4
    weight = weight_ref[...]

    def body(index, carry):
        first = index * group
        acc_re = [None] * group
        acc_im = [None] * group
        for w in range(windows):
            pre = other_ref[0, 0, w].astype(jnp.float32)
            pim = other_ref[0, 1, w].astype(jnp.float32)
            for g in range(group):
                ore = own_ref[0, w, pl.ds(first + g, 1), :]
                oim = own_ref[1, w, pl.ds(first + g, 1), :]
                re = ore * pre + oim * pim
                im = oim * pre - ore * pim
                acc_re[g] = re if w == 0 else acc_re[g] + re
                acc_im[g] = im if w == 0 else acc_im[g] + im
        for g in range(group):
            out_ref[0, 0, first + g] = (acc_re[g] * weight).astype(out_ref.dtype)
            out_ref[0, 1, first + g] = (acc_im[g] * weight).astype(out_ref.dtype)
        return carry

    lax.fori_loop(0, stations // group, body, 0)


def cross_spectra(weight, own, other):
    rounds, _, windows, stations, bins = other.shape
    return pl.pallas_call(
        cross_kernel,
        grid=(rounds,),
        in_specs=[
            pl.BlockSpec((1, bins), lambda r: (0, 0)),
            pl.BlockSpec(own.shape, lambda r: (0, 0, 0, 0)),
            pl.BlockSpec((1, 2, windows, stations, bins), lambda r: (r, 0, 0, 0, 0)),
        ],
        out_specs=pl.BlockSpec((1, 2, stations, stations, bins), lambda r: (r, 0, 0, 0, 0)),
        out_shape=jax.ShapeDtypeStruct((rounds, 2, stations, stations, bins), jnp.bfloat16),
    )(weight, own, other)


def per_device(records, plan):
    stations_dev, windows, length = records.shape
    sta_devices = lax.axis_size("sta")
    seg_devices = lax.axis_size("seg")
    transform = 2 * length
    row_count = stations_dev * windows
    cos_table, sin_table = fourier_tables(length, NBIN, transform)
    signal = jnp.transpose(records, (1, 0, 2)).reshape(row_count, length)
    mean_level = band_mean(jnp.abs(signal).astype(jnp.bfloat16), HALF)
    flattened = (signal / (mean_level + 1e-05)).astype(jnp.bfloat16)
    spec_real = jnp.dot(flattened, cos_table, preferred_element_type=jnp.float32)
    spec_imag = jnp.dot(flattened, sin_table, preferred_element_type=jnp.float32)
    magnitude = jnp.sqrt(spec_real * spec_real + spec_imag * spec_imag).astype(jnp.bfloat16)
    smooth = band_mean(magnitude, HALF)
    whitened = jnp.stack(
        [spec_real / (smooth + 1e-06), spec_imag / (smooth + 1e-06)], axis=0
    ).astype(jnp.bfloat16)
    whitened = whitened.reshape(2, windows, stations_dev, NBIN)
    quarter = NBIN // seg_devices
    own = lax.all_to_all(whitened, "seg", split_axis=3, concat_axis=1, tiled=True)
    all_windows = windows * seg_devices
    low = 2 * all_windows * stations_dev // sta_devices
    own_chunks = own.reshape(sta_devices, low, quarter)
    spread = lax.all_to_all(own_chunks, "sta", split_axis=0, concat_axis=0, tiled=True)
    partners = jnp.stack([jnp.take(spread, plan[number], axis=0) for number in range(ROUNDS)], axis=0)
    partner = lax.all_to_all(partners, "sta", split_axis=1, concat_axis=1, tiled=True)
    partner = partner.reshape(ROUNDS, 2, all_windows, stations_dev, quarter)
    first_bin = lax.axis_index("seg") * quarter
    bin_index = first_bin + jnp.arange(quarter, dtype=jnp.int32)
    weight = jnp.where(bin_index == 0, 1.0, 2.0).astype(jnp.float32).reshape(1, quarter)
    crossed = cross_spectra(weight, own.astype(jnp.float32), partner)
    mine = lax.all_to_all(crossed, "seg", split_axis=0, concat_axis=4, tiled=True)
    square = stations_dev * stations_dev
    mine = mine.reshape(2, square, NBIN)
    scaling = 1.0 / math.sqrt(4.0 * NBIN * all_windows)
    contract = (((1,), (1,)), ((), ()))
    lagged = lax.dot_general(cos_table, mine[0], contract, preferred_element_type=jnp.float32)
    lagged = lagged + lax.dot_general(
        sin_table, mine[1], contract, preferred_element_type=jnp.float32
    )
    lagged = (lagged * scaling).reshape(seg_devices, LAGS // seg_devices, square)
    lagged = lax.all_to_all(lagged, "seg", split_axis=0, concat_axis=0, tiled=True)
    return jnp.transpose(lagged, (1, 0, 2))


def solution(mesh):
    in_specs = (P("sta", "seg", None), P())
    out_specs = P("seg", None, "sta")
    return jax.shard_map(
        per_device, mesh=mesh, in_specs=in_specs, out_specs=out_specs, check_vma=False
    )
```

```python
import math

import jax
import jax.numpy as jnp
from jax import lax
from jax.experimental import pallas as pl
from jax.sharding import PartitionSpec as P

WLEN = 2048
NBIN = 1024
HALF = 64
ROUNDS = 4
LAGS = 2048


def band_mean(values, half_width):
    row_count, length = values.shape
    block_width = 2 * half_width
    blocks_count = length // block_width
    inside = jnp.arange(block_width, dtype=jnp.int32)
    source = inside[:, None]
    target = inside[None, :]
    inner_band = (jnp.abs(source - target) <= half_width).astype(jnp.bfloat16)
    before = (target + block_width - source <= half_width).astype(jnp.bfloat16)
    after_band = (source + block_width - target <= half_width).astype(jnp.bfloat16)
    blocks = values.reshape(row_count, blocks_count, block_width)
    earlier = jnp.pad(blocks[:, :-1], ((0, 0), (1, 0), (0, 0)))
    following = jnp.pad(blocks[:, 1:], ((0, 0), (0, 1), (0, 0)))
    flat_shape = (row_count * blocks_count, block_width)
    running = jnp.dot(blocks.reshape(flat_shape), inner_band, preferred_element_type=jnp.float32)
    running = running + jnp.dot(
        earlier.reshape(flat_shape), before, preferred_element_type=jnp.float32
    )
    running = running + jnp.dot(
        following.reshape(flat_shape), after_band, preferred_element_type=jnp.float32
    )
    position = jnp.arange(length, dtype=jnp.int32)
    counted = (
        jnp.minimum(position, half_width) + jnp.minimum(length - 1 - position, half_width) + 1
    ).astype(jnp.float32)
    return running.reshape(row_count, length) / counted


def angles_of(rows, step, bins, transform):
    phase_int = (rows[:, None] * step) * bins[None, :] % transform
    return phase_int.astype(jnp.float32) * (2.0 * math.pi / transform)


def fourier_tables(length, bin_count, transform):
    low_count = 64
    high_count = length // low_count
    bins = jnp.arange(bin_count, dtype=jnp.int32)
    high = angles_of(jnp.arange(high_count, dtype=jnp.int32), low_count, bins, transform)
    low = angles_of(jnp.arange(low_count, dtype=jnp.int32), 1, bins, transform)
    hc, hs = jnp.cos(high)[:, None], jnp.sin(high)[:, None]
    lc, ls = jnp.cos(low)[None], jnp.sin(low)[None]
    cos_part = (hc * lc - hs * ls).astype(jnp.bfloat16).reshape(length, bin_count)
    sin_part = (-(hs * lc + hc * ls)).astype(jnp.bfloat16).reshape(length, bin_count)
    return cos_part, sin_part


def cross_kernel(weight_ref, own_ref, other_ref, out_ref):
    windows = own_ref.shape[1]
    stations = own_ref.shape[2]
    group = 4
    weight = weight_ref[...]

    def body(index, carry):
        first = index * group
        acc_re = [None] * group
        acc_im = [None] * group
        for w in range(windows):
            pre = other_ref[0, 0, w].astype(jnp.float32)
            pim = other_ref[0, 1, w].astype(jnp.float32)
            for g in range(group):
                ore = own_ref[0, w, pl.ds(first + g, 1), :]
                oim = own_ref[1, w, pl.ds(first + g, 1), :]
                re = ore * pre + oim * pim
                im = oim * pre - ore * pim
                acc_re[g] = re if w == 0 else acc_re[g] + re
                acc_im[g] = im if w == 0 else acc_im[g] + im
        for g in range(group):
            out_ref[0, 0, first + g] = (acc_re[g] * weight).astype(out_ref.dtype)
            out_ref[0, 1, first + g] = (acc_im[g] * weight).astype(out_ref.dtype)
        return carry

    lax.fori_loop(0, stations // group, body, 0)


def cross_spectra(weight, own, other):
    rounds, _, windows, stations, bins = other.shape
    return pl.pallas_call(
        cross_kernel,
        grid=(rounds,),
        in_specs=[
            pl.BlockSpec((1, bins), lambda r: (0, 0)),
            pl.BlockSpec(own.shape, lambda r: (0, 0, 0, 0)),
            pl.BlockSpec((1, 2, windows, stations, bins), lambda r: (r, 0, 0, 0, 0)),
        ],
        out_specs=pl.BlockSpec((1, 2, stations, stations, bins), lambda r: (r, 0, 0, 0, 0)),
        out_shape=jax.ShapeDtypeStruct((rounds, 2, stations, stations, bins), jnp.bfloat16),
    )(weight, own, other)


def per_device(records, plan):
    stations_dev, windows, length = records.shape
    sta_devices = lax.axis_size("sta")
    seg_devices = lax.axis_size("seg")
    transform = 2 * length
    row_count = stations_dev * windows
    cos_table, sin_table = fourier_tables(length, NBIN, transform)
    signal = jnp.transpose(records, (1, 0, 2)).reshape(row_count, length)
    mean_level = band_mean(jnp.abs(signal).astype(jnp.bfloat16), HALF)
    flattened = (signal / (mean_level + 1e-05)).astype(jnp.bfloat16)
    spec_real = jnp.dot(flattened, cos_table, preferred_element_type=jnp.float32)
    spec_imag = jnp.dot(flattened, sin_table, preferred_element_type=jnp.float32)
    magnitude = jnp.sqrt(spec_real * spec_real + spec_imag * spec_imag).astype(jnp.bfloat16)
    smooth = band_mean(magnitude, HALF)
    whitened = jnp.stack(
        [spec_real / (smooth + 1e-06), spec_imag / (smooth + 1e-06)], axis=0
    ).astype(jnp.bfloat16)
    whitened = whitened.reshape(2, windows, stations_dev, NBIN)
    quarter = NBIN // seg_devices
    own = lax.all_to_all(whitened, "seg", split_axis=3, concat_axis=1, tiled=True)
    all_windows = windows * seg_devices
    low = 2 * all_windows * stations_dev // sta_devices
    own_chunks = own.reshape(sta_devices, low, quarter)
    spread = lax.all_to_all(own_chunks, "sta", split_axis=0, concat_axis=0, tiled=True)
    partners = jnp.stack([jnp.take(spread, plan[number], axis=0) for number in range(ROUNDS)], axis=0)
    partner = lax.all_to_all(partners, "sta", split_axis=1, concat_axis=1, tiled=True)
    partner = partner.reshape(ROUNDS, 2, all_windows, stations_dev, quarter)
    first_bin = lax.axis_index("seg") * quarter
    bin_index = first_bin + jnp.arange(quarter, dtype=jnp.int32)
    weight = jnp.where(bin_index == 0, 1.0, 2.0).astype(jnp.float32).reshape(1, quarter)
    crossed = cross_spectra(weight, own.astype(jnp.float32), partner)
    mine = lax.all_to_all(crossed, "seg", split_axis=0, concat_axis=4, tiled=True)
    square = stations_dev * stations_dev
    mine = mine.reshape(2, square, NBIN)
    scaling = 1.0 / math.sqrt(4.0 * NBIN * all_windows)
    contract = (((1,), (1,)), ((), ()))
    lagged = lax.dot_general(cos_table, mine[0], contract, preferred_element_type=jnp.float32)
    lagged = lagged + lax.dot_general(
        sin_table, mine[1], contract, preferred_element_type=jnp.float32
    )
    lagged = (lagged * scaling).astype(jnp.bfloat16).reshape(seg_devices, LAGS // seg_devices, square)
    lagged = lax.all_to_all(lagged, "seg", split_axis=0, concat_axis=0, tiled=True)
    return jnp.transpose(lagged, (1, 0, 2)).astype(jnp.float32)


def solution(mesh):
    in_specs = (P("sta", "seg", None), P())
    out_specs = P("seg", None, "sta")
    return jax.shard_map(
        per_device, mesh=mesh, in_specs=in_specs, out_specs=out_specs, check_vma=False
    )
```

```python
import math

import jax
import jax.numpy as jnp
from jax import lax
from jax.experimental import pallas as pl
from jax.experimental.pallas import tpu as pltpu
from jax.sharding import PartitionSpec as P

WLEN = 2048
NBIN = 1024
HALF = 64
ROUNDS = 4
LAGS = 2048


def band_mean(values, half_width):
    row_count, length = values.shape
    block_width = 2 * half_width
    blocks_count = length // block_width
    inside = jnp.arange(block_width, dtype=jnp.int32)
    source = inside[:, None]
    target = inside[None, :]
    inner_band = (jnp.abs(source - target) <= half_width).astype(jnp.bfloat16)
    before = (target + block_width - source <= half_width).astype(jnp.bfloat16)
    after_band = (source + block_width - target <= half_width).astype(jnp.bfloat16)
    blocks = values.reshape(row_count, blocks_count, block_width)
    earlier = jnp.pad(blocks[:, :-1], ((0, 0), (1, 0), (0, 0)))
    following = jnp.pad(blocks[:, 1:], ((0, 0), (0, 1), (0, 0)))
    flat_shape = (row_count * blocks_count, block_width)
    running = jnp.dot(blocks.reshape(flat_shape), inner_band, preferred_element_type=jnp.float32)
    running = running + jnp.dot(
        earlier.reshape(flat_shape), before, preferred_element_type=jnp.float32
    )
    running = running + jnp.dot(
        following.reshape(flat_shape), after_band, preferred_element_type=jnp.float32
    )
    position = jnp.arange(length, dtype=jnp.int32)
    counted = (
        jnp.minimum(position, half_width) + jnp.minimum(length - 1 - position, half_width) + 1
    ).astype(jnp.float32)
    return running.reshape(row_count, length) / counted


def angles_of(rows, step, bins, transform):
    phase_int = (rows[:, None] * step) * bins[None, :] % transform
    return phase_int.astype(jnp.float32) * (2.0 * math.pi / transform)


def fourier_tables(length, bin_count, transform):
    low_count = 64
    high_count = length // low_count
    bins = jnp.arange(bin_count, dtype=jnp.int32)
    high = angles_of(jnp.arange(high_count, dtype=jnp.int32), low_count, bins, transform)
    low = angles_of(jnp.arange(low_count, dtype=jnp.int32), 1, bins, transform)
    hc, hs = jnp.cos(high)[:, None], jnp.sin(high)[:, None]
    lc, ls = jnp.cos(low)[None], jnp.sin(low)[None]
    cos_part = (hc * lc - hs * ls).astype(jnp.bfloat16).reshape(length, bin_count)
    sin_part = (-(hs * lc + hc * ls)).astype(jnp.bfloat16).reshape(length, bin_count)
    return cos_part, sin_part


def cross_round(weight, own_ref, other_ref, r, dst):
    windows = own_ref.shape[1]
    stations = own_ref.shape[2]
    group = 4

    def body(index, carry):
        first = index * group
        acc_re = [None] * group
        acc_im = [None] * group
        for w in range(windows):
            pre = other_ref[r, 0, w].astype(jnp.float32)
            pim = other_ref[r, 1, w].astype(jnp.float32)
            for g in range(group):
                ore = own_ref[0, w, pl.ds(first + g, 1), :]
                oim = own_ref[1, w, pl.ds(first + g, 1), :]
                re = ore * pre + oim * pim
                im = oim * pre - ore * pim
                acc_re[g] = re if w == 0 else acc_re[g] + re
                acc_im[g] = im if w == 0 else acc_im[g] + im
        for g in range(group):
            dst[0, first + g] = (acc_re[g] * weight).astype(dst.dtype)
            dst[1, first + g] = (acc_im[g] * weight).astype(dst.dtype)
        return carry

    lax.fori_loop(0, stations // group, body, 0)


def cross_kernel(weight_ref, own_ref, other_ref, out_ref, staged, send_sems, recv_sems):
    count = out_ref.shape[0]
    me = lax.axis_index("seg")
    row = lax.axis_index("sta")
    barrier = pltpu.get_barrier_semaphore()
    for step in range(1, count):
        pl.semaphore_signal(
            barrier, inc=1, device_id=(row, lax.rem(me + step, count)),
            device_id_type=pl.DeviceIdType.MESH,
        )
    pl.semaphore_wait(barrier, count - 1)
    weight = weight_ref[...]
    copies = []
    for step in range(count - 1):
        target = lax.rem(me + 1 + step, count)
        cross_round(weight, own_ref, other_ref, target, staged.at[step])
        copy = pltpu.make_async_remote_copy(
            src_ref=staged.at[step],
            dst_ref=out_ref.at[me],
            send_sem=send_sems.at[step],
            recv_sem=recv_sems.at[step],
            device_id=(row, target),
            device_id_type=pl.DeviceIdType.MESH,
        )
        copy.start()
        copies.append(copy)
    cross_round(weight, own_ref, other_ref, me, out_ref.at[me])
    for copy in copies:
        copy.wait()


def cross_spectra(weight, own, other):
    rounds, _, windows, stations, bins = other.shape
    vmem = pl.BlockSpec(memory_space=pltpu.VMEM)
    return pl.pallas_call(
        cross_kernel,
        in_specs=[vmem, vmem, vmem],
        out_specs=vmem,
        out_shape=jax.ShapeDtypeStruct((rounds, 2, stations, stations, bins), jnp.bfloat16),
        scratch_shapes=[
            pltpu.VMEM((rounds - 1, 2, stations, stations, bins), jnp.bfloat16),
            pltpu.SemaphoreType.DMA((rounds - 1,)),
            pltpu.SemaphoreType.DMA((rounds - 1,)),
        ],
        compiler_params=pltpu.CompilerParams(collective_id=0, has_side_effects=True),
    )(weight, own, other)


def per_device(records, plan):
    stations_dev, windows, length = records.shape
    sta_devices = lax.axis_size("sta")
    seg_devices = lax.axis_size("seg")
    transform = 2 * length
    row_count = stations_dev * windows
    cos_table, sin_table = fourier_tables(length, NBIN, transform)
    signal = jnp.transpose(records, (1, 0, 2)).reshape(row_count, length)
    mean_level = band_mean(jnp.abs(signal).astype(jnp.bfloat16), HALF)
    flattened = (signal / (mean_level + 1e-05)).astype(jnp.bfloat16)
    spec_real = jnp.dot(flattened, cos_table, preferred_element_type=jnp.float32)
    spec_imag = jnp.dot(flattened, sin_table, preferred_element_type=jnp.float32)
    magnitude = jnp.sqrt(spec_real * spec_real + spec_imag * spec_imag).astype(jnp.bfloat16)
    smooth = band_mean(magnitude, HALF)
    whitened = jnp.stack(
        [spec_real / (smooth + 1e-06), spec_imag / (smooth + 1e-06)], axis=0
    ).astype(jnp.bfloat16)
    whitened = whitened.reshape(2, windows, stations_dev, NBIN)
    quarter = NBIN // seg_devices
    own = lax.all_to_all(whitened, "seg", split_axis=3, concat_axis=1, tiled=True)
    all_windows = windows * seg_devices
    low = 2 * all_windows * stations_dev // sta_devices
    own_chunks = own.reshape(sta_devices, low, quarter)
    spread = lax.all_to_all(own_chunks, "sta", split_axis=0, concat_axis=0, tiled=True)
    partners = jnp.stack([jnp.take(spread, plan[number], axis=0) for number in range(ROUNDS)], axis=0)
    partner = lax.all_to_all(partners, "sta", split_axis=1, concat_axis=1, tiled=True)
    partner = partner.reshape(ROUNDS, 2, all_windows, stations_dev, quarter)
    first_bin = lax.axis_index("seg") * quarter
    bin_index = first_bin + jnp.arange(quarter, dtype=jnp.int32)
    weight = jnp.where(bin_index == 0, 1.0, 2.0).astype(jnp.float32).reshape(1, quarter)
    crossed = cross_spectra(weight, own.astype(jnp.float32), partner)
    square = stations_dev * stations_dev
    mine = crossed.reshape(seg_devices, 2, square, quarter)
    scaling = 1.0 / math.sqrt(4.0 * NBIN * all_windows)
    contract = (((1, 2), (0, 2)), ((), ()))
    split_table = (LAGS, seg_devices, quarter)
    lagged = lax.dot_general(
        cos_table.reshape(split_table), mine[:, 0], contract, preferred_element_type=jnp.float32
    )
    lagged = lagged + lax.dot_general(
        sin_table.reshape(split_table), mine[:, 1], contract, preferred_element_type=jnp.float32
    )
    lagged = (lagged * scaling).astype(jnp.bfloat16).reshape(seg_devices, LAGS // seg_devices, square)
    lagged = lax.all_to_all(lagged, "seg", split_axis=0, concat_axis=0, tiled=True)
    return jnp.transpose(lagged, (1, 0, 2)).astype(jnp.float32)


def solution(mesh):
    in_specs = (P("sta", "seg", None), P())
    out_specs = P("seg", None, "sta")
    return jax.shard_map(
        per_device, mesh=mesh, in_specs=in_specs, out_specs=out_specs, check_vma=False
    )
```

```python
import functools
import math

import jax
import jax.numpy as jnp
from jax import lax
from jax.experimental import pallas as pl
from jax.experimental.pallas import tpu as pltpu
from jax.sharding import PartitionSpec as P

WLEN = 2048
NBIN = 1024
HALF = 64
ROUNDS = 4
LAGS = 2048


def band_mean(values, half_width):
    row_count, length = values.shape
    block_width = 2 * half_width
    blocks_count = length // block_width
    inside = jnp.arange(block_width, dtype=jnp.int32)
    source = inside[:, None]
    target = inside[None, :]
    inner_band = (jnp.abs(source - target) <= half_width).astype(jnp.bfloat16)
    before = (target + block_width - source <= half_width).astype(jnp.bfloat16)
    after_band = (source + block_width - target <= half_width).astype(jnp.bfloat16)
    blocks = values.reshape(row_count, blocks_count, block_width)
    earlier = jnp.pad(blocks[:, :-1], ((0, 0), (1, 0), (0, 0)))
    following = jnp.pad(blocks[:, 1:], ((0, 0), (0, 1), (0, 0)))
    flat_shape = (row_count * blocks_count, block_width)
    running = jnp.dot(blocks.reshape(flat_shape), inner_band, preferred_element_type=jnp.float32)
    running = running + jnp.dot(
        earlier.reshape(flat_shape), before, preferred_element_type=jnp.float32
    )
    running = running + jnp.dot(
        following.reshape(flat_shape), after_band, preferred_element_type=jnp.float32
    )
    position = jnp.arange(length, dtype=jnp.int32)
    counted = (
        jnp.minimum(position, half_width) + jnp.minimum(length - 1 - position, half_width) + 1
    ).astype(jnp.float32)
    return running.reshape(row_count, length) / counted


def angles_of(rows, step, bins, transform):
    phase_int = (rows[:, None] * step) * bins[None, :] % transform
    return phase_int.astype(jnp.float32) * (2.0 * math.pi / transform)


def fourier_tables(length, bin_count, transform):
    low_count = 64
    high_count = length // low_count
    bins = jnp.arange(bin_count, dtype=jnp.int32)
    high = angles_of(jnp.arange(high_count, dtype=jnp.int32), low_count, bins, transform)
    low = angles_of(jnp.arange(low_count, dtype=jnp.int32), 1, bins, transform)
    hc, hs = jnp.cos(high)[:, None], jnp.sin(high)[:, None]
    lc, ls = jnp.cos(low)[None], jnp.sin(low)[None]
    cos_part = (hc * lc - hs * ls).astype(jnp.bfloat16).reshape(length, bin_count)
    sin_part = (-(hs * lc + hc * ls)).astype(jnp.bfloat16).reshape(length, bin_count)
    return cos_part, sin_part


def cross_round(weight, own_ref, other_ref, r, dst):
    windows = own_ref.shape[1]
    stations = own_ref.shape[2]
    group = 4

    def body(index, carry):
        first = index * group
        acc_re = [None] * group
        acc_im = [None] * group
        for w in range(windows):
            pre = other_ref[r, 0, w].astype(jnp.float32)
            pim = other_ref[r, 1, w].astype(jnp.float32)
            for g in range(group):
                ore = own_ref[0, w, pl.ds(first + g, 1), :]
                oim = own_ref[1, w, pl.ds(first + g, 1), :]
                re = ore * pre + oim * pim
                im = oim * pre - ore * pim
                acc_re[g] = re if w == 0 else acc_re[g] + re
                acc_im[g] = im if w == 0 else acc_im[g] + im
        for g in range(group):
            dst[0, first + g] = (acc_re[g] * weight).astype(dst.dtype)
            dst[1, first + g] = (acc_im[g] * weight).astype(dst.dtype)
        return carry

    lax.fori_loop(0, stations // group, body, 0)


def cross_kernel(weight_ref, own_ref, other_ref, out_ref, staged, send_sems, recv_sems):
    count = out_ref.shape[0]
    me = lax.axis_index("seg")
    row = lax.axis_index("sta")
    barrier = pltpu.get_barrier_semaphore()
    for step in range(1, count):
        pl.semaphore_signal(
            barrier, inc=1, device_id=(row, lax.rem(me + step, count)),
            device_id_type=pl.DeviceIdType.MESH,
        )
    pl.semaphore_wait(barrier, count - 1)
    weight = weight_ref[...]
    copies = []
    for step in range(count - 1):
        target = lax.rem(me + 1 + step, count)
        cross_round(weight, own_ref, other_ref, target, staged.at[step])
        copy = pltpu.make_async_remote_copy(
            src_ref=staged.at[step],
            dst_ref=out_ref.at[me],
            send_sem=send_sems.at[step],
            recv_sem=recv_sems.at[step],
            device_id=(row, target),
            device_id_type=pl.DeviceIdType.MESH,
        )
        copy.start()
        copies.append(copy)
    cross_round(weight, own_ref, other_ref, me, out_ref.at[me])
    for copy in copies:
        copy.wait()


def cross_spectra(weight, own, other):
    rounds, _, windows, stations, bins = other.shape
    vmem = pl.BlockSpec(memory_space=pltpu.VMEM)
    return pl.pallas_call(
        cross_kernel,
        in_specs=[vmem, vmem, vmem],
        out_specs=vmem,
        out_shape=jax.ShapeDtypeStruct((rounds, 2, stations, stations, bins), jnp.bfloat16),
        scratch_shapes=[
            pltpu.VMEM((rounds - 1, 2, stations, stations, bins), jnp.bfloat16),
            pltpu.SemaphoreType.DMA((rounds - 1,)),
            pltpu.SemaphoreType.DMA((rounds - 1,)),
        ],
        compiler_params=pltpu.CompilerParams(collective_id=0, has_side_effects=True),
    )(weight, own, other)


def lag_kernel(scaling, cos_ref, sin_ref, y_ref, out_ref, staged, send_sems, recv_sems):
    count = out_ref.shape[0]
    chunk = out_ref.shape[1]
    quarter = y_ref.shape[3]
    rows = 128
    me = lax.axis_index("seg")
    row = lax.axis_index("sta")
    barrier = pltpu.get_barrier_semaphore()
    for step in range(1, count):
        pl.semaphore_signal(
            barrier, inc=1, device_id=(row, lax.rem(me + step, count)),
            device_id_type=pl.DeviceIdType.MESH,
        )
    pl.semaphore_wait(barrier, count - 1)
    contract = (((1,), (1,)), ((), ()))

    def compute(target, dst):
        def body(index, carry):
            first = pl.multiple_of(target * chunk + index * rows, rows)
            acc = None
            for q in range(count):
                cols = pl.ds(q * quarter, quarter)
                for c, table in enumerate((cos_ref, sin_ref)):
                    part = lax.dot_general(
                        table[pl.ds(first, rows), cols], y_ref[q, c], contract,
                        preferred_element_type=jnp.float32,
                    )
                    acc = part if acc is None else acc + part
            local = pl.multiple_of(index * rows, rows)
            dst[pl.ds(local, rows), :] = (acc * scaling).astype(dst.dtype)
            return carry

        lax.fori_loop(0, chunk // rows, body, 0)

    copies = []
    for step in range(count - 1):
        target = lax.rem(me + 1 + step, count)
        compute(target, staged.at[step])
        copy = pltpu.make_async_remote_copy(
            src_ref=staged.at[step],
            dst_ref=out_ref.at[me],
            send_sem=send_sems.at[step],
            recv_sem=recv_sems.at[step],
            device_id=(row, target),
            device_id_type=pl.DeviceIdType.MESH,
        )
        copy.start()
        copies.append(copy)
    compute(me, out_ref.at[me])
    for copy in copies:
        copy.wait()


def lag_transform(scaling, cos_table, sin_table, mine):
    count, _, square, _ = mine.shape
    chunk = LAGS // count
    vmem = pl.BlockSpec(memory_space=pltpu.VMEM)
    return pl.pallas_call(
        functools.partial(lag_kernel, scaling),
        in_specs=[vmem, vmem, vmem],
        out_specs=vmem,
        out_shape=jax.ShapeDtypeStruct((count, chunk, square), jnp.bfloat16),
        scratch_shapes=[
            pltpu.VMEM((count - 1, chunk, square), jnp.bfloat16),
            pltpu.SemaphoreType.DMA((count - 1,)),
            pltpu.SemaphoreType.DMA((count - 1,)),
        ],
        compiler_params=pltpu.CompilerParams(collective_id=1, has_side_effects=True),
    )(cos_table, sin_table, mine)


def per_device(records, plan):
    stations_dev, windows, length = records.shape
    sta_devices = lax.axis_size("sta")
    seg_devices = lax.axis_size("seg")
    transform = 2 * length
    row_count = stations_dev * windows
    cos_table, sin_table = fourier_tables(length, NBIN, transform)
    signal = jnp.transpose(records, (1, 0, 2)).reshape(row_count, length)
    mean_level = band_mean(jnp.abs(signal).astype(jnp.bfloat16), HALF)
    flattened = (signal / (mean_level + 1e-05)).astype(jnp.bfloat16)
    spec_real = jnp.dot(flattened, cos_table, preferred_element_type=jnp.float32)
    spec_imag = jnp.dot(flattened, sin_table, preferred_element_type=jnp.float32)
    magnitude = jnp.sqrt(spec_real * spec_real + spec_imag * spec_imag).astype(jnp.bfloat16)
    smooth = band_mean(magnitude, HALF)
    whitened = jnp.stack(
        [spec_real / (smooth + 1e-06), spec_imag / (smooth + 1e-06)], axis=0
    ).astype(jnp.bfloat16)
    whitened = whitened.reshape(2, windows, stations_dev, NBIN)
    quarter = NBIN // seg_devices
    own = lax.all_to_all(whitened, "seg", split_axis=3, concat_axis=1, tiled=True)
    all_windows = windows * seg_devices
    low = 2 * all_windows * stations_dev // sta_devices
    own_chunks = own.reshape(sta_devices, low, quarter)
    spread = lax.all_to_all(own_chunks, "sta", split_axis=0, concat_axis=0, tiled=True)
    partners = jnp.stack([jnp.take(spread, plan[number], axis=0) for number in range(ROUNDS)], axis=0)
    partner = lax.all_to_all(partners, "sta", split_axis=1, concat_axis=1, tiled=True)
    partner = partner.reshape(ROUNDS, 2, all_windows, stations_dev, quarter)
    first_bin = lax.axis_index("seg") * quarter
    bin_index = first_bin + jnp.arange(quarter, dtype=jnp.int32)
    weight = jnp.where(bin_index == 0, 1.0, 2.0).astype(jnp.float32).reshape(1, quarter)
    crossed = cross_spectra(weight, own.astype(jnp.float32), partner)
    square = stations_dev * stations_dev
    mine = crossed.reshape(seg_devices, 2, square, quarter)
    scaling = 1.0 / math.sqrt(4.0 * NBIN * all_windows)
    lagged = lag_transform(scaling, cos_table, sin_table, mine)
    return jnp.transpose(lagged, (1, 0, 2)).astype(jnp.float32)


def solution(mesh):
    in_specs = (P("sta", "seg", None), P())
    out_specs = P("seg", None, "sta")
    return jax.shard_map(
        per_device, mesh=mesh, in_specs=in_specs, out_specs=out_specs, check_vma=False
    )
```

```python
import functools
import math

import jax
import jax.numpy as jnp
from jax import lax
from jax.experimental import pallas as pl
from jax.experimental.pallas import tpu as pltpu
from jax.sharding import PartitionSpec as P

WLEN = 2048
NBIN = 1024
HALF = 64
ROUNDS = 4
LAGS = 2048


def band_mean(values, half_width):
    row_count, length = values.shape
    block_width = 2 * half_width
    blocks_count = length // block_width
    inside = jnp.arange(block_width, dtype=jnp.int32)
    source = inside[:, None]
    target = inside[None, :]
    inner_band = (jnp.abs(source - target) <= half_width).astype(jnp.bfloat16)
    before = (target + block_width - source <= half_width).astype(jnp.bfloat16)
    after_band = (source + block_width - target <= half_width).astype(jnp.bfloat16)
    blocks = values.reshape(row_count, blocks_count, block_width)
    earlier = jnp.pad(blocks[:, :-1], ((0, 0), (1, 0), (0, 0)))
    following = jnp.pad(blocks[:, 1:], ((0, 0), (0, 1), (0, 0)))
    flat_shape = (row_count * blocks_count, block_width)
    running = jnp.dot(blocks.reshape(flat_shape), inner_band, preferred_element_type=jnp.float32)
    running = running + jnp.dot(
        earlier.reshape(flat_shape), before, preferred_element_type=jnp.float32
    )
    running = running + jnp.dot(
        following.reshape(flat_shape), after_band, preferred_element_type=jnp.float32
    )
    position = jnp.arange(length, dtype=jnp.int32)
    counted = (
        jnp.minimum(position, half_width) + jnp.minimum(length - 1 - position, half_width) + 1
    ).astype(jnp.float32)
    return running.reshape(row_count, length) / counted


def angles_of(rows, step, bins, transform):
    phase_int = (rows[:, None] * step) * bins[None, :] % transform
    return phase_int.astype(jnp.float32) * (2.0 * math.pi / transform)


def fourier_tables(length, bin_count, transform):
    low_count = 64
    high_count = length // low_count
    bins = jnp.arange(bin_count, dtype=jnp.int32)
    high = angles_of(jnp.arange(high_count, dtype=jnp.int32), low_count, bins, transform)
    low = angles_of(jnp.arange(low_count, dtype=jnp.int32), 1, bins, transform)
    hc, hs = jnp.cos(high)[:, None], jnp.sin(high)[:, None]
    lc, ls = jnp.cos(low)[None], jnp.sin(low)[None]
    cos_part = (hc * lc - hs * ls).astype(jnp.bfloat16).reshape(length, bin_count)
    sin_part = (-(hs * lc + hc * ls)).astype(jnp.bfloat16).reshape(length, bin_count)
    return cos_part, sin_part


def cross_round(weight, own_ref, other_ref, r, dst):
    windows = own_ref.shape[1]
    stations = own_ref.shape[2]
    group = 4

    def body(index, carry):
        first = index * group
        acc_re = [None] * group
        acc_im = [None] * group
        for w in range(windows):
            pre = other_ref[r, 0, w].astype(jnp.float32)
            pim = other_ref[r, 1, w].astype(jnp.float32)
            for g in range(group):
                ore = own_ref[0, w, pl.ds(first + g, 1), :]
                oim = own_ref[1, w, pl.ds(first + g, 1), :]
                re = ore * pre + oim * pim
                im = oim * pre - ore * pim
                acc_re[g] = re if w == 0 else acc_re[g] + re
                acc_im[g] = im if w == 0 else acc_im[g] + im
        for g in range(group):
            dst[0, first + g] = (acc_re[g] * weight).astype(dst.dtype)
            dst[1, first + g] = (acc_im[g] * weight).astype(dst.dtype)
        return carry

    lax.fori_loop(0, stations // group, body, 0)


def cross_kernel(weight_ref, own_ref, other_ref, out_ref, staged, send_sems, recv_sems):
    count = out_ref.shape[0]
    me = lax.axis_index("seg")
    row = lax.axis_index("sta")
    barrier = pltpu.get_barrier_semaphore()
    for step in range(1, count):
        pl.semaphore_signal(
            barrier, inc=1, device_id=(row, lax.rem(me + step, count)),
            device_id_type=pl.DeviceIdType.MESH,
        )
    pl.semaphore_wait(barrier, count - 1)
    weight = weight_ref[...]
    copies = []
    for step in range(count - 1):
        target = lax.rem(me + 1 + step, count)
        cross_round(weight, own_ref, other_ref, target, staged.at[step])
        copy = pltpu.make_async_remote_copy(
            src_ref=staged.at[step],
            dst_ref=out_ref.at[me],
            send_sem=send_sems.at[step],
            recv_sem=recv_sems.at[step],
            device_id=(row, target),
            device_id_type=pl.DeviceIdType.MESH,
        )
        copy.start()
        copies.append(copy)
    cross_round(weight, own_ref, other_ref, me, out_ref.at[me])
    for copy in copies:
        copy.wait()


def cross_spectra(weight, own, other):
    rounds, _, windows, stations, bins = other.shape
    vmem = pl.BlockSpec(memory_space=pltpu.VMEM)
    return pl.pallas_call(
        cross_kernel,
        in_specs=[vmem, vmem, vmem],
        out_specs=vmem,
        out_shape=jax.ShapeDtypeStruct((rounds, 2, stations, stations, bins), jnp.bfloat16),
        scratch_shapes=[
            pltpu.VMEM((rounds - 1, 2, stations, stations, bins), jnp.bfloat16),
            pltpu.SemaphoreType.DMA((rounds - 1,)),
            pltpu.SemaphoreType.DMA((rounds - 1,)),
        ],
        compiler_params=pltpu.CompilerParams(collective_id=0, has_side_effects=True),
    )(weight, own, other)


def lag_kernel(scaling, cos_ref, sin_ref, y_ref, out_ref, staged, send_sems, recv_sems):
    count = out_ref.shape[0]
    chunk = out_ref.shape[1]
    quarter = y_ref.shape[3]
    rows = 128
    me = lax.axis_index("seg")
    row = lax.axis_index("sta")
    barrier = pltpu.get_barrier_semaphore()
    for step in range(1, count):
        pl.semaphore_signal(
            barrier, inc=1, device_id=(row, lax.rem(me + step, count)),
            device_id_type=pl.DeviceIdType.MESH,
        )
    pl.semaphore_wait(barrier, count - 1)
    contract = (((1,), (1,)), ((), ()))

    def compute(target, dst):
        def body(index, carry):
            first = pl.multiple_of(target * chunk + index * rows, rows)
            acc = None
            for q in range(count):
                cols = pl.ds(q * quarter, quarter)
                for c, table in enumerate((cos_ref, sin_ref)):
                    part = lax.dot_general(
                        table[pl.ds(first, rows), cols], y_ref[q, c], contract,
                        preferred_element_type=jnp.float32,
                    )
                    acc = part if acc is None else acc + part
            local = pl.multiple_of(index * rows, rows)
            dst[pl.ds(local, rows), :] = (acc * scaling).astype(dst.dtype)
            return carry

        lax.fori_loop(0, chunk // rows, body, 0)

    copies = []
    for step in range(count - 1):
        target = lax.rem(me + 1 + step, count)
        compute(target, staged.at[step])
        copy = pltpu.make_async_remote_copy(
            src_ref=staged.at[step],
            dst_ref=out_ref.at[me],
            send_sem=send_sems.at[step],
            recv_sem=recv_sems.at[step],
            device_id=(row, target),
            device_id_type=pl.DeviceIdType.MESH,
        )
        copy.start()
        copies.append(copy)
    compute(me, out_ref.at[me])
    for copy in copies:
        copy.wait()


def lag_transform(scaling, cos_table, sin_table, mine):
    count, _, square, _ = mine.shape
    chunk = LAGS // count
    vmem = pl.BlockSpec(memory_space=pltpu.VMEM)
    return pl.pallas_call(
        functools.partial(lag_kernel, scaling),
        in_specs=[vmem, vmem, vmem],
        out_specs=vmem,
        out_shape=jax.ShapeDtypeStruct((count, chunk, square), jnp.bfloat16),
        scratch_shapes=[
            pltpu.VMEM((count - 1, chunk, square), jnp.bfloat16),
            pltpu.SemaphoreType.DMA((count - 1,)),
            pltpu.SemaphoreType.DMA((count - 1,)),
        ],
        compiler_params=pltpu.CompilerParams(collective_id=1, has_side_effects=True),
    )(cos_table, sin_table, mine)


def exchange_kernel(x_ref, y_ref, send_sems, recv_sems):
    count = x_ref.shape[0]
    me = lax.axis_index("sta")
    col = lax.axis_index("seg")
    barrier = pltpu.get_barrier_semaphore()

    def greet(step, carry):
        pl.semaphore_signal(
            barrier, inc=1, device_id=(lax.rem(me + step, count), col),
            device_id_type=pl.DeviceIdType.MESH,
        )
        return carry

    lax.fori_loop(1, count, greet, 0)
    pl.semaphore_wait(barrier, count - 1)

    def describe(step):
        target = lax.rem(me + step, count)
        return pltpu.make_async_remote_copy(
            src_ref=x_ref.at[target],
            dst_ref=y_ref.at[me],
            send_sem=send_sems.at[step],
            recv_sem=recv_sems.at[step],
            device_id=(target, col),
            device_id_type=pl.DeviceIdType.MESH,
        )

    def send(step, carry):
        describe(step).start()
        return carry

    lax.fori_loop(1, count, send, 0)
    y_ref[me] = x_ref[me]

    def finish(step, carry):
        describe(step).wait()
        return carry

    lax.fori_loop(1, count, finish, 0)


def exchange(x, collective):
    count = x.shape[0]
    vmem = pl.BlockSpec(memory_space=pltpu.VMEM)
    return pl.pallas_call(
        exchange_kernel,
        in_specs=[vmem],
        out_specs=vmem,
        out_shape=jax.ShapeDtypeStruct(x.shape, x.dtype),
        scratch_shapes=[pltpu.SemaphoreType.DMA((count,)), pltpu.SemaphoreType.DMA((count,))],
        compiler_params=pltpu.CompilerParams(collective_id=collective, has_side_effects=True),
    )(x)


def per_device(records, plan):
    stations_dev, windows, length = records.shape
    sta_devices = lax.axis_size("sta")
    seg_devices = lax.axis_size("seg")
    transform = 2 * length
    row_count = stations_dev * windows
    cos_table, sin_table = fourier_tables(length, NBIN, transform)
    signal = jnp.transpose(records, (1, 0, 2)).reshape(row_count, length)
    mean_level = band_mean(jnp.abs(signal).astype(jnp.bfloat16), HALF)
    flattened = (signal / (mean_level + 1e-05)).astype(jnp.bfloat16)
    spec_real = jnp.dot(flattened, cos_table, preferred_element_type=jnp.float32)
    spec_imag = jnp.dot(flattened, sin_table, preferred_element_type=jnp.float32)
    magnitude = jnp.sqrt(spec_real * spec_real + spec_imag * spec_imag).astype(jnp.bfloat16)
    smooth = band_mean(magnitude, HALF)
    whitened = jnp.stack(
        [spec_real / (smooth + 1e-06), spec_imag / (smooth + 1e-06)], axis=0
    ).astype(jnp.bfloat16)
    whitened = whitened.reshape(2, windows, stations_dev, NBIN)
    quarter = NBIN // seg_devices
    own = lax.all_to_all(whitened, "seg", split_axis=3, concat_axis=1, tiled=True)
    all_windows = windows * seg_devices
    low = 2 * all_windows * stations_dev // sta_devices
    own_chunks = own.reshape(sta_devices, low, quarter)
    spread = exchange(own_chunks, 2)
    partners = jnp.stack([jnp.take(spread, plan[number], axis=0) for number in range(ROUNDS)], axis=1)
    partner = jnp.transpose(exchange(partners, 3), (1, 0, 2, 3))
    partner = partner.reshape(ROUNDS, 2, all_windows, stations_dev, quarter)
    first_bin = lax.axis_index("seg") * quarter
    bin_index = first_bin + jnp.arange(quarter, dtype=jnp.int32)
    weight = jnp.where(bin_index == 0, 1.0, 2.0).astype(jnp.float32).reshape(1, quarter)
    crossed = cross_spectra(weight, own.astype(jnp.float32), partner)
    square = stations_dev * stations_dev
    mine = crossed.reshape(seg_devices, 2, square, quarter)
    scaling = 1.0 / math.sqrt(4.0 * NBIN * all_windows)
    lagged = lag_transform(scaling, cos_table, sin_table, mine)
    return jnp.transpose(lagged, (1, 0, 2)).astype(jnp.float32)


def solution(mesh):
    in_specs = (P("sta", "seg", None), P())
    out_specs = P("seg", None, "sta")
    return jax.shard_map(
        per_device, mesh=mesh, in_specs=in_specs, out_specs=out_specs, check_vma=False
    )
```

```python
import functools
import math

import jax
import jax.numpy as jnp
from jax import lax
from jax.experimental import pallas as pl
from jax.experimental.pallas import tpu as pltpu
from jax.sharding import PartitionSpec as P

WLEN = 2048
NBIN = 1024
HALF = 64
ROUNDS = 4
LAGS = 2048


def band_mean(values, half_width):
    row_count, length = values.shape
    block_width = 2 * half_width
    blocks_count = length // block_width
    inside = jnp.arange(block_width, dtype=jnp.int32)
    source = inside[:, None]
    target = inside[None, :]
    inner_band = (jnp.abs(source - target) <= half_width).astype(jnp.bfloat16)
    before = (target + block_width - source <= half_width).astype(jnp.bfloat16)
    after_band = (source + block_width - target <= half_width).astype(jnp.bfloat16)
    blocks = values.reshape(row_count, blocks_count, block_width)
    earlier = jnp.pad(blocks[:, :-1], ((0, 0), (1, 0), (0, 0)))
    following = jnp.pad(blocks[:, 1:], ((0, 0), (0, 1), (0, 0)))
    flat_shape = (row_count * blocks_count, block_width)
    running = jnp.dot(blocks.reshape(flat_shape), inner_band, preferred_element_type=jnp.float32)
    running = running + jnp.dot(
        earlier.reshape(flat_shape), before, preferred_element_type=jnp.float32
    )
    running = running + jnp.dot(
        following.reshape(flat_shape), after_band, preferred_element_type=jnp.float32
    )
    position = jnp.arange(length, dtype=jnp.int32)
    counted = (
        jnp.minimum(position, half_width) + jnp.minimum(length - 1 - position, half_width) + 1
    ).astype(jnp.float32)
    return running.reshape(row_count, length) / counted


def angles_of(rows, step, bins, transform):
    phase_int = (rows[:, None] * step) * bins[None, :] % transform
    return phase_int.astype(jnp.float32) * (2.0 * math.pi / transform)


def fourier_tables(length, bin_count, transform):
    low_count = 64
    high_count = length // low_count
    bins = jnp.arange(bin_count, dtype=jnp.int32)
    high = angles_of(jnp.arange(high_count, dtype=jnp.int32), low_count, bins, transform)
    low = angles_of(jnp.arange(low_count, dtype=jnp.int32), 1, bins, transform)
    hc, hs = jnp.cos(high)[:, None], jnp.sin(high)[:, None]
    lc, ls = jnp.cos(low)[None], jnp.sin(low)[None]
    cos_part = (hc * lc - hs * ls).astype(jnp.bfloat16).reshape(length, bin_count)
    sin_part = (-(hs * lc + hc * ls)).astype(jnp.bfloat16).reshape(length, bin_count)
    return cos_part, sin_part


def cross_round(weight, own_ref, other_ref, r, dst):
    windows = own_ref.shape[1]
    stations = own_ref.shape[2]
    group = 4

    def body(index, carry):
        first = index * group
        acc_re = [None] * group
        acc_im = [None] * group
        for w in range(windows):
            pre = other_ref[r, 0, w].astype(jnp.float32)
            pim = other_ref[r, 1, w].astype(jnp.float32)
            for g in range(group):
                ore = own_ref[0, w, pl.ds(first + g, 1), :]
                oim = own_ref[1, w, pl.ds(first + g, 1), :]
                re = ore * pre + oim * pim
                im = oim * pre - ore * pim
                acc_re[g] = re if w == 0 else acc_re[g] + re
                acc_im[g] = im if w == 0 else acc_im[g] + im
        for g in range(group):
            dst[0, first + g] = (acc_re[g] * weight).astype(dst.dtype)
            dst[1, first + g] = (acc_im[g] * weight).astype(dst.dtype)
        return carry

    lax.fori_loop(0, stations // group, body, 0)


def cross_kernel(weight_ref, own_ref, other_ref, out_ref, staged, send_sems, recv_sems):
    count = out_ref.shape[0]
    me = lax.axis_index("seg")
    row = lax.axis_index("sta")
    barrier = pltpu.get_barrier_semaphore()
    for step in range(1, count):
        pl.semaphore_signal(
            barrier, inc=1, device_id=(row, lax.rem(me + step, count)),
            device_id_type=pl.DeviceIdType.MESH,
        )
    pl.semaphore_wait(barrier, count - 1)
    weight = weight_ref[...]
    copies = []
    for step in range(count - 1):
        target = lax.rem(me + 1 + step, count)
        cross_round(weight, own_ref, other_ref, target, staged.at[step])
        copy = pltpu.make_async_remote_copy(
            src_ref=staged.at[step],
            dst_ref=out_ref.at[me],
            send_sem=send_sems.at[step],
            recv_sem=recv_sems.at[step],
            device_id=(row, target),
            device_id_type=pl.DeviceIdType.MESH,
        )
        copy.start()
        copies.append(copy)
    cross_round(weight, own_ref, other_ref, me, out_ref.at[me])
    for copy in copies:
        copy.wait()


def cross_spectra(weight, own, other):
    rounds, _, windows, stations, bins = other.shape
    vmem = pl.BlockSpec(memory_space=pltpu.VMEM)
    return pl.pallas_call(
        cross_kernel,
        in_specs=[vmem, vmem, vmem],
        out_specs=vmem,
        out_shape=jax.ShapeDtypeStruct((rounds, 2, stations, stations, bins), jnp.bfloat16),
        scratch_shapes=[
            pltpu.VMEM((rounds - 1, 2, stations, stations, bins), jnp.bfloat16),
            pltpu.SemaphoreType.DMA((rounds - 1,)),
            pltpu.SemaphoreType.DMA((rounds - 1,)),
        ],
        compiler_params=pltpu.CompilerParams(collective_id=0, has_side_effects=True),
    )(weight, own, other)


def lag_kernel(scaling, cos_ref, sin_ref, y_ref, out_ref, staged, send_sems, recv_sems):
    count = out_ref.shape[0]
    chunk = out_ref.shape[1]
    quarter = y_ref.shape[3]
    rows = 128
    me = lax.axis_index("seg")
    row = lax.axis_index("sta")
    barrier = pltpu.get_barrier_semaphore()
    for step in range(1, count):
        pl.semaphore_signal(
            barrier, inc=1, device_id=(row, lax.rem(me + step, count)),
            device_id_type=pl.DeviceIdType.MESH,
        )
    pl.semaphore_wait(barrier, count - 1)
    contract = (((1,), (1,)), ((), ()))

    def compute(target, dst):
        def body(index, carry):
            first = pl.multiple_of(target * chunk + index * rows, rows)
            acc = None
            for q in range(count):
                cols = pl.ds(q * quarter, quarter)
                for c, table in enumerate((cos_ref, sin_ref)):
                    part = lax.dot_general(
                        table[pl.ds(first, rows), cols], y_ref[q, c], contract,
                        preferred_element_type=jnp.float32,
                    )
                    acc = part if acc is None else acc + part
            local = pl.multiple_of(index * rows, rows)
            dst[pl.ds(local, rows), :] = (acc * scaling).astype(dst.dtype)
            return carry

        lax.fori_loop(0, chunk // rows, body, 0)

    copies = []
    for step in range(count - 1):
        target = lax.rem(me + 1 + step, count)
        compute(target, staged.at[step])
        copy = pltpu.make_async_remote_copy(
            src_ref=staged.at[step],
            dst_ref=out_ref.at[me],
            send_sem=send_sems.at[step],
            recv_sem=recv_sems.at[step],
            device_id=(row, target),
            device_id_type=pl.DeviceIdType.MESH,
        )
        copy.start()
        copies.append(copy)
    compute(me, out_ref.at[me])
    for copy in copies:
        copy.wait()


def lag_transform(scaling, cos_table, sin_table, mine):
    count, _, square, _ = mine.shape
    chunk = LAGS // count
    vmem = pl.BlockSpec(memory_space=pltpu.VMEM)
    return pl.pallas_call(
        functools.partial(lag_kernel, scaling),
        in_specs=[vmem, vmem, vmem],
        out_specs=vmem,
        out_shape=jax.ShapeDtypeStruct((count, chunk, square), jnp.bfloat16),
        scratch_shapes=[
            pltpu.VMEM((count - 1, chunk, square), jnp.bfloat16),
            pltpu.SemaphoreType.DMA((count - 1,)),
            pltpu.SemaphoreType.DMA((count - 1,)),
        ],
        compiler_params=pltpu.CompilerParams(collective_id=1, has_side_effects=True),
    )(cos_table, sin_table, mine)


def route_kernel(plan_ref, x_ref, y_ref, spread, outgoing, first_sems, second_sems):
    count = x_ref.shape[0]
    rounds = plan_ref.shape[0]
    me = lax.axis_index("sta")
    col = lax.axis_index("seg")
    barrier = pltpu.get_barrier_semaphore()

    def greet(step, carry):
        pl.semaphore_signal(
            barrier, inc=1, device_id=(lax.rem(me + step, count), col),
            device_id_type=pl.DeviceIdType.MESH,
        )
        return carry

    lax.fori_loop(1, count, greet, 0)
    pl.semaphore_wait(barrier, count - 1)

    def describe(source, target_buf, sems, step):
        target = lax.rem(me + step, count)
        return pltpu.make_async_remote_copy(
            src_ref=source.at[target],
            dst_ref=target_buf.at[me],
            send_sem=sems.at[step],
            recv_sem=sems.at[count + step],
            device_id=(target, col),
            device_id_type=pl.DeviceIdType.MESH,
        )

    def send_first(step, carry):
        describe(x_ref, spread, first_sems, step).start()
        return carry

    def finish_first(step, carry):
        describe(x_ref, spread, first_sems, step).wait()
        return carry

    lax.fori_loop(1, count, send_first, 0)
    spread[me] = x_ref[me]
    lax.fori_loop(1, count, finish_first, 0)

    def pick(block, carry):
        for r in range(rounds):
            outgoing[block, r] = spread[plan_ref[r, block]]
        return carry

    lax.fori_loop(0, count, pick, 0)

    def send_second(step, carry):
        describe(outgoing, y_ref, second_sems, step).start()
        return carry

    def finish_second(step, carry):
        describe(outgoing, y_ref, second_sems, step).wait()
        return carry

    lax.fori_loop(1, count, send_second, 0)
    y_ref[me] = outgoing[me]
    lax.fori_loop(1, count, finish_second, 0)


def route_partners(plan, x):
    count, low, bins = x.shape
    rounds = plan.shape[0]
    vmem = pl.BlockSpec(memory_space=pltpu.VMEM)
    return pl.pallas_call(
        route_kernel,
        in_specs=[pl.BlockSpec(memory_space=pltpu.SMEM), vmem],
        out_specs=vmem,
        out_shape=jax.ShapeDtypeStruct((count, rounds, low, bins), x.dtype),
        scratch_shapes=[
            pltpu.VMEM((count, low, bins), x.dtype),
            pltpu.VMEM((count, rounds, low, bins), x.dtype),
            pltpu.SemaphoreType.DMA((2 * count,)),
            pltpu.SemaphoreType.DMA((2 * count,)),
        ],
        compiler_params=pltpu.CompilerParams(collective_id=2, has_side_effects=True),
    )(plan, x)


def per_device(records, plan):
    stations_dev, windows, length = records.shape
    sta_devices = lax.axis_size("sta")
    seg_devices = lax.axis_size("seg")
    transform = 2 * length
    row_count = stations_dev * windows
    cos_table, sin_table = fourier_tables(length, NBIN, transform)
    signal = jnp.transpose(records, (1, 0, 2)).reshape(row_count, length)
    mean_level = band_mean(jnp.abs(signal).astype(jnp.bfloat16), HALF)
    flattened = (signal / (mean_level + 1e-05)).astype(jnp.bfloat16)
    spec_real = jnp.dot(flattened, cos_table, preferred_element_type=jnp.float32)
    spec_imag = jnp.dot(flattened, sin_table, preferred_element_type=jnp.float32)
    magnitude = jnp.sqrt(spec_real * spec_real + spec_imag * spec_imag).astype(jnp.bfloat16)
    smooth = band_mean(magnitude, HALF)
    whitened = jnp.stack(
        [spec_real / (smooth + 1e-06), spec_imag / (smooth + 1e-06)], axis=0
    ).astype(jnp.bfloat16)
    whitened = whitened.reshape(2, windows, stations_dev, NBIN)
    quarter = NBIN // seg_devices
    own = lax.all_to_all(whitened, "seg", split_axis=3, concat_axis=1, tiled=True)
    all_windows = windows * seg_devices
    low = 2 * all_windows * stations_dev // sta_devices
    own_chunks = own.reshape(sta_devices, low, quarter)
    partner = jnp.transpose(route_partners(plan, own_chunks), (1, 0, 2, 3))
    partner = partner.reshape(ROUNDS, 2, all_windows, stations_dev, quarter)
    first_bin = lax.axis_index("seg") * quarter
    bin_index = first_bin + jnp.arange(quarter, dtype=jnp.int32)
    weight = jnp.where(bin_index == 0, 1.0, 2.0).astype(jnp.float32).reshape(1, quarter)
    crossed = cross_spectra(weight, own.astype(jnp.float32), partner)
    square = stations_dev * stations_dev
    mine = crossed.reshape(seg_devices, 2, square, quarter)
    scaling = 1.0 / math.sqrt(4.0 * NBIN * all_windows)
    lagged = lag_transform(scaling, cos_table, sin_table, mine)
    return jnp.transpose(lagged, (1, 0, 2)).astype(jnp.float32)


def solution(mesh):
    in_specs = (P("sta", "seg", None), P())
    out_specs = P("seg", None, "sta")
    return jax.shard_map(
        per_device, mesh=mesh, in_specs=in_specs, out_specs=out_specs, check_vma=False
    )
```

```python
import functools
import math

import jax
import jax.numpy as jnp
from jax import lax
from jax.experimental import pallas as pl
from jax.experimental.pallas import tpu as pltpu
from jax.sharding import PartitionSpec as P

WLEN = 2048
NBIN = 1024
HALF = 64
ROUNDS = 4
LAGS = 2048


def band_mean(values, half_width):
    row_count, length = values.shape
    block_width = 2 * half_width
    blocks_count = length // block_width
    inside = jnp.arange(block_width, dtype=jnp.int32)
    source = inside[:, None]
    target = inside[None, :]
    inner_band = (jnp.abs(source - target) <= half_width).astype(jnp.bfloat16)
    before = (target + block_width - source <= half_width).astype(jnp.bfloat16)
    after_band = (source + block_width - target <= half_width).astype(jnp.bfloat16)
    blocks = values.reshape(row_count, blocks_count, block_width)
    earlier = jnp.pad(blocks[:, :-1], ((0, 0), (1, 0), (0, 0)))
    following = jnp.pad(blocks[:, 1:], ((0, 0), (0, 1), (0, 0)))
    flat_shape = (row_count * blocks_count, block_width)
    running = jnp.dot(blocks.reshape(flat_shape), inner_band, preferred_element_type=jnp.float32)
    running = running + jnp.dot(
        earlier.reshape(flat_shape), before, preferred_element_type=jnp.float32
    )
    running = running + jnp.dot(
        following.reshape(flat_shape), after_band, preferred_element_type=jnp.float32
    )
    position = jnp.arange(length, dtype=jnp.int32)
    counted = (
        jnp.minimum(position, half_width) + jnp.minimum(length - 1 - position, half_width) + 1
    ).astype(jnp.float32)
    return running.reshape(row_count, length) / counted


def angles_of(rows, step, bins, transform):
    phase_int = (rows[:, None] * step) * bins[None, :] % transform
    return phase_int.astype(jnp.float32) * (2.0 * math.pi / transform)


def fourier_tables(length, bin_count, transform):
    low_count = 64
    high_count = length // low_count
    bins = jnp.arange(bin_count, dtype=jnp.int32)
    high = angles_of(jnp.arange(high_count, dtype=jnp.int32), low_count, bins, transform)
    low = angles_of(jnp.arange(low_count, dtype=jnp.int32), 1, bins, transform)
    hc, hs = jnp.cos(high)[:, None], jnp.sin(high)[:, None]
    lc, ls = jnp.cos(low)[None], jnp.sin(low)[None]
    cos_part = (hc * lc - hs * ls).astype(jnp.bfloat16).reshape(length, bin_count)
    sin_part = (-(hs * lc + hc * ls)).astype(jnp.bfloat16).reshape(length, bin_count)
    return cos_part, sin_part


def cross_round(weight, own_ref, other_ref, r, dst):
    windows = own_ref.shape[1]
    stations = own_ref.shape[2]
    group = 4

    def body(index, carry):
        first = index * group
        acc_re = [None] * group
        acc_im = [None] * group
        for w in range(windows):
            pre = other_ref[r, 0, w].astype(jnp.float32)
            pim = other_ref[r, 1, w].astype(jnp.float32)
            for g in range(group):
                ore = own_ref[0, w, pl.ds(first + g, 1), :]
                oim = own_ref[1, w, pl.ds(first + g, 1), :]
                re = ore * pre + oim * pim
                im = oim * pre - ore * pim
                acc_re[g] = re if w == 0 else acc_re[g] + re
                acc_im[g] = im if w == 0 else acc_im[g] + im
        for g in range(group):
            dst[0, first + g] = (acc_re[g] * weight).astype(dst.dtype)
            dst[1, first + g] = (acc_im[g] * weight).astype(dst.dtype)
        return carry

    lax.fori_loop(0, stations // group, body, 0)


def cross_kernel(weight_ref, own_ref, other_ref, out_ref, staged, send_sems, recv_sems):
    count = out_ref.shape[0]
    me = lax.axis_index("seg")
    row = lax.axis_index("sta")
    barrier = pltpu.get_barrier_semaphore()
    for step in range(1, count):
        pl.semaphore_signal(
            barrier, inc=1, device_id=(row, lax.rem(me + step, count)),
            device_id_type=pl.DeviceIdType.MESH,
        )
    pl.semaphore_wait(barrier, count - 1)
    weight = weight_ref[...]
    copies = []
    for step in range(count - 1):
        target = lax.rem(me + 1 + step, count)
        cross_round(weight, own_ref, other_ref, target, staged.at[step])
        copy = pltpu.make_async_remote_copy(
            src_ref=staged.at[step],
            dst_ref=out_ref.at[me],
            send_sem=send_sems.at[step],
            recv_sem=recv_sems.at[step],
            device_id=(row, target),
            device_id_type=pl.DeviceIdType.MESH,
        )
        copy.start()
        copies.append(copy)
    cross_round(weight, own_ref, other_ref, me, out_ref.at[me])
    for copy in copies:
        copy.wait()


def cross_spectra(weight, own, other):
    rounds, _, windows, stations, bins = other.shape
    vmem = pl.BlockSpec(memory_space=pltpu.VMEM)
    return pl.pallas_call(
        cross_kernel,
        in_specs=[vmem, vmem, vmem],
        out_specs=vmem,
        out_shape=jax.ShapeDtypeStruct((rounds, 2, stations, stations, bins), jnp.bfloat16),
        scratch_shapes=[
            pltpu.VMEM((rounds - 1, 2, stations, stations, bins), jnp.bfloat16),
            pltpu.SemaphoreType.DMA((rounds - 1,)),
            pltpu.SemaphoreType.DMA((rounds - 1,)),
        ],
        compiler_params=pltpu.CompilerParams(collective_id=0, has_side_effects=True),
    )(weight, own, other)


def lag_kernel(scaling, cos_ref, sin_ref, y_ref, out_ref, staged, send_sems, recv_sems):
    count = out_ref.shape[0]
    chunk = out_ref.shape[1]
    quarter = y_ref.shape[3]
    rows = 128
    me = lax.axis_index("seg")
    row = lax.axis_index("sta")
    barrier = pltpu.get_barrier_semaphore()
    for step in range(1, count):
        pl.semaphore_signal(
            barrier, inc=1, device_id=(row, lax.rem(me + step, count)),
            device_id_type=pl.DeviceIdType.MESH,
        )
    pl.semaphore_wait(barrier, count - 1)
    contract = (((1,), (1,)), ((), ()))

    def compute(target, dst):
        def body(index, carry):
            first = pl.multiple_of(target * chunk + index * rows, rows)
            acc = None
            for q in range(count):
                cols = pl.ds(q * quarter, quarter)
                for c, table in enumerate((cos_ref, sin_ref)):
                    part = lax.dot_general(
                        table[pl.ds(first, rows), cols], y_ref[q, c], contract,
                        preferred_element_type=jnp.float32,
                    )
                    acc = part if acc is None else acc + part
            local = pl.multiple_of(index * rows, rows)
            dst[pl.ds(local, rows), :] = (acc * scaling).astype(dst.dtype)
            return carry

        lax.fori_loop(0, chunk // rows, body, 0)

    copies = []
    for step in range(count - 1):
        target = lax.rem(me + 1 + step, count)
        compute(target, staged.at[step])
        copy = pltpu.make_async_remote_copy(
            src_ref=staged.at[step],
            dst_ref=out_ref.at[me],
            send_sem=send_sems.at[step],
            recv_sem=recv_sems.at[step],
            device_id=(row, target),
            device_id_type=pl.DeviceIdType.MESH,
        )
        copy.start()
        copies.append(copy)
    compute(me, out_ref.at[me])
    for copy in copies:
        copy.wait()


def lag_transform(scaling, cos_table, sin_table, mine):
    count, _, square, _ = mine.shape
    chunk = LAGS // count
    vmem = pl.BlockSpec(memory_space=pltpu.VMEM)
    return pl.pallas_call(
        functools.partial(lag_kernel, scaling),
        in_specs=[vmem, vmem, vmem],
        out_specs=vmem,
        out_shape=jax.ShapeDtypeStruct((count, chunk, square), jnp.bfloat16),
        scratch_shapes=[
            pltpu.VMEM((count - 1, chunk, square), jnp.bfloat16),
            pltpu.SemaphoreType.DMA((count - 1,)),
            pltpu.SemaphoreType.DMA((count - 1,)),
        ],
        compiler_params=pltpu.CompilerParams(collective_id=1, has_side_effects=True),
    )(cos_table, sin_table, mine)


def route_kernel(plan_ref, x_ref, own_ref, y_ref, spread, outgoing, zero_sems, first_sems, second_sems):
    count = spread.shape[0]
    low = spread.shape[1]
    rounds = plan_ref.shape[0]
    parts = own_ref.shape[1] // x_ref.shape[1]
    windows_dev = x_ref.shape[1]
    quarter = own_ref.shape[3]
    windows = own_ref.shape[1]
    halves = own_ref.shape[2] // low
    me = lax.axis_index("sta")
    col = lax.axis_index("seg")
    mesh_ids = pl.DeviceIdType.MESH
    barrier = pltpu.get_barrier_semaphore()

    def greet(step, carry):
        pl.semaphore_signal(
            barrier, inc=1, device_id=(lax.rem(me + step, count), col), device_id_type=mesh_ids
        )
        return carry

    lax.fori_loop(1, count, greet, 0)
    for step in range(1, parts):
        pl.semaphore_signal(
            barrier, inc=1, device_id=(me, lax.rem(col + step, parts)), device_id_type=mesh_ids
        )
    pl.semaphore_wait(barrier, count - 1 + parts - 1)

    def describe_zero(step):
        target = lax.rem(col + step, parts)
        return pltpu.make_async_remote_copy(
            src_ref=x_ref.at[:, :, :, pl.ds(pl.multiple_of(target * quarter, quarter), quarter)],
            dst_ref=own_ref.at[:, pl.ds(col * windows_dev, windows_dev)],
            send_sem=zero_sems.at[step],
            recv_sem=zero_sems.at[parts + step],
            device_id=(me, target),
            device_id_type=mesh_ids,
        )

    for step in range(1, parts):
        describe_zero(step).start()
    own_ref[:, pl.ds(col * windows_dev, windows_dev)] = x_ref[
        :, :, :, pl.ds(pl.multiple_of(col * quarter, quarter), quarter)
    ]
    for step in range(1, parts):
        describe_zero(step).wait()

    def chunk_of(j):
        c = j // (windows * halves)
        w = lax.rem(j // halves, windows)
        s_hi = lax.rem(j, halves)
        return own_ref.at[c, w, pl.ds(s_hi * low, low)]

    def describe_first(step):
        target = lax.rem(me + step, count)
        return pltpu.make_async_remote_copy(
            src_ref=chunk_of(target),
            dst_ref=spread.at[me],
            send_sem=first_sems.at[step],
            recv_sem=first_sems.at[count + step],
            device_id=(target, col),
            device_id_type=mesh_ids,
        )

    def describe_second(step):
        target = lax.rem(me + step, count)
        return pltpu.make_async_remote_copy(
            src_ref=outgoing.at[target],
            dst_ref=y_ref.at[me],
            send_sem=second_sems.at[step],
            recv_sem=second_sems.at[count + step],
            device_id=(target, col),
            device_id_type=mesh_ids,
        )

    def send_first(step, carry):
        describe_first(step).start()
        return carry

    def finish_first(step, carry):
        describe_first(step).wait()
        return carry

    lax.fori_loop(1, count, send_first, 0)
    spread[me] = chunk_of(me)[...]
    lax.fori_loop(1, count, finish_first, 0)

    def pick(block, carry):
        for r in range(rounds):
            outgoing[block, r] = spread[plan_ref[r, block]]
        return carry

    lax.fori_loop(0, count, pick, 0)

    def send_second(step, carry):
        describe_second(step).start()
        return carry

    def finish_second(step, carry):
        describe_second(step).wait()
        return carry

    lax.fori_loop(1, count, send_second, 0)
    y_ref[me] = outgoing[me]
    lax.fori_loop(1, count, finish_second, 0)


def route_partners(plan, x, count, parts):
    channels, windows_dev, stations, bins = x.shape
    rounds = plan.shape[0]
    quarter = bins // parts
    windows = windows_dev * parts
    low = channels * windows * stations // count
    vmem = pl.BlockSpec(memory_space=pltpu.VMEM)
    return pl.pallas_call(
        route_kernel,
        in_specs=[pl.BlockSpec(memory_space=pltpu.SMEM), vmem],
        out_specs=[vmem, vmem],
        out_shape=[
            jax.ShapeDtypeStruct((channels, windows, stations, quarter), x.dtype),
            jax.ShapeDtypeStruct((count, rounds, low, quarter), x.dtype),
        ],
        scratch_shapes=[
            pltpu.VMEM((count, low, quarter), x.dtype),
            pltpu.VMEM((count, rounds, low, quarter), x.dtype),
            pltpu.SemaphoreType.DMA((2 * parts,)),
            pltpu.SemaphoreType.DMA((2 * count,)),
            pltpu.SemaphoreType.DMA((2 * count,)),
        ],
        compiler_params=pltpu.CompilerParams(collective_id=2, has_side_effects=True),
    )(plan, x)


def per_device(records, plan):
    stations_dev, windows, length = records.shape
    sta_devices = lax.axis_size("sta")
    seg_devices = lax.axis_size("seg")
    transform = 2 * length
    row_count = stations_dev * windows
    cos_table, sin_table = fourier_tables(length, NBIN, transform)
    signal = jnp.transpose(records, (1, 0, 2)).reshape(row_count, length)
    mean_level = band_mean(jnp.abs(signal).astype(jnp.bfloat16), HALF)
    flattened = (signal / (mean_level + 1e-05)).astype(jnp.bfloat16)
    spec_real = jnp.dot(flattened, cos_table, preferred_element_type=jnp.float32)
    spec_imag = jnp.dot(flattened, sin_table, preferred_element_type=jnp.float32)
    magnitude = jnp.sqrt(spec_real * spec_real + spec_imag * spec_imag).astype(jnp.bfloat16)
    smooth = band_mean(magnitude, HALF)
    whitened = jnp.stack(
        [spec_real / (smooth + 1e-06), spec_imag / (smooth + 1e-06)], axis=0
    ).astype(jnp.bfloat16)
    whitened = whitened.reshape(2, windows, stations_dev, NBIN)
    quarter = NBIN // seg_devices
    all_windows = windows * seg_devices
    own, partner = route_partners(plan, whitened, sta_devices, seg_devices)
    partner = jnp.transpose(partner, (1, 0, 2, 3))
    partner = partner.reshape(ROUNDS, 2, all_windows, stations_dev, quarter)
    first_bin = lax.axis_index("seg") * quarter
    bin_index = first_bin + jnp.arange(quarter, dtype=jnp.int32)
    weight = jnp.where(bin_index == 0, 1.0, 2.0).astype(jnp.float32).reshape(1, quarter)
    crossed = cross_spectra(weight, own.astype(jnp.float32), partner)
    square = stations_dev * stations_dev
    mine = crossed.reshape(seg_devices, 2, square, quarter)
    scaling = 1.0 / math.sqrt(4.0 * NBIN * all_windows)
    lagged = lag_transform(scaling, cos_table, sin_table, mine)
    return jnp.transpose(lagged, (1, 0, 2)).astype(jnp.float32)


def solution(mesh):
    in_specs = (P("sta", "seg", None), P())
    out_specs = P("seg", None, "sta")
    return jax.shard_map(
        per_device, mesh=mesh, in_specs=in_specs, out_specs=out_specs, check_vma=False
    )
```

```python
import functools
import math

import jax
import jax.numpy as jnp
from jax import lax
from jax.experimental import pallas as pl
from jax.experimental.pallas import tpu as pltpu
from jax.sharding import PartitionSpec as P

WLEN = 2048
NBIN = 1024
HALF = 64
ROUNDS = 4
LAGS = 2048


def band_mean(values, half_width):
    row_count, length = values.shape
    block_width = 2 * half_width
    blocks_count = length // block_width
    inside = jnp.arange(block_width, dtype=jnp.int32)
    source = inside[:, None]
    target = inside[None, :]
    inner_band = (jnp.abs(source - target) <= half_width).astype(jnp.bfloat16)
    before = (target + block_width - source <= half_width).astype(jnp.bfloat16)
    after_band = (source + block_width - target <= half_width).astype(jnp.bfloat16)
    blocks = values.reshape(row_count, blocks_count, block_width)
    earlier = jnp.pad(blocks[:, :-1], ((0, 0), (1, 0), (0, 0)))
    following = jnp.pad(blocks[:, 1:], ((0, 0), (0, 1), (0, 0)))
    flat_shape = (row_count * blocks_count, block_width)
    running = jnp.dot(blocks.reshape(flat_shape), inner_band, preferred_element_type=jnp.float32)
    running = running + jnp.dot(
        earlier.reshape(flat_shape), before, preferred_element_type=jnp.float32
    )
    running = running + jnp.dot(
        following.reshape(flat_shape), after_band, preferred_element_type=jnp.float32
    )
    position = jnp.arange(length, dtype=jnp.int32)
    counted = (
        jnp.minimum(position, half_width) + jnp.minimum(length - 1 - position, half_width) + 1
    ).astype(jnp.float32)
    return running.reshape(row_count, length) / counted


def angles_of(rows, step, bins, transform):
    phase_int = (rows[:, None] * step) * bins[None, :] % transform
    return phase_int.astype(jnp.float32) * (2.0 * math.pi / transform)


def fourier_tables(length, bin_count, transform):
    low_count = 64
    high_count = length // low_count
    bins = jnp.arange(bin_count, dtype=jnp.int32)
    high = angles_of(jnp.arange(high_count, dtype=jnp.int32), low_count, bins, transform)
    low = angles_of(jnp.arange(low_count, dtype=jnp.int32), 1, bins, transform)
    hc, hs = jnp.cos(high)[:, None], jnp.sin(high)[:, None]
    lc, ls = jnp.cos(low)[None], jnp.sin(low)[None]
    cos_part = (hc * lc - hs * ls).astype(jnp.bfloat16).reshape(length, bin_count)
    sin_part = (-(hs * lc + hc * ls)).astype(jnp.bfloat16).reshape(length, bin_count)
    return cos_part, sin_part


def cross_round(weight, own_ref, other_ref, r, dst):
    windows = own_ref.shape[1]
    stations = own_ref.shape[2]
    low = other_ref.shape[2]
    halves = stations // low
    group = 4

    def rows_of(c, w):
        first = (c * windows + w) * halves
        return jnp.concatenate(
            [other_ref[first + h, r].astype(jnp.float32) for h in range(halves)], axis=0
        )

    def body(index, carry):
        first = index * group
        acc_re = [None] * group
        acc_im = [None] * group
        for w in range(windows):
            pre = rows_of(0, w)
            pim = rows_of(1, w)
            for g in range(group):
                ore = own_ref[0, w, pl.ds(first + g, 1), :]
                oim = own_ref[1, w, pl.ds(first + g, 1), :]
                re = ore * pre + oim * pim
                im = oim * pre - ore * pim
                acc_re[g] = re if w == 0 else acc_re[g] + re
                acc_im[g] = im if w == 0 else acc_im[g] + im
        for g in range(group):
            dst[0, first + g] = (acc_re[g] * weight).astype(dst.dtype)
            dst[1, first + g] = (acc_im[g] * weight).astype(dst.dtype)
        return carry

    lax.fori_loop(0, stations // group, body, 0)


def lag_kernel(scaling, cos_ref, sin_ref, y_ref, out_ref, staged, send_sems, recv_sems):
    count = out_ref.shape[0]
    chunk = out_ref.shape[1]
    quarter = y_ref.shape[3]
    rows = 128
    me = lax.axis_index("seg")
    row = lax.axis_index("sta")
    barrier = pltpu.get_barrier_semaphore()
    for step in range(1, count):
        pl.semaphore_signal(
            barrier, inc=1, device_id=(row, lax.rem(me + step, count)),
            device_id_type=pl.DeviceIdType.MESH,
        )
    pl.semaphore_wait(barrier, count - 1)
    contract = (((1,), (1,)), ((), ()))

    def compute(target, dst):
        def body(index, carry):
            first = pl.multiple_of(target * chunk + index * rows, rows)
            acc = None
            for q in range(count):
                cols = pl.ds(q * quarter, quarter)
                for c, table in enumerate((cos_ref, sin_ref)):
                    part = lax.dot_general(
                        table[pl.ds(first, rows), cols], y_ref[q, c], contract,
                        preferred_element_type=jnp.float32,
                    )
                    acc = part if acc is None else acc + part
            local = pl.multiple_of(index * rows, rows)
            dst[pl.ds(local, rows), :] = (acc * scaling).astype(dst.dtype)
            return carry

        lax.fori_loop(0, chunk // rows, body, 0)

    copies = []
    for step in range(count - 1):
        target = lax.rem(me + 1 + step, count)
        compute(target, staged.at[step])
        copy = pltpu.make_async_remote_copy(
            src_ref=staged.at[step],
            dst_ref=out_ref.at[me],
            send_sem=send_sems.at[step],
            recv_sem=recv_sems.at[step],
            device_id=(row, target),
            device_id_type=pl.DeviceIdType.MESH,
        )
        copy.start()
        copies.append(copy)
    compute(me, out_ref.at[me])
    for copy in copies:
        copy.wait()


def lag_transform(scaling, cos_table, sin_table, mine):
    count, _, square, _ = mine.shape
    chunk = LAGS // count
    vmem = pl.BlockSpec(memory_space=pltpu.VMEM)
    return pl.pallas_call(
        functools.partial(lag_kernel, scaling),
        in_specs=[vmem, vmem, vmem],
        out_specs=vmem,
        out_shape=jax.ShapeDtypeStruct((count, chunk, square), jnp.bfloat16),
        scratch_shapes=[
            pltpu.VMEM((count - 1, chunk, square), jnp.bfloat16),
            pltpu.SemaphoreType.DMA((count - 1,)),
            pltpu.SemaphoreType.DMA((count - 1,)),
        ],
        compiler_params=pltpu.CompilerParams(collective_id=1, has_side_effects=True),
    )(cos_table, sin_table, mine)


def route_kernel(plan_ref, weight_ref, x_ref, out_ref, own, own_f, spread, outgoing, partner,
                 staged, zero_sems, first_sems, second_sems, cross_sems):
    count = spread.shape[0]
    low = spread.shape[1]
    rounds = plan_ref.shape[0]
    parts = own.shape[1] // x_ref.shape[1]
    windows_dev = x_ref.shape[1]
    quarter = own.shape[3]
    windows = own.shape[1]
    halves = own.shape[2] // low
    me = lax.axis_index("sta")
    col = lax.axis_index("seg")
    mesh_ids = pl.DeviceIdType.MESH
    barrier = pltpu.get_barrier_semaphore()

    def greet(step, carry):
        pl.semaphore_signal(
            barrier, inc=1, device_id=(lax.rem(me + step, count), col), device_id_type=mesh_ids
        )
        return carry

    lax.fori_loop(1, count, greet, 0)
    for step in range(1, parts):
        pl.semaphore_signal(
            barrier, inc=1, device_id=(me, lax.rem(col + step, parts)), device_id_type=mesh_ids
        )
    pl.semaphore_wait(barrier, count - 1 + parts - 1)

    def describe_zero(step):
        target = lax.rem(col + step, parts)
        return pltpu.make_async_remote_copy(
            src_ref=x_ref.at[:, :, :, pl.ds(pl.multiple_of(target * quarter, quarter), quarter)],
            dst_ref=own.at[:, pl.ds(col * windows_dev, windows_dev)],
            send_sem=zero_sems.at[step],
            recv_sem=zero_sems.at[parts + step],
            device_id=(me, target),
            device_id_type=mesh_ids,
        )

    for step in range(1, parts):
        describe_zero(step).start()
    own[:, pl.ds(col * windows_dev, windows_dev)] = x_ref[
        :, :, :, pl.ds(pl.multiple_of(col * quarter, quarter), quarter)
    ]
    for step in range(1, parts):
        describe_zero(step).wait()

    def chunk_of(j):
        c = j // (windows * halves)
        w = lax.rem(j // halves, windows)
        s_hi = lax.rem(j, halves)
        return own.at[c, w, pl.ds(s_hi * low, low)]

    def describe_first(step):
        target = lax.rem(me + step, count)
        return pltpu.make_async_remote_copy(
            src_ref=chunk_of(target),
            dst_ref=spread.at[me],
            send_sem=first_sems.at[step],
            recv_sem=first_sems.at[count + step],
            device_id=(target, col),
            device_id_type=mesh_ids,
        )

    def send_first(step, carry):
        describe_first(step).start()
        return carry

    def finish_first(step, carry):
        describe_first(step).wait()
        return carry

    lax.fori_loop(1, count, send_first, 0)
    spread[me] = chunk_of(me)[...]
    lax.fori_loop(1, count, finish_first, 0)

    def pick(block, carry):
        for r in range(rounds):
            outgoing[block, r] = spread[plan_ref[r, block]]
        return carry

    lax.fori_loop(0, count, pick, 0)

    def round_of(order):
        return lax.rem(col + 1 + order, rounds)

    def describe_second(order, step):
        target = lax.rem(me + step, count)
        r = round_of(order)
        return pltpu.make_async_remote_copy(
            src_ref=outgoing.at[target, r],
            dst_ref=partner.at[me, r],
            send_sem=second_sems.at[order * count + step],
            recv_sem=second_sems.at[(rounds + order) * count + step],
            device_id=(target, col),
            device_id_type=mesh_ids,
        )

    for order in range(rounds):
        def send_second(step, carry, order=order):
            describe_second(order, step).start()
            return carry

        lax.fori_loop(1, count, send_second, 0)
    for r in range(rounds):
        partner[me, r] = outgoing[me, r]
    own_f[...] = own[...].astype(jnp.float32)
    weight = weight_ref[...]

    def describe_cross(order):
        target = round_of(order)
        return pltpu.make_async_remote_copy(
            src_ref=staged.at[order],
            dst_ref=out_ref.at[col],
            send_sem=cross_sems.at[order],
            recv_sem=cross_sems.at[rounds + order],
            device_id=(me, target),
            device_id_type=mesh_ids,
        )

    for order in range(rounds):
        def arrived(step, carry, order=order):
            describe_second(order, step).wait_recv()
            return carry

        lax.fori_loop(1, count, arrived, 0)
        r = round_of(order)
        if order < rounds - 1:
            cross_round(weight, own_f, partner, r, staged.at[order])
            describe_cross(order).start()
        else:
            cross_round(weight, own_f, partner, r, out_ref.at[col])

    for order in range(rounds):
        def sent(step, carry, order=order):
            describe_second(order, step).wait_send()
            return carry

        lax.fori_loop(1, count, sent, 0)
    for order in range(rounds - 1):
        describe_cross(order).wait()


def route_and_cross(plan, weight, x, count, parts):
    channels, windows_dev, stations, bins = x.shape
    rounds = plan.shape[0]
    quarter = bins // parts
    windows = windows_dev * parts
    low = channels * windows * stations // count
    vmem = pl.BlockSpec(memory_space=pltpu.VMEM)
    return pl.pallas_call(
        route_kernel,
        in_specs=[pl.BlockSpec(memory_space=pltpu.SMEM), vmem, vmem],
        out_specs=vmem,
        out_shape=jax.ShapeDtypeStruct((parts, channels, stations, stations, quarter), x.dtype),
        scratch_shapes=[
            pltpu.VMEM((channels, windows, stations, quarter), x.dtype),
            pltpu.VMEM((channels, windows, stations, quarter), jnp.float32),
            pltpu.VMEM((count, low, quarter), x.dtype),
            pltpu.VMEM((count, rounds, low, quarter), x.dtype),
            pltpu.VMEM((count, rounds, low, quarter), x.dtype),
            pltpu.VMEM((rounds - 1, channels, stations, stations, quarter), x.dtype),
            pltpu.SemaphoreType.DMA((2 * parts,)),
            pltpu.SemaphoreType.DMA((2 * count,)),
            pltpu.SemaphoreType.DMA((2 * rounds * count,)),
            pltpu.SemaphoreType.DMA((2 * rounds,)),
        ],
        compiler_params=pltpu.CompilerParams(collective_id=2, has_side_effects=True),
    )(plan, weight, x)


def per_device(records, plan):
    stations_dev, windows, length = records.shape
    sta_devices = lax.axis_size("sta")
    seg_devices = lax.axis_size("seg")
    transform = 2 * length
    row_count = stations_dev * windows
    cos_table, sin_table = fourier_tables(length, NBIN, transform)
    signal = jnp.transpose(records, (1, 0, 2)).reshape(row_count, length)
    mean_level = band_mean(jnp.abs(signal).astype(jnp.bfloat16), HALF)
    flattened = (signal / (mean_level + 1e-05)).astype(jnp.bfloat16)
    spec_real = jnp.dot(flattened, cos_table, preferred_element_type=jnp.float32)
    spec_imag = jnp.dot(flattened, sin_table, preferred_element_type=jnp.float32)
    magnitude = jnp.sqrt(spec_real * spec_real + spec_imag * spec_imag).astype(jnp.bfloat16)
    smooth = band_mean(magnitude, HALF)
    whitened = jnp.stack(
        [spec_real / (smooth + 1e-06), spec_imag / (smooth + 1e-06)], axis=0
    ).astype(jnp.bfloat16)
    whitened = whitened.reshape(2, windows, stations_dev, NBIN)
    quarter = NBIN // seg_devices
    all_windows = windows * seg_devices
    first_bin = lax.axis_index("seg") * quarter
    bin_index = first_bin + jnp.arange(quarter, dtype=jnp.int32)
    weight = jnp.where(bin_index == 0, 1.0, 2.0).astype(jnp.float32).reshape(1, quarter)
    crossed = route_and_cross(plan, weight, whitened, sta_devices, seg_devices)
    square = stations_dev * stations_dev
    mine = crossed.reshape(seg_devices, 2, square, quarter)
    scaling = 1.0 / math.sqrt(4.0 * NBIN * all_windows)
    lagged = lag_transform(scaling, cos_table, sin_table, mine)
    return jnp.transpose(lagged, (1, 0, 2)).astype(jnp.float32)


def solution(mesh):
    in_specs = (P("sta", "seg", None), P())
    out_specs = P("seg", None, "sta")
    return jax.shard_map(
        per_device, mesh=mesh, in_specs=in_specs, out_specs=out_specs, check_vma=False
    )
```

```python
import functools
import math

import jax
import jax.numpy as jnp
from jax import lax
from jax.experimental import pallas as pl
from jax.experimental.pallas import tpu as pltpu
from jax.sharding import PartitionSpec as P

WLEN = 2048
NBIN = 1024
HALF = 64
ROUNDS = 4
LAGS = 2048


def band_mean(values, half_width):
    row_count, length = values.shape
    block_width = 2 * half_width
    blocks_count = length // block_width
    inside = jnp.arange(block_width, dtype=jnp.int32)
    source = inside[:, None]
    target = inside[None, :]
    inner_band = (jnp.abs(source - target) <= half_width).astype(jnp.bfloat16)
    before = (target + block_width - source <= half_width).astype(jnp.bfloat16)
    after_band = (source + block_width - target <= half_width).astype(jnp.bfloat16)
    blocks = values.reshape(row_count, blocks_count, block_width)
    earlier = jnp.pad(blocks[:, :-1], ((0, 0), (1, 0), (0, 0)))
    following = jnp.pad(blocks[:, 1:], ((0, 0), (0, 1), (0, 0)))
    flat_shape = (row_count * blocks_count, block_width)
    running = jnp.dot(blocks.reshape(flat_shape), inner_band, preferred_element_type=jnp.float32)
    running = running + jnp.dot(
        earlier.reshape(flat_shape), before, preferred_element_type=jnp.float32
    )
    running = running + jnp.dot(
        following.reshape(flat_shape), after_band, preferred_element_type=jnp.float32
    )
    position = jnp.arange(length, dtype=jnp.int32)
    counted = (
        jnp.minimum(position, half_width) + jnp.minimum(length - 1 - position, half_width) + 1
    ).astype(jnp.float32)
    return running.reshape(row_count, length) / counted


def angles_of(rows, step, bins, transform):
    phase_int = (rows[:, None] * step) * bins[None, :] % transform
    return phase_int.astype(jnp.float32) * (2.0 * math.pi / transform)


def fourier_tables(length, bin_count, transform):
    low_count = 64
    high_count = length // low_count
    bins = jnp.arange(bin_count, dtype=jnp.int32)
    high = angles_of(jnp.arange(high_count, dtype=jnp.int32), low_count, bins, transform)
    low = angles_of(jnp.arange(low_count, dtype=jnp.int32), 1, bins, transform)
    hc, hs = jnp.cos(high)[:, None], jnp.sin(high)[:, None]
    lc, ls = jnp.cos(low)[None], jnp.sin(low)[None]
    cos_part = (hc * lc - hs * ls).astype(jnp.bfloat16).reshape(length, bin_count)
    sin_part = (-(hs * lc + hc * ls)).astype(jnp.bfloat16).reshape(length, bin_count)
    return cos_part, sin_part


def cross_round(weight, own_ref, other_ref, r, dst):
    windows = own_ref.shape[1]
    stations = own_ref.shape[2]
    low = other_ref.shape[2]
    halves = stations // low
    group = 4

    def rows_of(c, w):
        first = (c * windows + w) * halves
        return jnp.concatenate(
            [other_ref[first + h, r].astype(jnp.float32) for h in range(halves)], axis=0
        )

    def body(index, carry):
        first = index * group
        acc_re = [None] * group
        acc_im = [None] * group
        for w in range(windows):
            pre = rows_of(0, w)
            pim = rows_of(1, w)
            for g in range(group):
                ore = own_ref[0, w, pl.ds(first + g, 1), :]
                oim = own_ref[1, w, pl.ds(first + g, 1), :]
                re = ore * pre + oim * pim
                im = oim * pre - ore * pim
                acc_re[g] = re if w == 0 else acc_re[g] + re
                acc_im[g] = im if w == 0 else acc_im[g] + im
        for g in range(group):
            rows = pl.ds(pl.multiple_of((first + g) * stations, stations), stations)
            dst[0, rows] = (acc_re[g] * weight).astype(dst.dtype)
            dst[1, rows] = (acc_im[g] * weight).astype(dst.dtype)
        return carry

    lax.fori_loop(0, stations // group, body, 0)


def lag_phase(scaling, cos_ref, sin_ref, y_ref, out_ref, staged, send_sems, recv_sems):
    count = out_ref.shape[0]
    chunk = out_ref.shape[1]
    quarter = y_ref.shape[3]
    rows = 128
    me = lax.axis_index("seg")
    row = lax.axis_index("sta")
    contract = (((1,), (1,)), ((), ()))

    def compute(target, dst):
        def body(index, carry):
            first = pl.multiple_of(target * chunk + index * rows, rows)
            acc = None
            for q in range(count):
                cols = pl.ds(q * quarter, quarter)
                for c, table in enumerate((cos_ref, sin_ref)):
                    part = lax.dot_general(
                        table[pl.ds(first, rows), cols], y_ref[q, c], contract,
                        preferred_element_type=jnp.float32,
                    )
                    acc = part if acc is None else acc + part
            local = pl.multiple_of(index * rows, rows)
            dst[pl.ds(local, rows), :] = (acc * scaling).astype(dst.dtype)
            return carry

        lax.fori_loop(0, chunk // rows, body, 0)

    copies = []
    for step in range(count - 1):
        target = lax.rem(me + 1 + step, count)
        compute(target, staged.at[step])
        copy = pltpu.make_async_remote_copy(
            src_ref=staged.at[step],
            dst_ref=out_ref.at[me],
            send_sem=send_sems.at[step],
            recv_sem=recv_sems.at[step],
            device_id=(row, target),
            device_id_type=pl.DeviceIdType.MESH,
        )
        copy.start()
        copies.append(copy)
    compute(me, out_ref.at[me])
    for copy in copies:
        copy.wait()


def route_kernel(scaling, plan_ref, weight_ref, x_ref, cos_ref, sin_ref, lag_ref, out_ref, own,
                 own_f, spread, outgoing, partner, staged, lag_staged, zero_sems, first_sems,
                 second_sems, cross_sems, lag_sends, lag_recvs):
    count = spread.shape[0]
    low = spread.shape[1]
    rounds = plan_ref.shape[0]
    parts = own.shape[1] // x_ref.shape[1]
    windows_dev = x_ref.shape[1]
    quarter = own.shape[3]
    windows = own.shape[1]
    halves = own.shape[2] // low
    stations = own.shape[2]
    me = lax.axis_index("sta")
    col = lax.axis_index("seg")
    mesh_ids = pl.DeviceIdType.MESH
    barrier = pltpu.get_barrier_semaphore()

    def greet(step, carry):
        pl.semaphore_signal(
            barrier, inc=1, device_id=(lax.rem(me + step, count), col), device_id_type=mesh_ids
        )
        return carry

    lax.fori_loop(1, count, greet, 0)
    for step in range(1, parts):
        pl.semaphore_signal(
            barrier, inc=1, device_id=(me, lax.rem(col + step, parts)), device_id_type=mesh_ids
        )
    pl.semaphore_wait(barrier, count - 1 + parts - 1)

    def describe_zero(step):
        target = lax.rem(col + step, parts)
        return pltpu.make_async_remote_copy(
            src_ref=x_ref.at[:, :, :, pl.ds(pl.multiple_of(target * quarter, quarter), quarter)],
            dst_ref=own.at[:, pl.ds(col * windows_dev, windows_dev)],
            send_sem=zero_sems.at[step],
            recv_sem=zero_sems.at[parts + step],
            device_id=(me, target),
            device_id_type=mesh_ids,
        )

    for step in range(1, parts):
        describe_zero(step).start()
    own[:, pl.ds(col * windows_dev, windows_dev)] = x_ref[
        :, :, :, pl.ds(pl.multiple_of(col * quarter, quarter), quarter)
    ]
    for step in range(1, parts):
        describe_zero(step).wait()

    def chunk_of(j):
        c = j // (windows * halves)
        w = lax.rem(j // halves, windows)
        s_hi = lax.rem(j, halves)
        return own.at[c, w, pl.ds(s_hi * low, low)]

    def describe_first(step):
        target = lax.rem(me + step, count)
        return pltpu.make_async_remote_copy(
            src_ref=chunk_of(target),
            dst_ref=spread.at[me],
            send_sem=first_sems.at[step],
            recv_sem=first_sems.at[count + step],
            device_id=(target, col),
            device_id_type=mesh_ids,
        )

    def send_first(step, carry):
        describe_first(step).start()
        return carry

    def finish_first(step, carry):
        describe_first(step).wait()
        return carry

    lax.fori_loop(1, count, send_first, 0)
    spread[me] = chunk_of(me)[...]
    lax.fori_loop(1, count, finish_first, 0)

    def pick(block, carry):
        for r in range(rounds):
            outgoing[block, r] = spread[plan_ref[r, block]]
        return carry

    lax.fori_loop(0, count, pick, 0)

    def round_of(order):
        return lax.rem(col + 1 + order, rounds)

    def describe_second(order, step):
        target = lax.rem(me + step, count)
        r = round_of(order)
        return pltpu.make_async_remote_copy(
            src_ref=outgoing.at[target, r],
            dst_ref=partner.at[me, r],
            send_sem=second_sems.at[order * count + step],
            recv_sem=second_sems.at[(rounds + order) * count + step],
            device_id=(target, col),
            device_id_type=mesh_ids,
        )

    for order in range(rounds):
        def send_second(step, carry, order=order):
            describe_second(order, step).start()
            return carry

        lax.fori_loop(1, count, send_second, 0)
    for r in range(rounds):
        partner[me, r] = outgoing[me, r]
    own_f[...] = own[...].astype(jnp.float32)
    weight = weight_ref[...]

    def describe_cross(order):
        target = round_of(order)
        return pltpu.make_async_remote_copy(
            src_ref=staged.at[order],
            dst_ref=out_ref.at[col],
            send_sem=cross_sems.at[order],
            recv_sem=cross_sems.at[rounds + order],
            device_id=(me, target),
            device_id_type=mesh_ids,
        )

    for order in range(rounds):
        def arrived(step, carry, order=order):
            describe_second(order, step).wait_recv()
            return carry

        lax.fori_loop(1, count, arrived, 0)
        r = round_of(order)
        if order < rounds - 1:
            cross_round(weight, own_f, partner, r, staged.at[order])
            describe_cross(order).start()
        else:
            cross_round(weight, own_f, partner, r, out_ref.at[col])

    for order in range(rounds):
        def sent(step, carry, order=order):
            describe_second(order, step).wait_send()
            return carry

        lax.fori_loop(1, count, sent, 0)
    for order in range(rounds - 1):
        describe_cross(order).wait()
    lag_phase(scaling, cos_ref, sin_ref, out_ref, lag_ref, lag_staged, lag_sends, lag_recvs)


def route_and_cross(scaling, plan, weight, x, cos_table, sin_table, count, parts):
    channels, windows_dev, stations, bins = x.shape
    rounds = plan.shape[0]
    quarter = bins // parts
    windows = windows_dev * parts
    low = channels * windows * stations // count
    square = stations * stations
    chunk = LAGS // parts
    vmem = pl.BlockSpec(memory_space=pltpu.VMEM)
    return pl.pallas_call(
        functools.partial(route_kernel, scaling),
        in_specs=[pl.BlockSpec(memory_space=pltpu.SMEM), vmem, vmem, vmem, vmem],
        out_specs=vmem,
        out_shape=jax.ShapeDtypeStruct((rounds, chunk, square), x.dtype),
        scratch_shapes=[
            pltpu.VMEM((parts, channels, square, quarter), x.dtype),
            pltpu.VMEM((channels, windows, stations, quarter), x.dtype),
            pltpu.VMEM((channels, windows, stations, quarter), jnp.float32),
            pltpu.VMEM((count, low, quarter), x.dtype),
            pltpu.VMEM((count, rounds, low, quarter), x.dtype),
            pltpu.VMEM((count, rounds, low, quarter), x.dtype),
            pltpu.VMEM((rounds - 1, channels, square, quarter), x.dtype),
            pltpu.VMEM((rounds - 1, chunk, square), x.dtype),
            pltpu.SemaphoreType.DMA((2 * parts,)),
            pltpu.SemaphoreType.DMA((2 * count,)),
            pltpu.SemaphoreType.DMA((2 * rounds * count,)),
            pltpu.SemaphoreType.DMA((2 * rounds,)),
            pltpu.SemaphoreType.DMA((rounds,)),
            pltpu.SemaphoreType.DMA((rounds,)),
        ],
        compiler_params=pltpu.CompilerParams(collective_id=2, has_side_effects=True),
    )(plan, weight, x, cos_table, sin_table)


def per_device(records, plan):
    stations_dev, windows, length = records.shape
    sta_devices = lax.axis_size("sta")
    seg_devices = lax.axis_size("seg")
    transform = 2 * length
    row_count = stations_dev * windows
    cos_table, sin_table = fourier_tables(length, NBIN, transform)
    signal = jnp.transpose(records, (1, 0, 2)).reshape(row_count, length)
    mean_level = band_mean(jnp.abs(signal).astype(jnp.bfloat16), HALF)
    flattened = (signal / (mean_level + 1e-05)).astype(jnp.bfloat16)
    spec_real = jnp.dot(flattened, cos_table, preferred_element_type=jnp.float32)
    spec_imag = jnp.dot(flattened, sin_table, preferred_element_type=jnp.float32)
    magnitude = jnp.sqrt(spec_real * spec_real + spec_imag * spec_imag).astype(jnp.bfloat16)
    smooth = band_mean(magnitude, HALF)
    whitened = jnp.stack(
        [spec_real / (smooth + 1e-06), spec_imag / (smooth + 1e-06)], axis=0
    ).astype(jnp.bfloat16)
    whitened = whitened.reshape(2, windows, stations_dev, NBIN)
    quarter = NBIN // seg_devices
    all_windows = windows * seg_devices
    first_bin = lax.axis_index("seg") * quarter
    bin_index = first_bin + jnp.arange(quarter, dtype=jnp.int32)
    weight = jnp.where(bin_index == 0, 1.0, 2.0).astype(jnp.float32).reshape(1, quarter)
    scaling = 1.0 / math.sqrt(4.0 * NBIN * all_windows)
    lagged = route_and_cross(
        scaling, plan, weight, whitened, cos_table, sin_table, sta_devices, seg_devices
    )
    return jnp.transpose(lagged, (1, 0, 2)).astype(jnp.float32)


def solution(mesh):
    in_specs = (P("sta", "seg", None), P())
    out_specs = P("seg", None, "sta")
    return jax.shard_map(
        per_device, mesh=mesh, in_specs=in_specs, out_specs=out_specs, check_vma=False
    )
```

```python
import functools
import math

import jax
import jax.numpy as jnp
from jax import lax
from jax.experimental import pallas as pl
from jax.experimental.pallas import tpu as pltpu
from jax.sharding import PartitionSpec as P

WLEN = 2048
NBIN = 1024
HALF = 64
ROUNDS = 4
LAGS = 2048


def band_mean(values, half_width):
    row_count, length = values.shape
    block_width = 2 * half_width
    blocks_count = length // block_width
    inside = jnp.arange(block_width, dtype=jnp.int32)
    source = inside[:, None]
    target = inside[None, :]
    inner_band = (jnp.abs(source - target) <= half_width).astype(jnp.bfloat16)
    before = (target + block_width - source <= half_width).astype(jnp.bfloat16)
    after_band = (source + block_width - target <= half_width).astype(jnp.bfloat16)
    blocks = values.reshape(row_count, blocks_count, block_width)
    earlier = jnp.pad(blocks[:, :-1], ((0, 0), (1, 0), (0, 0)))
    following = jnp.pad(blocks[:, 1:], ((0, 0), (0, 1), (0, 0)))
    flat_shape = (row_count * blocks_count, block_width)
    running = jnp.dot(blocks.reshape(flat_shape), inner_band, preferred_element_type=jnp.float32)
    running = running + jnp.dot(
        earlier.reshape(flat_shape), before, preferred_element_type=jnp.float32
    )
    running = running + jnp.dot(
        following.reshape(flat_shape), after_band, preferred_element_type=jnp.float32
    )
    position = jnp.arange(length, dtype=jnp.int32)
    counted = (
        jnp.minimum(position, half_width) + jnp.minimum(length - 1 - position, half_width) + 1
    ).astype(jnp.float32)
    return running.reshape(row_count, length) / counted


def angles_of(rows, step, bins, transform):
    phase_int = (rows[:, None] * step) * bins[None, :] % transform
    return phase_int.astype(jnp.float32) * (2.0 * math.pi / transform)


def fourier_tables(length, bin_count, transform):
    low_count = 64
    high_count = length // low_count
    bins = jnp.arange(bin_count, dtype=jnp.int32)
    high = angles_of(jnp.arange(high_count, dtype=jnp.int32), low_count, bins, transform)
    low = angles_of(jnp.arange(low_count, dtype=jnp.int32), 1, bins, transform)
    hc, hs = jnp.cos(high)[:, None], jnp.sin(high)[:, None]
    lc, ls = jnp.cos(low)[None], jnp.sin(low)[None]
    cos_part = (hc * lc - hs * ls).astype(jnp.bfloat16).reshape(length, bin_count)
    sin_part = (-(hs * lc + hc * ls)).astype(jnp.bfloat16).reshape(length, bin_count)
    return cos_part, sin_part


def cross_round(weight, own_ref, other_ref, r, dst):
    windows = own_ref.shape[1]
    stations = own_ref.shape[2]
    low = other_ref.shape[2]
    halves = stations // low
    group = 4

    def rows_of(c, w):
        first = (c * windows + w) * halves
        return jnp.concatenate(
            [other_ref[first + h, r].astype(jnp.float32) for h in range(halves)], axis=0
        )

    def body(index, carry):
        first = index * group
        acc_re = [None] * group
        acc_im = [None] * group
        for w in range(windows):
            pre = rows_of(0, w)
            pim = rows_of(1, w)
            for g in range(group):
                ore = own_ref[0, w, pl.ds(first + g, 1), :]
                oim = own_ref[1, w, pl.ds(first + g, 1), :]
                re = ore * pre + oim * pim
                im = oim * pre - ore * pim
                acc_re[g] = re if w == 0 else acc_re[g] + re
                acc_im[g] = im if w == 0 else acc_im[g] + im
        for g in range(group):
            rows = pl.ds(pl.multiple_of((first + g) * stations, stations), stations)
            dst[0, rows] = (acc_re[g] * weight).astype(dst.dtype)
            dst[1, rows] = (acc_im[g] * weight).astype(dst.dtype)
        return carry

    lax.fori_loop(0, stations // group, body, 0)


def lag_phase(scaling, cos_ref, sin_ref, y_ref, out_ref, staged, send_sems, recv_sems):
    count = out_ref.shape[0]
    chunk = out_ref.shape[1]
    quarter = y_ref.shape[3]
    rows = 128
    me = lax.axis_index("seg")
    row = lax.axis_index("sta")
    contract = (((1,), (1,)), ((), ()))

    def compute(target, dst):
        def body(index, carry):
            first = pl.multiple_of(target * chunk + index * rows, rows)
            acc = None
            for q in range(count):
                cols = pl.ds(q * quarter, quarter)
                for c, table in enumerate((cos_ref, sin_ref)):
                    part = lax.dot_general(
                        table[pl.ds(first, rows), cols], y_ref[q, c], contract,
                        preferred_element_type=jnp.float32,
                    )
                    acc = part if acc is None else acc + part
            local = pl.multiple_of(index * rows, rows)
            dst[pl.ds(local, rows), :] = (acc * scaling).astype(dst.dtype)
            return carry

        lax.fori_loop(0, chunk // rows, body, 0)

    copies = []
    for step in range(count - 1):
        target = lax.rem(me + 1 + step, count)
        compute(target, staged.at[step])
        copy = pltpu.make_async_remote_copy(
            src_ref=staged.at[step],
            dst_ref=out_ref.at[me],
            send_sem=send_sems.at[step],
            recv_sem=recv_sems.at[step],
            device_id=(row, target),
            device_id_type=pl.DeviceIdType.MESH,
        )
        copy.start()
        copies.append(copy)
    compute(me, out_ref.at[me])
    for copy in copies:
        copy.wait()


def route_kernel(scaling, plan_ref, weight_ref, x_ref, cos_ref, sin_ref, lag_ref, out_ref, own,
                 own_f, spread, outgoing, partner, staged, lag_staged, zero_sems, first_sems,
                 second_sems, cross_sems, lag_sends, lag_recvs):
    count = spread.shape[0]
    low = spread.shape[1]
    rounds = plan_ref.shape[0]
    parts = own.shape[1] // x_ref.shape[1]
    windows_dev = x_ref.shape[1]
    quarter = own.shape[3]
    windows = own.shape[1]
    halves = own.shape[2] // low
    stations = own.shape[2]
    me = lax.axis_index("sta")
    col = lax.axis_index("seg")
    mesh_ids = pl.DeviceIdType.MESH
    barrier = pltpu.get_barrier_semaphore()

    def greet(step, carry):
        pl.semaphore_signal(
            barrier, inc=1, device_id=(lax.rem(me + step, count), col), device_id_type=mesh_ids
        )
        return carry

    lax.fori_loop(1, count, greet, 0)
    for step in range(1, parts):
        pl.semaphore_signal(
            barrier, inc=1, device_id=(me, lax.rem(col + step, parts)), device_id_type=mesh_ids
        )
    pl.semaphore_wait(barrier, count - 1 + parts - 1)

    def describe_zero(step):
        target = lax.rem(col + step, parts)
        return pltpu.make_async_remote_copy(
            src_ref=x_ref.at[:, :, :, pl.ds(pl.multiple_of(target * quarter, quarter), quarter)],
            dst_ref=own.at[:, pl.ds(col * windows_dev, windows_dev)],
            send_sem=zero_sems.at[step],
            recv_sem=zero_sems.at[parts + step],
            device_id=(me, target),
            device_id_type=mesh_ids,
        )

    for step in range(1, parts):
        describe_zero(step).start()
    own[:, pl.ds(col * windows_dev, windows_dev)] = x_ref[
        :, :, :, pl.ds(pl.multiple_of(col * quarter, quarter), quarter)
    ]
    for step in range(1, parts):
        describe_zero(step).wait()

    def chunk_of(j):
        c = j // (windows * halves)
        w = lax.rem(j // halves, windows)
        s_hi = lax.rem(j, halves)
        return own.at[c, w, pl.ds(s_hi * low, low)]

    def describe_first(step):
        target = lax.rem(me + step, count)
        return pltpu.make_async_remote_copy(
            src_ref=chunk_of(target),
            dst_ref=spread.at[me],
            send_sem=first_sems.at[step],
            recv_sem=first_sems.at[count + step],
            device_id=(target, col),
            device_id_type=mesh_ids,
        )

    def send_first(step, carry):
        describe_first(step).start()
        return carry

    def finish_first(step, carry):
        describe_first(step).wait()
        return carry

    lax.fori_loop(1, count, send_first, 0)
    spread[me] = chunk_of(me)[...]
    lax.fori_loop(1, count, finish_first, 0)

    def round_of(order):
        return lax.rem(col + 1 + order, rounds)

    def describe_second(order, step):
        target = lax.rem(me + step, count)
        r = round_of(order)
        return pltpu.make_async_remote_copy(
            src_ref=outgoing.at[target, r],
            dst_ref=partner.at[me, r],
            send_sem=second_sems.at[order * count + step],
            recv_sem=second_sems.at[(rounds + order) * count + step],
            device_id=(target, col),
            device_id_type=mesh_ids,
        )

    for order in range(rounds):
        r = round_of(order)

        def pick(block, carry, r=r):
            outgoing[block, r] = spread[plan_ref[r, block]]
            return carry

        def send_second(step, carry, order=order):
            describe_second(order, step).start()
            return carry

        lax.fori_loop(0, count, pick, 0)
        lax.fori_loop(1, count, send_second, 0)
        partner[me, r] = outgoing[me, r]
    own_f[...] = own[...].astype(jnp.float32)
    weight = weight_ref[...]

    def describe_cross(order):
        target = round_of(order)
        return pltpu.make_async_remote_copy(
            src_ref=staged.at[order],
            dst_ref=out_ref.at[col],
            send_sem=cross_sems.at[order],
            recv_sem=cross_sems.at[rounds + order],
            device_id=(me, target),
            device_id_type=mesh_ids,
        )

    for order in range(rounds):
        def arrived(step, carry, order=order):
            describe_second(order, step).wait_recv()
            return carry

        lax.fori_loop(1, count, arrived, 0)
        r = round_of(order)
        if order < rounds - 1:
            cross_round(weight, own_f, partner, r, staged.at[order])
            describe_cross(order).start()
        else:
            cross_round(weight, own_f, partner, r, out_ref.at[col])

    for order in range(rounds):
        def sent(step, carry, order=order):
            describe_second(order, step).wait_send()
            return carry

        lax.fori_loop(1, count, sent, 0)
    for order in range(rounds - 1):
        describe_cross(order).wait()
    lag_phase(scaling, cos_ref, sin_ref, out_ref, lag_ref, lag_staged, lag_sends, lag_recvs)


def route_and_cross(scaling, plan, weight, x, cos_table, sin_table, count, parts):
    channels, windows_dev, stations, bins = x.shape
    rounds = plan.shape[0]
    quarter = bins // parts
    windows = windows_dev * parts
    low = channels * windows * stations // count
    square = stations * stations
    chunk = LAGS // parts
    vmem = pl.BlockSpec(memory_space=pltpu.VMEM)
    return pl.pallas_call(
        functools.partial(route_kernel, scaling),
        in_specs=[pl.BlockSpec(memory_space=pltpu.SMEM), vmem, vmem, vmem, vmem],
        out_specs=vmem,
        out_shape=jax.ShapeDtypeStruct((rounds, chunk, square), x.dtype),
        scratch_shapes=[
            pltpu.VMEM((parts, channels, square, quarter), x.dtype),
            pltpu.VMEM((channels, windows, stations, quarter), x.dtype),
            pltpu.VMEM((channels, windows, stations, quarter), jnp.float32),
            pltpu.VMEM((count, low, quarter), x.dtype),
            pltpu.VMEM((count, rounds, low, quarter), x.dtype),
            pltpu.VMEM((count, rounds, low, quarter), x.dtype),
            pltpu.VMEM((rounds - 1, channels, square, quarter), x.dtype),
            pltpu.VMEM((rounds - 1, chunk, square), x.dtype),
            pltpu.SemaphoreType.DMA((2 * parts,)),
            pltpu.SemaphoreType.DMA((2 * count,)),
            pltpu.SemaphoreType.DMA((2 * rounds * count,)),
            pltpu.SemaphoreType.DMA((2 * rounds,)),
            pltpu.SemaphoreType.DMA((rounds,)),
            pltpu.SemaphoreType.DMA((rounds,)),
        ],
        compiler_params=pltpu.CompilerParams(collective_id=2, has_side_effects=True),
    )(plan, weight, x, cos_table, sin_table)


def per_device(records, plan):
    stations_dev, windows, length = records.shape
    sta_devices = lax.axis_size("sta")
    seg_devices = lax.axis_size("seg")
    transform = 2 * length
    row_count = stations_dev * windows
    cos_table, sin_table = fourier_tables(length, NBIN, transform)
    signal = jnp.transpose(records, (1, 0, 2)).reshape(row_count, length)
    mean_level = band_mean(jnp.abs(signal).astype(jnp.bfloat16), HALF)
    flattened = (signal / (mean_level + 1e-05)).astype(jnp.bfloat16)
    spec_real = jnp.dot(flattened, cos_table, preferred_element_type=jnp.float32)
    spec_imag = jnp.dot(flattened, sin_table, preferred_element_type=jnp.float32)
    magnitude = jnp.sqrt(spec_real * spec_real + spec_imag * spec_imag).astype(jnp.bfloat16)
    smooth = band_mean(magnitude, HALF)
    whitened = jnp.stack(
        [spec_real / (smooth + 1e-06), spec_imag / (smooth + 1e-06)], axis=0
    ).astype(jnp.bfloat16)
    whitened = whitened.reshape(2, windows, stations_dev, NBIN)
    quarter = NBIN // seg_devices
    all_windows = windows * seg_devices
    first_bin = lax.axis_index("seg") * quarter
    bin_index = first_bin + jnp.arange(quarter, dtype=jnp.int32)
    weight = jnp.where(bin_index == 0, 1.0, 2.0).astype(jnp.float32).reshape(1, quarter)
    scaling = 1.0 / math.sqrt(4.0 * NBIN * all_windows)
    lagged = route_and_cross(
        scaling, plan, weight, whitened, cos_table, sin_table, sta_devices, seg_devices
    )
    return jnp.transpose(lagged, (1, 0, 2)).astype(jnp.float32)


def solution(mesh):
    in_specs = (P("sta", "seg", None), P())
    out_specs = P("seg", None, "sta")
    return jax.shard_map(
        per_device, mesh=mesh, in_specs=in_specs, out_specs=out_specs, check_vma=False
    )
```

```python
import functools
import math

import jax
import jax.numpy as jnp
from jax import lax
from jax.experimental import pallas as pl
from jax.experimental.pallas import tpu as pltpu
from jax.sharding import PartitionSpec as P

WLEN = 2048
NBIN = 1024
HALF = 64
ROUNDS = 4
LAGS = 2048


def band_mean(values, half_width):
    row_count, length = values.shape
    block_width = 2 * half_width
    blocks_count = length // block_width
    inside = jnp.arange(block_width, dtype=jnp.int32)
    source = inside[:, None]
    target = inside[None, :]
    inner_band = (jnp.abs(source - target) <= half_width).astype(jnp.bfloat16)
    before = (target + block_width - source <= half_width).astype(jnp.bfloat16)
    after_band = (source + block_width - target <= half_width).astype(jnp.bfloat16)
    blocks = values.reshape(row_count, blocks_count, block_width)
    earlier = jnp.pad(blocks[:, :-1], ((0, 0), (1, 0), (0, 0)))
    following = jnp.pad(blocks[:, 1:], ((0, 0), (0, 1), (0, 0)))
    flat_shape = (row_count * blocks_count, block_width)
    running = jnp.dot(blocks.reshape(flat_shape), inner_band, preferred_element_type=jnp.float32)
    running = running + jnp.dot(
        earlier.reshape(flat_shape), before, preferred_element_type=jnp.float32
    )
    running = running + jnp.dot(
        following.reshape(flat_shape), after_band, preferred_element_type=jnp.float32
    )
    position = jnp.arange(length, dtype=jnp.int32)
    counted = (
        jnp.minimum(position, half_width) + jnp.minimum(length - 1 - position, half_width) + 1
    ).astype(jnp.float32)
    return running.reshape(row_count, length) / counted


def angles_of(rows, step, bins, transform):
    phase_int = (rows[:, None] * step) * bins[None, :] % transform
    return phase_int.astype(jnp.float32) * (2.0 * math.pi / transform)


def fourier_tables(length, bin_count, transform):
    low_count = 64
    high_count = length // low_count
    bins = jnp.arange(bin_count, dtype=jnp.int32)
    high = angles_of(jnp.arange(high_count, dtype=jnp.int32), low_count, bins, transform)
    low = angles_of(jnp.arange(low_count, dtype=jnp.int32), 1, bins, transform)
    hc, hs = jnp.cos(high)[:, None], jnp.sin(high)[:, None]
    lc, ls = jnp.cos(low)[None], jnp.sin(low)[None]
    cos_part = (hc * lc - hs * ls).astype(jnp.bfloat16).reshape(length, bin_count)
    sin_part = (-(hs * lc + hc * ls)).astype(jnp.bfloat16).reshape(length, bin_count)
    return cos_part, sin_part


def cross_round(weight, own_ref, other_ref, r, dst):
    windows = own_ref.shape[1]
    stations = own_ref.shape[2]
    low = other_ref.shape[2]
    halves = stations // low
    group = 4

    def rows_of(c, w):
        first = (c * windows + w) * halves
        return jnp.concatenate(
            [other_ref[first + h, r].astype(jnp.float32) for h in range(halves)], axis=0
        )

    def body(index, carry):
        first = index * group
        acc_re = [None] * group
        acc_im = [None] * group
        for w in range(windows):
            pre = rows_of(0, w)
            pim = rows_of(1, w)
            for g in range(group):
                ore = own_ref[0, w, pl.ds(first + g, 1), :]
                oim = own_ref[1, w, pl.ds(first + g, 1), :]
                re = ore * pre + oim * pim
                im = oim * pre - ore * pim
                acc_re[g] = re if w == 0 else acc_re[g] + re
                acc_im[g] = im if w == 0 else acc_im[g] + im
        for g in range(group):
            rows = pl.ds(pl.multiple_of((first + g) * stations, stations), stations)
            dst[0, rows] = (acc_re[g] * weight).astype(dst.dtype)
            dst[1, rows] = (acc_im[g] * weight).astype(dst.dtype)
        return carry

    lax.fori_loop(0, stations // group, body, 0)


def lag_phase(scaling, cos_ref, sin_ref, y_ref, out_ref, staged, send_sems, recv_sems):
    count = out_ref.shape[0]
    chunk = out_ref.shape[1]
    quarter = y_ref.shape[3]
    rows = 128
    me = lax.axis_index("seg")
    row = lax.axis_index("sta")
    contract = (((1,), (1,)), ((), ()))

    def compute(target, dst):
        def body(index, carry):
            first = pl.multiple_of(target * chunk + index * rows, rows)
            acc = None
            for q in range(count):
                cols = pl.ds(q * quarter, quarter)
                for c, table in enumerate((cos_ref, sin_ref)):
                    part = lax.dot_general(
                        table[pl.ds(first, rows), cols], y_ref[q, c], contract,
                        preferred_element_type=jnp.float32,
                    )
                    acc = part if acc is None else acc + part
            local = pl.multiple_of(index * rows, rows)
            dst[pl.ds(local, rows), :] = (acc * scaling).astype(dst.dtype)
            return carry

        lax.fori_loop(0, chunk // rows, body, 0)

    copies = []
    for step in range(count - 1):
        target = lax.rem(me + 1 + step, count)
        compute(target, staged.at[step])
        copy = pltpu.make_async_remote_copy(
            src_ref=staged.at[step],
            dst_ref=out_ref.at[me],
            send_sem=send_sems.at[step],
            recv_sem=recv_sems.at[step],
            device_id=(row, target),
            device_id_type=pl.DeviceIdType.MESH,
        )
        copy.start()
        copies.append(copy)
    compute(me, out_ref.at[me])
    for copy in copies:
        copy.wait()


def route_kernel(scaling, plan_ref, weight_ref, x_ref, cos_ref, sin_ref, lag_ref, out_ref, own,
                 own_f, spread, outgoing, partner, staged, lag_staged, zero_sems, first_sems,
                 second_sems, cross_sems, lag_sends, lag_recvs):
    count = spread.shape[0]
    low = spread.shape[1]
    rounds = plan_ref.shape[0]
    parts = own.shape[1] // x_ref.shape[1]
    windows_dev = x_ref.shape[1]
    quarter = own.shape[3]
    windows = own.shape[1]
    halves = own.shape[2] // low
    stations = own.shape[2]
    me = lax.axis_index("sta")
    col = lax.axis_index("seg")
    mesh_ids = pl.DeviceIdType.MESH
    barrier = pltpu.get_barrier_semaphore()

    def greet(step, carry):
        pl.semaphore_signal(
            barrier, inc=1, device_id=(lax.rem(me + step, count), col), device_id_type=mesh_ids
        )
        return carry

    lax.fori_loop(1, count, greet, 0)
    for step in range(1, parts):
        pl.semaphore_signal(
            barrier, inc=1, device_id=(me, lax.rem(col + step, parts)), device_id_type=mesh_ids
        )
    pl.semaphore_wait(barrier, count - 1 + parts - 1)

    def describe_zero(step):
        target = lax.rem(col + step, parts)
        return pltpu.make_async_remote_copy(
            src_ref=x_ref.at[:, :, :, pl.ds(pl.multiple_of(target * quarter, quarter), quarter)],
            dst_ref=own.at[:, pl.ds(col * windows_dev, windows_dev)],
            send_sem=zero_sems.at[step],
            recv_sem=zero_sems.at[parts + step],
            device_id=(me, target),
            device_id_type=mesh_ids,
        )

    for step in range(1, parts):
        describe_zero(step).start()
    own[:, pl.ds(col * windows_dev, windows_dev)] = x_ref[
        :, :, :, pl.ds(pl.multiple_of(col * quarter, quarter), quarter)
    ]
    for step in range(1, parts):
        describe_zero(step).wait()

    def chunk_of(j):
        c = j // (windows * halves)
        w = lax.rem(j // halves, windows)
        s_hi = lax.rem(j, halves)
        return own.at[c, w, pl.ds(s_hi * low, low)]

    def describe_first(step):
        target = lax.rem(me + step, count)
        return pltpu.make_async_remote_copy(
            src_ref=chunk_of(target),
            dst_ref=spread.at[me],
            send_sem=first_sems.at[step],
            recv_sem=first_sems.at[count + step],
            device_id=(target, col),
            device_id_type=mesh_ids,
        )

    def send_first(step, carry):
        describe_first(step).start()
        return carry

    def finish_first(step, carry):
        describe_first(step).wait()
        return carry

    lax.fori_loop(1, count, send_first, 0)
    spread[me] = chunk_of(me)[...]
    lax.fori_loop(1, count, finish_first, 0)

    def round_of(order):
        return lax.rem(col + 1 + order, rounds)

    def describe_second(step):
        target = lax.rem(me + step, count)
        return pltpu.make_async_remote_copy(
            src_ref=outgoing.at[target],
            dst_ref=partner.at[me],
            send_sem=second_sems.at[step],
            recv_sem=second_sems.at[count + step],
            device_id=(target, col),
            device_id_type=mesh_ids,
        )

    def pick(block, carry):
        for r in range(rounds):
            outgoing[block, r] = spread[plan_ref[r, block]]
        return carry

    def send_second(step, carry):
        describe_second(step).start()
        return carry

    def finish_second(step, carry):
        describe_second(step).wait()
        return carry

    lax.fori_loop(0, count, pick, 0)
    lax.fori_loop(1, count, send_second, 0)
    partner[me] = outgoing[me]
    own_f[...] = own[...].astype(jnp.float32)
    weight = weight_ref[...]
    lax.fori_loop(1, count, finish_second, 0)

    def describe_cross(order):
        target = round_of(order)
        return pltpu.make_async_remote_copy(
            src_ref=staged.at[order],
            dst_ref=out_ref.at[col],
            send_sem=cross_sems.at[order],
            recv_sem=cross_sems.at[rounds + order],
            device_id=(me, target),
            device_id_type=mesh_ids,
        )

    for order in range(rounds):
        r = round_of(order)
        if order < rounds - 1:
            cross_round(weight, own_f, partner, r, staged.at[order])
            describe_cross(order).start()
        else:
            cross_round(weight, own_f, partner, r, out_ref.at[col])

    for order in range(rounds - 1):
        describe_cross(order).wait()
    lag_phase(scaling, cos_ref, sin_ref, out_ref, lag_ref, lag_staged, lag_sends, lag_recvs)


def route_and_cross(scaling, plan, weight, x, cos_table, sin_table, count, parts):
    channels, windows_dev, stations, bins = x.shape
    rounds = plan.shape[0]
    quarter = bins // parts
    windows = windows_dev * parts
    low = channels * windows * stations // count
    square = stations * stations
    chunk = LAGS // parts
    vmem = pl.BlockSpec(memory_space=pltpu.VMEM)
    return pl.pallas_call(
        functools.partial(route_kernel, scaling),
        in_specs=[pl.BlockSpec(memory_space=pltpu.SMEM), vmem, vmem, vmem, vmem],
        out_specs=vmem,
        out_shape=jax.ShapeDtypeStruct((rounds, chunk, square), x.dtype),
        scratch_shapes=[
            pltpu.VMEM((parts, channels, square, quarter), x.dtype),
            pltpu.VMEM((channels, windows, stations, quarter), x.dtype),
            pltpu.VMEM((channels, windows, stations, quarter), jnp.float32),
            pltpu.VMEM((count, low, quarter), x.dtype),
            pltpu.VMEM((count, rounds, low, quarter), x.dtype),
            pltpu.VMEM((count, rounds, low, quarter), x.dtype),
            pltpu.VMEM((rounds - 1, channels, square, quarter), x.dtype),
            pltpu.VMEM((rounds - 1, chunk, square), x.dtype),
            pltpu.SemaphoreType.DMA((2 * parts,)),
            pltpu.SemaphoreType.DMA((2 * count,)),
            pltpu.SemaphoreType.DMA((2 * count,)),
            pltpu.SemaphoreType.DMA((2 * rounds,)),
            pltpu.SemaphoreType.DMA((rounds,)),
            pltpu.SemaphoreType.DMA((rounds,)),
        ],
        compiler_params=pltpu.CompilerParams(collective_id=2, has_side_effects=True),
    )(plan, weight, x, cos_table, sin_table)


def per_device(records, plan):
    stations_dev, windows, length = records.shape
    sta_devices = lax.axis_size("sta")
    seg_devices = lax.axis_size("seg")
    transform = 2 * length
    row_count = stations_dev * windows
    cos_table, sin_table = fourier_tables(length, NBIN, transform)
    signal = jnp.transpose(records, (1, 0, 2)).reshape(row_count, length)
    mean_level = band_mean(jnp.abs(signal).astype(jnp.bfloat16), HALF)
    flattened = (signal / (mean_level + 1e-05)).astype(jnp.bfloat16)
    spec_real = jnp.dot(flattened, cos_table, preferred_element_type=jnp.float32)
    spec_imag = jnp.dot(flattened, sin_table, preferred_element_type=jnp.float32)
    magnitude = jnp.sqrt(spec_real * spec_real + spec_imag * spec_imag).astype(jnp.bfloat16)
    smooth = band_mean(magnitude, HALF)
    whitened = jnp.stack(
        [spec_real / (smooth + 1e-06), spec_imag / (smooth + 1e-06)], axis=0
    ).astype(jnp.bfloat16)
    whitened = whitened.reshape(2, windows, stations_dev, NBIN)
    quarter = NBIN // seg_devices
    all_windows = windows * seg_devices
    first_bin = lax.axis_index("seg") * quarter
    bin_index = first_bin + jnp.arange(quarter, dtype=jnp.int32)
    weight = jnp.where(bin_index == 0, 1.0, 2.0).astype(jnp.float32).reshape(1, quarter)
    scaling = 1.0 / math.sqrt(4.0 * NBIN * all_windows)
    lagged = route_and_cross(
        scaling, plan, weight, whitened, cos_table, sin_table, sta_devices, seg_devices
    )
    return jnp.transpose(lagged, (1, 0, 2)).astype(jnp.float32)


def solution(mesh):
    in_specs = (P("sta", "seg", None), P())
    out_specs = P("seg", None, "sta")
    return jax.shard_map(
        per_device, mesh=mesh, in_specs=in_specs, out_specs=out_specs, check_vma=False
    )
```

```python
import functools
import math

import jax
import jax.numpy as jnp
from jax import lax
from jax.experimental import pallas as pl
from jax.experimental.pallas import tpu as pltpu
from jax.sharding import PartitionSpec as P

WLEN = 2048
NBIN = 1024
HALF = 64
ROUNDS = 4
LAGS = 2048


def band_mean(values, half_width):
    row_count, length = values.shape
    block_width = 2 * half_width
    blocks_count = length // block_width
    inside = jnp.arange(block_width, dtype=jnp.int32)
    source = inside[:, None]
    target = inside[None, :]
    inner_band = (jnp.abs(source - target) <= half_width).astype(jnp.bfloat16)
    before = (target + block_width - source <= half_width).astype(jnp.bfloat16)
    after_band = (source + block_width - target <= half_width).astype(jnp.bfloat16)
    blocks = values.reshape(row_count, blocks_count, block_width)
    earlier = jnp.pad(blocks[:, :-1], ((0, 0), (1, 0), (0, 0)))
    following = jnp.pad(blocks[:, 1:], ((0, 0), (0, 1), (0, 0)))
    flat_shape = (row_count * blocks_count, block_width)
    running = jnp.dot(blocks.reshape(flat_shape), inner_band, preferred_element_type=jnp.float32)
    running = running + jnp.dot(
        earlier.reshape(flat_shape), before, preferred_element_type=jnp.float32
    )
    running = running + jnp.dot(
        following.reshape(flat_shape), after_band, preferred_element_type=jnp.float32
    )
    position = jnp.arange(length, dtype=jnp.int32)
    counted = (
        jnp.minimum(position, half_width) + jnp.minimum(length - 1 - position, half_width) + 1
    ).astype(jnp.float32)
    return running.reshape(row_count, length) / counted


def angles_of(rows, step, bins, transform):
    phase_int = (rows[:, None] * step) * bins[None, :] % transform
    return phase_int.astype(jnp.float32) * (2.0 * math.pi / transform)


def fourier_tables(length, bin_count, transform):
    low_count = 64
    high_count = length // low_count
    bins = jnp.arange(bin_count, dtype=jnp.int32)
    high = angles_of(jnp.arange(high_count, dtype=jnp.int32), low_count, bins, transform)
    low = angles_of(jnp.arange(low_count, dtype=jnp.int32), 1, bins, transform)
    hc, hs = jnp.cos(high)[:, None], jnp.sin(high)[:, None]
    lc, ls = jnp.cos(low)[None], jnp.sin(low)[None]
    cos_part = (hc * lc - hs * ls).astype(jnp.bfloat16).reshape(length, bin_count)
    sin_part = (-(hs * lc + hc * ls)).astype(jnp.bfloat16).reshape(length, bin_count)
    return cos_part, sin_part


def cross_round(weight, own_ref, other_ref, r, dst):
    windows = own_ref.shape[1]
    stations = own_ref.shape[2]
    low = other_ref.shape[2]
    halves = stations // low
    group = 4

    def rows_of(c, w):
        first = (c * windows + w) * halves
        return jnp.concatenate(
            [other_ref[first + h, r].astype(jnp.float32) for h in range(halves)], axis=0
        )

    def body(index, carry):
        first = index * group
        acc_re = [None] * group
        acc_im = [None] * group
        for w in range(windows):
            pre = rows_of(0, w)
            pim = rows_of(1, w)
            for g in range(group):
                ore = own_ref[0, w, pl.ds(first + g, 1), :]
                oim = own_ref[1, w, pl.ds(first + g, 1), :]
                re = ore * pre + oim * pim
                im = oim * pre - ore * pim
                acc_re[g] = re if w == 0 else acc_re[g] + re
                acc_im[g] = im if w == 0 else acc_im[g] + im
        for g in range(group):
            rows = pl.ds(pl.multiple_of((first + g) * stations, stations), stations)
            dst[0, rows] = (acc_re[g] * weight).astype(dst.dtype)
            dst[1, rows] = (acc_im[g] * weight).astype(dst.dtype)
        return carry

    lax.fori_loop(0, stations // group, body, 0)


def lag_phase(scaling, cos_ref, sin_ref, y_ref, out_ref, staged, send_sems, recv_sems):
    count = out_ref.shape[0]
    chunk = out_ref.shape[1]
    quarter = y_ref.shape[3]
    rows = 256
    me = lax.axis_index("seg")
    row = lax.axis_index("sta")
    contract = (((1,), (1,)), ((), ()))

    def compute(target, dst):
        def body(index, carry):
            first = pl.multiple_of(target * chunk + index * rows, rows)
            acc = None
            for q in range(count):
                cols = pl.ds(q * quarter, quarter)
                for c, table in enumerate((cos_ref, sin_ref)):
                    part = lax.dot_general(
                        table[pl.ds(first, rows), cols], y_ref[q, c], contract,
                        preferred_element_type=jnp.float32,
                    )
                    acc = part if acc is None else acc + part
            local = pl.multiple_of(index * rows, rows)
            dst[pl.ds(local, rows), :] = (acc * scaling).astype(dst.dtype)
            return carry

        lax.fori_loop(0, chunk // rows, body, 0)

    copies = []
    for step in range(count - 1):
        target = lax.rem(me + 1 + step, count)
        compute(target, staged.at[step])
        copy = pltpu.make_async_remote_copy(
            src_ref=staged.at[step],
            dst_ref=out_ref.at[me],
            send_sem=send_sems.at[step],
            recv_sem=recv_sems.at[step],
            device_id=(row, target),
            device_id_type=pl.DeviceIdType.MESH,
        )
        copy.start()
        copies.append(copy)
    compute(me, out_ref.at[me])
    for copy in copies:
        copy.wait()


def route_kernel(scaling, plan_ref, weight_ref, x_ref, cos_ref, sin_ref, lag_ref, out_ref, own,
                 own_f, spread, outgoing, partner, staged, lag_staged, zero_sems, first_sems,
                 second_sems, cross_sems, lag_sends, lag_recvs):
    count = spread.shape[0]
    low = spread.shape[1]
    rounds = plan_ref.shape[0]
    parts = own.shape[1] // x_ref.shape[1]
    windows_dev = x_ref.shape[1]
    quarter = own.shape[3]
    windows = own.shape[1]
    halves = own.shape[2] // low
    stations = own.shape[2]
    me = lax.axis_index("sta")
    col = lax.axis_index("seg")
    mesh_ids = pl.DeviceIdType.MESH
    barrier = pltpu.get_barrier_semaphore()

    def greet(step, carry):
        pl.semaphore_signal(
            barrier, inc=1, device_id=(lax.rem(me + step, count), col), device_id_type=mesh_ids
        )
        return carry

    lax.fori_loop(1, count, greet, 0)
    for step in range(1, parts):
        pl.semaphore_signal(
            barrier, inc=1, device_id=(me, lax.rem(col + step, parts)), device_id_type=mesh_ids
        )
    pl.semaphore_wait(barrier, count - 1 + parts - 1)

    def describe_zero(step):
        target = lax.rem(col + step, parts)
        return pltpu.make_async_remote_copy(
            src_ref=x_ref.at[:, :, :, pl.ds(pl.multiple_of(target * quarter, quarter), quarter)],
            dst_ref=own.at[:, pl.ds(col * windows_dev, windows_dev)],
            send_sem=zero_sems.at[step],
            recv_sem=zero_sems.at[parts + step],
            device_id=(me, target),
            device_id_type=mesh_ids,
        )

    for step in range(1, parts):
        describe_zero(step).start()
    own[:, pl.ds(col * windows_dev, windows_dev)] = x_ref[
        :, :, :, pl.ds(pl.multiple_of(col * quarter, quarter), quarter)
    ]
    for step in range(1, parts):
        describe_zero(step).wait()

    def chunk_of(j):
        c = j // (windows * halves)
        w = lax.rem(j // halves, windows)
        s_hi = lax.rem(j, halves)
        return own.at[c, w, pl.ds(s_hi * low, low)]

    def describe_first(step):
        target = lax.rem(me + step, count)
        return pltpu.make_async_remote_copy(
            src_ref=chunk_of(target),
            dst_ref=spread.at[me],
            send_sem=first_sems.at[step],
            recv_sem=first_sems.at[count + step],
            device_id=(target, col),
            device_id_type=mesh_ids,
        )

    def send_first(step, carry):
        describe_first(step).start()
        return carry

    def finish_first(step, carry):
        describe_first(step).wait()
        return carry

    lax.fori_loop(1, count, send_first, 0)
    spread[me] = chunk_of(me)[...]
    lax.fori_loop(1, count, finish_first, 0)

    def pick(block, carry):
        for r in range(rounds):
            outgoing[block, r] = spread[plan_ref[r, block]]
        return carry

    lax.fori_loop(0, count, pick, 0)

    def round_of(order):
        return lax.rem(col + 1 + order, rounds)

    def describe_second(order, step):
        target = lax.rem(me + step, count)
        r = round_of(order)
        return pltpu.make_async_remote_copy(
            src_ref=outgoing.at[target, r],
            dst_ref=partner.at[me, r],
            send_sem=second_sems.at[order * count + step],
            recv_sem=second_sems.at[(rounds + order) * count + step],
            device_id=(target, col),
            device_id_type=mesh_ids,
        )

    for order in range(rounds):
        def send_second(step, carry, order=order):
            describe_second(order, step).start()
            return carry

        lax.fori_loop(1, count, send_second, 0)
    for r in range(rounds):
        partner[me, r] = outgoing[me, r]
    own_f[...] = own[...].astype(jnp.float32)
    weight = weight_ref[...]

    def describe_cross(order):
        target = round_of(order)
        return pltpu.make_async_remote_copy(
            src_ref=staged.at[order],
            dst_ref=out_ref.at[col],
            send_sem=cross_sems.at[order],
            recv_sem=cross_sems.at[rounds + order],
            device_id=(me, target),
            device_id_type=mesh_ids,
        )

    for order in range(rounds):
        def arrived(step, carry, order=order):
            describe_second(order, step).wait_recv()
            return carry

        lax.fori_loop(1, count, arrived, 0)
        r = round_of(order)
        if order < rounds - 1:
            cross_round(weight, own_f, partner, r, staged.at[order])
            describe_cross(order).start()
        else:
            cross_round(weight, own_f, partner, r, out_ref.at[col])

    for order in range(rounds):
        def sent(step, carry, order=order):
            describe_second(order, step).wait_send()
            return carry

        lax.fori_loop(1, count, sent, 0)
    for order in range(rounds - 1):
        describe_cross(order).wait_recv()
    lag_phase(scaling, cos_ref, sin_ref, out_ref, lag_ref, lag_staged, lag_sends, lag_recvs)
    for order in range(rounds - 1):
        describe_cross(order).wait_send()


def route_and_cross(scaling, plan, weight, x, cos_table, sin_table, count, parts):
    channels, windows_dev, stations, bins = x.shape
    rounds = plan.shape[0]
    quarter = bins // parts
    windows = windows_dev * parts
    low = channels * windows * stations // count
    square = stations * stations
    chunk = LAGS // parts
    vmem = pl.BlockSpec(memory_space=pltpu.VMEM)
    return pl.pallas_call(
        functools.partial(route_kernel, scaling),
        in_specs=[pl.BlockSpec(memory_space=pltpu.SMEM), vmem, vmem, vmem, vmem],
        out_specs=vmem,
        out_shape=jax.ShapeDtypeStruct((rounds, chunk, square), x.dtype),
        scratch_shapes=[
            pltpu.VMEM((parts, channels, square, quarter), x.dtype),
            pltpu.VMEM((channels, windows, stations, quarter), x.dtype),
            pltpu.VMEM((channels, windows, stations, quarter), jnp.float32),
            pltpu.VMEM((count, low, quarter), x.dtype),
            pltpu.VMEM((count, rounds, low, quarter), x.dtype),
            pltpu.VMEM((count, rounds, low, quarter), x.dtype),
            pltpu.VMEM((rounds - 1, channels, square, quarter), x.dtype),
            pltpu.VMEM((rounds - 1, chunk, square), x.dtype),
            pltpu.SemaphoreType.DMA((2 * parts,)),
            pltpu.SemaphoreType.DMA((2 * count,)),
            pltpu.SemaphoreType.DMA((2 * rounds * count,)),
            pltpu.SemaphoreType.DMA((2 * rounds,)),
            pltpu.SemaphoreType.DMA((rounds,)),
            pltpu.SemaphoreType.DMA((rounds,)),
        ],
        compiler_params=pltpu.CompilerParams(collective_id=2, has_side_effects=True),
    )(plan, weight, x, cos_table, sin_table)


def per_device(records, plan):
    stations_dev, windows, length = records.shape
    sta_devices = lax.axis_size("sta")
    seg_devices = lax.axis_size("seg")
    transform = 2 * length
    row_count = stations_dev * windows
    cos_table, sin_table = fourier_tables(length, NBIN, transform)
    signal = jnp.transpose(records, (1, 0, 2)).reshape(row_count, length)
    mean_level = band_mean(jnp.abs(signal).astype(jnp.bfloat16), HALF)
    flattened = (signal / (mean_level + 1e-05)).astype(jnp.bfloat16)
    spec_real = jnp.dot(flattened, cos_table, preferred_element_type=jnp.float32)
    spec_imag = jnp.dot(flattened, sin_table, preferred_element_type=jnp.float32)
    magnitude = jnp.sqrt(spec_real * spec_real + spec_imag * spec_imag).astype(jnp.bfloat16)
    smooth = band_mean(magnitude, HALF)
    whitened = jnp.stack(
        [spec_real / (smooth + 1e-06), spec_imag / (smooth + 1e-06)], axis=0
    ).astype(jnp.bfloat16)
    whitened = whitened.reshape(2, windows, stations_dev, NBIN)
    quarter = NBIN // seg_devices
    all_windows = windows * seg_devices
    first_bin = lax.axis_index("seg") * quarter
    bin_index = first_bin + jnp.arange(quarter, dtype=jnp.int32)
    weight = jnp.where(bin_index == 0, 1.0, 2.0).astype(jnp.float32).reshape(1, quarter)
    scaling = 1.0 / math.sqrt(4.0 * NBIN * all_windows)
    lagged = route_and_cross(
        scaling, plan, weight, whitened, cos_table, sin_table, sta_devices, seg_devices
    )
    return jnp.transpose(lagged, (1, 0, 2)).astype(jnp.float32)


def solution(mesh):
    in_specs = (P("sta", "seg", None), P())
    out_specs = P("seg", None, "sta")
    return jax.shard_map(
        per_device, mesh=mesh, in_specs=in_specs, out_specs=out_specs, check_vma=False
    )
```

```python
import functools
import math

import jax
import jax.numpy as jnp
from jax import lax
from jax.experimental import pallas as pl
from jax.experimental.pallas import tpu as pltpu
from jax.sharding import PartitionSpec as P

WLEN = 2048
NBIN = 1024
HALF = 64
ROUNDS = 4
LAGS = 2048


def band_mean(values, half_width):
    row_count, length = values.shape
    block_width = 2 * half_width
    blocks_count = length // block_width
    inside = jnp.arange(block_width, dtype=jnp.int32)
    source = inside[:, None]
    target = inside[None, :]
    inner_band = (jnp.abs(source - target) <= half_width).astype(jnp.bfloat16)
    before = (target + block_width - source <= half_width).astype(jnp.bfloat16)
    after_band = (source + block_width - target <= half_width).astype(jnp.bfloat16)
    blocks = values.reshape(row_count, blocks_count, block_width)
    earlier = jnp.pad(blocks[:, :-1], ((0, 0), (1, 0), (0, 0)))
    following = jnp.pad(blocks[:, 1:], ((0, 0), (0, 1), (0, 0)))
    flat_shape = (row_count * blocks_count, block_width)
    running = jnp.dot(blocks.reshape(flat_shape), inner_band, preferred_element_type=jnp.float32)
    running = running + jnp.dot(
        earlier.reshape(flat_shape), before, preferred_element_type=jnp.float32
    )
    running = running + jnp.dot(
        following.reshape(flat_shape), after_band, preferred_element_type=jnp.float32
    )
    position = jnp.arange(length, dtype=jnp.int32)
    counted = (
        jnp.minimum(position, half_width) + jnp.minimum(length - 1 - position, half_width) + 1
    ).astype(jnp.float32)
    return running.reshape(row_count, length) / counted


def angles_of(rows, step, bins, transform):
    phase_int = (rows[:, None] * step) * bins[None, :] % transform
    return phase_int.astype(jnp.float32) * (2.0 * math.pi / transform)


def fourier_tables(length, bin_count, transform):
    low_count = 64
    high_count = length // low_count
    bins = jnp.arange(bin_count, dtype=jnp.int32)
    high = angles_of(jnp.arange(high_count, dtype=jnp.int32), low_count, bins, transform)
    low = angles_of(jnp.arange(low_count, dtype=jnp.int32), 1, bins, transform)
    hc, hs = jnp.cos(high)[:, None], jnp.sin(high)[:, None]
    lc, ls = jnp.cos(low)[None], jnp.sin(low)[None]
    cos_part = (hc * lc - hs * ls).astype(jnp.bfloat16).reshape(length, bin_count)
    sin_part = (-(hs * lc + hc * ls)).astype(jnp.bfloat16).reshape(length, bin_count)
    return cos_part, sin_part


def cross_round(weight, own_ref, other_ref, r, dst):
    windows = own_ref.shape[1]
    stations = own_ref.shape[2]
    low = other_ref.shape[2]
    halves = stations // low
    group = 4

    def rows_of(c, w):
        first = (c * windows + w) * halves
        return jnp.concatenate(
            [other_ref[first + h, r].astype(jnp.float32) for h in range(halves)], axis=0
        )

    def body(index, carry):
        first = index * group
        acc_re = [None] * group
        acc_im = [None] * group
        for w in range(windows):
            pre = rows_of(0, w)
            pim = rows_of(1, w)
            for g in range(group):
                ore = own_ref[0, w, pl.ds(first + g, 1), :]
                oim = own_ref[1, w, pl.ds(first + g, 1), :]
                re = ore * pre + oim * pim
                im = oim * pre - ore * pim
                acc_re[g] = re if w == 0 else acc_re[g] + re
                acc_im[g] = im if w == 0 else acc_im[g] + im
        for g in range(group):
            rows = pl.ds(pl.multiple_of((first + g) * stations, stations), stations)
            dst[0, rows] = (acc_re[g] * weight).astype(dst.dtype)
            dst[1, rows] = (acc_im[g] * weight).astype(dst.dtype)
        return carry

    lax.fori_loop(0, stations // group, body, 0)


def lag_phase(scaling, cos_ref, sin_ref, y_ref, out_ref, staged, send_sems, recv_sems):
    count = out_ref.shape[0]
    chunk = out_ref.shape[1]
    quarter = y_ref.shape[3]
    rows = 256
    me = lax.axis_index("seg")
    row = lax.axis_index("sta")
    contract = (((1,), (1,)), ((), ()))

    def compute(target, dst):
        def body(index, carry):
            first = pl.multiple_of(target * chunk + index * rows, rows)
            acc = None
            for q in range(count):
                cols = pl.ds(q * quarter, quarter)
                for c, table in enumerate((cos_ref, sin_ref)):
                    part = lax.dot_general(
                        table[pl.ds(first, rows), cols], y_ref[q, c], contract,
                        preferred_element_type=jnp.float32,
                    )
                    acc = part if acc is None else acc + part
            local = pl.multiple_of(index * rows, rows)
            dst[pl.ds(local, rows), :] = (acc * scaling).astype(dst.dtype)
            return carry

        lax.fori_loop(0, chunk // rows, body, 0)

    copies = []
    for step in range(count - 1):
        target = lax.rem(me + 1 + step, count)
        compute(target, staged.at[step])
        copy = pltpu.make_async_remote_copy(
            src_ref=staged.at[step],
            dst_ref=out_ref.at[me],
            send_sem=send_sems.at[step],
            recv_sem=recv_sems.at[step],
            device_id=(row, target),
            device_id_type=pl.DeviceIdType.MESH,
        )
        copy.start()
        copies.append(copy)
    compute(me, out_ref.at[me])
    for copy in copies:
        copy.wait()


def route_kernel(scaling, plan_ref, weight_ref, x_ref, cos_ref, sin_ref, lag_ref, out_ref, own,
                 own_f, spread, outgoing, partner, staged, lag_staged, zero_sems, first_sems,
                 second_sems, cross_sems, lag_sends, lag_recvs):
    count = spread.shape[0]
    low = spread.shape[1]
    rounds = plan_ref.shape[0]
    parts = own.shape[1] // x_ref.shape[1]
    windows_dev = x_ref.shape[1]
    quarter = own.shape[3]
    windows = own.shape[1]
    halves = own.shape[2] // low
    stations = own.shape[2]
    me = lax.axis_index("sta")
    col = lax.axis_index("seg")
    mesh_ids = pl.DeviceIdType.MESH
    barrier = pltpu.get_barrier_semaphore()

    def greet(step, carry):
        pl.semaphore_signal(
            barrier, inc=1, device_id=(lax.rem(me + step, count), col), device_id_type=mesh_ids
        )
        return carry

    lax.fori_loop(1, count, greet, 0)
    for step in range(1, parts):
        pl.semaphore_signal(
            barrier, inc=1, device_id=(me, lax.rem(col + step, parts)), device_id_type=mesh_ids
        )
    pl.semaphore_wait(barrier, count - 1 + parts - 1)

    def describe_zero(step):
        target = lax.rem(col + step, parts)
        return pltpu.make_async_remote_copy(
            src_ref=x_ref.at[:, :, :, pl.ds(pl.multiple_of(target * quarter, quarter), quarter)],
            dst_ref=own.at[:, pl.ds(col * windows_dev, windows_dev)],
            send_sem=zero_sems.at[step],
            recv_sem=zero_sems.at[parts + step],
            device_id=(me, target),
            device_id_type=mesh_ids,
        )

    for step in range(1, parts):
        describe_zero(step).start()
    local_zero = pltpu.make_async_copy(
        x_ref.at[:, :, :, pl.ds(pl.multiple_of(col * quarter, quarter), quarter)],
        own.at[:, pl.ds(col * windows_dev, windows_dev)],
        zero_sems.at[0],
    )
    local_zero.start()
    local_zero.wait()

    def chunk_of(j):
        c = j // (windows * halves)
        w = lax.rem(j // halves, windows)
        s_hi = lax.rem(j, halves)
        return own.at[c, w, pl.ds(s_hi * low, low)]

    def segment_of(j):
        return lax.rem(j // halves, windows) // windows_dev

    def describe_first(target, source):
        return pltpu.make_async_remote_copy(
            src_ref=chunk_of(target),
            dst_ref=spread.at[me],
            send_sem=first_sems.at[target],
            recv_sem=first_sems.at[count + source],
            device_id=(target, col),
            device_id_type=mesh_ids,
        )

    def send_local(step, carry):
        target = lax.rem(me + step, count)

        @pl.when(segment_of(target) == col)
        def _():
            describe_first(target, me).start()

        return carry

    def send_rest(step, carry):
        target = lax.rem(me + step, count)

        @pl.when(segment_of(target) != col)
        def _():
            describe_first(target, me).start()

        return carry

    def finish_first(step, carry):
        target = lax.rem(me + step, count)
        source = lax.rem(me + count - step, count)
        describe_first(target, me).wait_send()
        describe_first(me, source).wait_recv()
        return carry

    lax.fori_loop(1, count, send_local, 0)
    for step in range(1, parts):
        describe_zero(step).wait()
    lax.fori_loop(1, count, send_rest, 0)
    spread[me] = chunk_of(me)[...]
    lax.fori_loop(1, count, finish_first, 0)

    def pick(block, carry):
        for r in range(rounds):
            outgoing[block, r] = spread[plan_ref[r, block]]
        return carry

    lax.fori_loop(0, count, pick, 0)

    def round_of(order):
        return lax.rem(col + 1 + order, rounds)

    def describe_second(order, step):
        target = lax.rem(me + step, count)
        r = round_of(order)
        return pltpu.make_async_remote_copy(
            src_ref=outgoing.at[target, r],
            dst_ref=partner.at[me, r],
            send_sem=second_sems.at[order * count + step],
            recv_sem=second_sems.at[(rounds + order) * count + step],
            device_id=(target, col),
            device_id_type=mesh_ids,
        )

    for order in range(rounds):
        def send_second(step, carry, order=order):
            describe_second(order, step).start()
            return carry

        lax.fori_loop(1, count, send_second, 0)
    for r in range(rounds):
        partner[me, r] = outgoing[me, r]
    own_f[...] = own[...].astype(jnp.float32)
    weight = weight_ref[...]

    def describe_cross(order):
        target = round_of(order)
        return pltpu.make_async_remote_copy(
            src_ref=staged.at[order],
            dst_ref=out_ref.at[col],
            send_sem=cross_sems.at[order],
            recv_sem=cross_sems.at[rounds + order],
            device_id=(me, target),
            device_id_type=mesh_ids,
        )

    for order in range(rounds):
        def arrived(step, carry, order=order):
            describe_second(order, step).wait_recv()
            return carry

        lax.fori_loop(1, count, arrived, 0)
        r = round_of(order)
        if order < rounds - 1:
            cross_round(weight, own_f, partner, r, staged.at[order])
            describe_cross(order).start()
        else:
            cross_round(weight, own_f, partner, r, out_ref.at[col])

    for order in range(rounds):
        def sent(step, carry, order=order):
            describe_second(order, step).wait_send()
            return carry

        lax.fori_loop(1, count, sent, 0)
    for order in range(rounds - 1):
        describe_cross(order).wait_recv()
    lag_phase(scaling, cos_ref, sin_ref, out_ref, lag_ref, lag_staged, lag_sends, lag_recvs)
    for order in range(rounds - 1):
        describe_cross(order).wait_send()


def route_and_cross(scaling, plan, weight, x, cos_table, sin_table, count, parts):
    channels, windows_dev, stations, bins = x.shape
    rounds = plan.shape[0]
    quarter = bins // parts
    windows = windows_dev * parts
    low = channels * windows * stations // count
    square = stations * stations
    chunk = LAGS // parts
    vmem = pl.BlockSpec(memory_space=pltpu.VMEM)
    return pl.pallas_call(
        functools.partial(route_kernel, scaling),
        in_specs=[pl.BlockSpec(memory_space=pltpu.SMEM), vmem, vmem, vmem, vmem],
        out_specs=vmem,
        out_shape=jax.ShapeDtypeStruct((rounds, chunk, square), x.dtype),
        scratch_shapes=[
            pltpu.VMEM((parts, channels, square, quarter), x.dtype),
            pltpu.VMEM((channels, windows, stations, quarter), x.dtype),
            pltpu.VMEM((channels, windows, stations, quarter), jnp.float32),
            pltpu.VMEM((count, low, quarter), x.dtype),
            pltpu.VMEM((count, rounds, low, quarter), x.dtype),
            pltpu.VMEM((count, rounds, low, quarter), x.dtype),
            pltpu.VMEM((rounds - 1, channels, square, quarter), x.dtype),
            pltpu.VMEM((rounds - 1, chunk, square), x.dtype),
            pltpu.SemaphoreType.DMA((2 * parts,)),
            pltpu.SemaphoreType.DMA((2 * count,)),
            pltpu.SemaphoreType.DMA((2 * rounds * count,)),
            pltpu.SemaphoreType.DMA((2 * rounds,)),
            pltpu.SemaphoreType.DMA((rounds,)),
            pltpu.SemaphoreType.DMA((rounds,)),
        ],
        compiler_params=pltpu.CompilerParams(collective_id=2, has_side_effects=True),
    )(plan, weight, x, cos_table, sin_table)


def per_device(records, plan):
    stations_dev, windows, length = records.shape
    sta_devices = lax.axis_size("sta")
    seg_devices = lax.axis_size("seg")
    transform = 2 * length
    row_count = stations_dev * windows
    cos_table, sin_table = fourier_tables(length, NBIN, transform)
    signal = jnp.transpose(records, (1, 0, 2)).reshape(row_count, length)
    mean_level = band_mean(jnp.abs(signal).astype(jnp.bfloat16), HALF)
    flattened = (signal / (mean_level + 1e-05)).astype(jnp.bfloat16)
    spec_real = jnp.dot(flattened, cos_table, preferred_element_type=jnp.float32)
    spec_imag = jnp.dot(flattened, sin_table, preferred_element_type=jnp.float32)
    magnitude = jnp.sqrt(spec_real * spec_real + spec_imag * spec_imag).astype(jnp.bfloat16)
    smooth = band_mean(magnitude, HALF)
    whitened = jnp.stack(
        [spec_real / (smooth + 1e-06), spec_imag / (smooth + 1e-06)], axis=0
    ).astype(jnp.bfloat16)
    whitened = whitened.reshape(2, windows, stations_dev, NBIN)
    quarter = NBIN // seg_devices
    all_windows = windows * seg_devices
    first_bin = lax.axis_index("seg") * quarter
    bin_index = first_bin + jnp.arange(quarter, dtype=jnp.int32)
    weight = jnp.where(bin_index == 0, 1.0, 2.0).astype(jnp.float32).reshape(1, quarter)
    scaling = 1.0 / math.sqrt(4.0 * NBIN * all_windows)
    lagged = route_and_cross(
        scaling, plan, weight, whitened, cos_table, sin_table, sta_devices, seg_devices
    )
    return jnp.transpose(lagged, (1, 0, 2)).astype(jnp.float32)


def solution(mesh):
    in_specs = (P("sta", "seg", None), P())
    out_specs = P("seg", None, "sta")
    return jax.shard_map(
        per_device, mesh=mesh, in_specs=in_specs, out_specs=out_specs, check_vma=False
    )
```

```python
import functools
import math

import jax
import jax.numpy as jnp
from jax import lax
from jax.experimental import pallas as pl
from jax.experimental.pallas import tpu as pltpu
from jax.sharding import PartitionSpec as P

WLEN = 2048
NBIN = 1024
HALF = 64
ROUNDS = 4
LAGS = 2048


def band_mean(values, half_width):
    row_count, length = values.shape
    block_width = 2 * half_width
    blocks_count = length // block_width
    inside = jnp.arange(block_width, dtype=jnp.int32)
    source = inside[:, None]
    target = inside[None, :]
    inner_band = (jnp.abs(source - target) <= half_width).astype(jnp.bfloat16)
    before = (target + block_width - source <= half_width).astype(jnp.bfloat16)
    after_band = (source + block_width - target <= half_width).astype(jnp.bfloat16)
    blocks = values.reshape(row_count, blocks_count, block_width)
    earlier = jnp.pad(blocks[:, :-1], ((0, 0), (1, 0), (0, 0)))
    following = jnp.pad(blocks[:, 1:], ((0, 0), (0, 1), (0, 0)))
    flat_shape = (row_count * blocks_count, block_width)
    running = jnp.dot(blocks.reshape(flat_shape), inner_band, preferred_element_type=jnp.float32)
    running = running + jnp.dot(
        earlier.reshape(flat_shape), before, preferred_element_type=jnp.float32
    )
    running = running + jnp.dot(
        following.reshape(flat_shape), after_band, preferred_element_type=jnp.float32
    )
    position = jnp.arange(length, dtype=jnp.int32)
    counted = (
        jnp.minimum(position, half_width) + jnp.minimum(length - 1 - position, half_width) + 1
    ).astype(jnp.float32)
    return running.reshape(row_count, length) / counted


def angles_of(rows, step, bins, transform):
    phase_int = (rows[:, None] * step) * bins[None, :] % transform
    return phase_int.astype(jnp.float32) * (2.0 * math.pi / transform)


def fourier_tables(length, bin_count, transform):
    low_count = 64
    high_count = length // low_count
    bins = jnp.arange(bin_count, dtype=jnp.int32)
    high = angles_of(jnp.arange(high_count, dtype=jnp.int32), low_count, bins, transform)
    low = angles_of(jnp.arange(low_count, dtype=jnp.int32), 1, bins, transform)
    hc, hs = jnp.cos(high)[:, None], jnp.sin(high)[:, None]
    lc, ls = jnp.cos(low)[None], jnp.sin(low)[None]
    cos_part = (hc * lc - hs * ls).astype(jnp.bfloat16).reshape(length, bin_count)
    sin_part = (-(hs * lc + hc * ls)).astype(jnp.bfloat16).reshape(length, bin_count)
    return cos_part, sin_part


def cross_round(weight, own_ref, other_ref, r, dst):
    windows = own_ref.shape[1]
    stations = own_ref.shape[2]
    low = other_ref.shape[2]
    halves = stations // low
    group = 4

    def rows_of(c, w):
        first = (c * windows + w) * halves
        return jnp.concatenate(
            [other_ref[first + h, r].astype(jnp.float32) for h in range(halves)], axis=0
        )

    def body(index, carry):
        first = index * group
        acc_re = [None] * group
        acc_im = [None] * group
        for w in range(windows):
            pre = rows_of(0, w)
            pim = rows_of(1, w)
            for g in range(group):
                ore = own_ref[0, w, pl.ds(first + g, 1), :]
                oim = own_ref[1, w, pl.ds(first + g, 1), :]
                re = ore * pre + oim * pim
                im = oim * pre - ore * pim
                acc_re[g] = re if w == 0 else acc_re[g] + re
                acc_im[g] = im if w == 0 else acc_im[g] + im
        for g in range(group):
            rows = pl.ds(pl.multiple_of((first + g) * stations, stations), stations)
            dst[0, rows] = (acc_re[g] * weight).astype(dst.dtype)
            dst[1, rows] = (acc_im[g] * weight).astype(dst.dtype)
        return carry

    lax.fori_loop(0, stations // group, body, 0)


def lag_phase(scaling, cos_ref, sin_ref, y_ref, out_ref, staged, send_sems, recv_sems):
    count = out_ref.shape[0]
    chunk = out_ref.shape[1]
    quarter = y_ref.shape[3]
    rows = 256
    me = lax.axis_index("seg")
    row = lax.axis_index("sta")
    contract = (((1,), (1,)), ((), ()))

    def compute(target, dst):
        def body(index, carry):
            first = pl.multiple_of(target * chunk + index * rows, rows)
            acc = None
            for q in range(count):
                cols = pl.ds(q * quarter, quarter)
                for c, table in enumerate((cos_ref, sin_ref)):
                    part = lax.dot_general(
                        table[pl.ds(first, rows), cols], y_ref[q, c], contract,
                        preferred_element_type=jnp.float32,
                    )
                    acc = part if acc is None else acc + part
            local = pl.multiple_of(index * rows, rows)
            dst[pl.ds(local, rows), :] = (acc * scaling).astype(dst.dtype)
            return carry

        lax.fori_loop(0, chunk // rows, body, 0)

    copies = []
    for step in range(count - 1):
        target = lax.rem(me + 1 + step, count)
        compute(target, staged.at[step])
        copy = pltpu.make_async_remote_copy(
            src_ref=staged.at[step],
            dst_ref=out_ref.at[me],
            send_sem=send_sems.at[step],
            recv_sem=recv_sems.at[step],
            device_id=(row, target),
            device_id_type=pl.DeviceIdType.MESH,
        )
        copy.start()
        copies.append(copy)
    compute(me, out_ref.at[me])
    for copy in copies:
        copy.wait()


def route_kernel(scaling, plan_ref, weight_ref, x_ref, cos_ref, sin_ref, lag_ref, out_ref, own,
                 own_f, spread, outgoing, partner, staged, lag_staged, zero_sems, first_sems,
                 second_sems, cross_sems, lag_sends, lag_recvs):
    count = spread.shape[0]
    low = spread.shape[1]
    rounds = plan_ref.shape[0]
    parts = own.shape[1] // x_ref.shape[1]
    windows_dev = x_ref.shape[1]
    quarter = own.shape[3]
    windows = own.shape[1]
    halves = own.shape[2] // low
    stations = own.shape[2]
    me = lax.axis_index("sta")
    col = lax.axis_index("seg")
    mesh_ids = pl.DeviceIdType.MESH
    barrier = pltpu.get_barrier_semaphore()

    def greet(step, carry):
        pl.semaphore_signal(
            barrier, inc=1, device_id=(lax.rem(me + step, count), col), device_id_type=mesh_ids
        )
        return carry

    lax.fori_loop(1, count, greet, 0)
    for step in range(1, parts):
        pl.semaphore_signal(
            barrier, inc=1, device_id=(me, lax.rem(col + step, parts)), device_id_type=mesh_ids
        )
    pl.semaphore_wait(barrier, count - 1 + parts - 1)

    def describe_zero(step):
        target = lax.rem(col + step, parts)
        return pltpu.make_async_remote_copy(
            src_ref=x_ref.at[:, :, :, pl.ds(pl.multiple_of(target * quarter, quarter), quarter)],
            dst_ref=own.at[:, pl.ds(col * windows_dev, windows_dev)],
            send_sem=zero_sems.at[step],
            recv_sem=zero_sems.at[parts + step],
            device_id=(me, target),
            device_id_type=mesh_ids,
        )

    for step in range(1, parts):
        describe_zero(step).start()
    local_zero = pltpu.make_async_copy(
        x_ref.at[:, :, :, pl.ds(pl.multiple_of(col * quarter, quarter), quarter)],
        own.at[:, pl.ds(col * windows_dev, windows_dev)],
        zero_sems.at[0],
    )
    local_zero.start()
    local_zero.wait()

    def chunk_of(j):
        c = j // (windows * halves)
        w = lax.rem(j // halves, windows)
        s_hi = lax.rem(j, halves)
        return own.at[c, w, pl.ds(s_hi * low, low)]

    def segment_of(j):
        return lax.rem(j // halves, windows) // windows_dev

    def describe_first(target, source):
        return pltpu.make_async_remote_copy(
            src_ref=chunk_of(target),
            dst_ref=spread.at[me],
            send_sem=first_sems.at[target],
            recv_sem=first_sems.at[count + source],
            device_id=(target, col),
            device_id_type=mesh_ids,
        )

    def send_local(step, carry):
        target = lax.rem(me + step, count)

        @pl.when(segment_of(target) == col)
        def _():
            describe_first(target, me).start()

        return carry

    def send_segment(segment):
        def body(step, carry):
            target = lax.rem(me + step, count)

            @pl.when(segment_of(target) == segment)
            def _():
                describe_first(target, me).start()

            return carry

        return body

    def finish_first(step, carry):
        target = lax.rem(me + step, count)
        source = lax.rem(me + count - step, count)
        describe_first(target, me).wait_send()
        describe_first(me, source).wait_recv()
        return carry

    lax.fori_loop(1, count, send_local, 0)
    for step in range(1, parts):
        describe_zero(step).wait_recv()
        lax.fori_loop(1, count, send_segment(lax.rem(col + parts - step, parts)), 0)
    for step in range(1, parts):
        describe_zero(step).wait_send()
    spread[me] = chunk_of(me)[...]
    lax.fori_loop(1, count, finish_first, 0)

    def pick(block, carry):
        for r in range(rounds):
            outgoing[block, r] = spread[plan_ref[r, block]]
        return carry

    lax.fori_loop(0, count, pick, 0)

    def round_of(order):
        return lax.rem(col + 1 + order, rounds)

    def describe_second(order, step):
        target = lax.rem(me + step, count)
        r = round_of(order)
        return pltpu.make_async_remote_copy(
            src_ref=outgoing.at[target, r],
            dst_ref=partner.at[me, r],
            send_sem=second_sems.at[order * count + step],
            recv_sem=second_sems.at[(rounds + order) * count + step],
            device_id=(target, col),
            device_id_type=mesh_ids,
        )

    for order in range(rounds):
        def send_second(step, carry, order=order):
            describe_second(order, step).start()
            return carry

        lax.fori_loop(1, count, send_second, 0)
    for r in range(rounds):
        partner[me, r] = outgoing[me, r]
    own_f[...] = own[...].astype(jnp.float32)
    weight = weight_ref[...]

    def describe_cross(order):
        target = round_of(order)
        return pltpu.make_async_remote_copy(
            src_ref=staged.at[order],
            dst_ref=out_ref.at[col],
            send_sem=cross_sems.at[order],
            recv_sem=cross_sems.at[rounds + order],
            device_id=(me, target),
            device_id_type=mesh_ids,
        )

    for order in range(rounds):
        def arrived(step, carry, order=order):
            describe_second(order, step).wait_recv()
            return carry

        lax.fori_loop(1, count, arrived, 0)
        r = round_of(order)
        if order < rounds - 1:
            cross_round(weight, own_f, partner, r, staged.at[order])
            describe_cross(order).start()
        else:
            cross_round(weight, own_f, partner, r, out_ref.at[col])

    for order in range(rounds):
        def sent(step, carry, order=order):
            describe_second(order, step).wait_send()
            return carry

        lax.fori_loop(1, count, sent, 0)
    for order in range(rounds - 1):
        describe_cross(order).wait_recv()
    lag_phase(scaling, cos_ref, sin_ref, out_ref, lag_ref, lag_staged, lag_sends, lag_recvs)
    for order in range(rounds - 1):
        describe_cross(order).wait_send()


def route_and_cross(scaling, plan, weight, x, cos_table, sin_table, count, parts):
    channels, windows_dev, stations, bins = x.shape
    rounds = plan.shape[0]
    quarter = bins // parts
    windows = windows_dev * parts
    low = channels * windows * stations // count
    square = stations * stations
    chunk = LAGS // parts
    vmem = pl.BlockSpec(memory_space=pltpu.VMEM)
    return pl.pallas_call(
        functools.partial(route_kernel, scaling),
        in_specs=[pl.BlockSpec(memory_space=pltpu.SMEM), vmem, vmem, vmem, vmem],
        out_specs=vmem,
        out_shape=jax.ShapeDtypeStruct((rounds, chunk, square), x.dtype),
        scratch_shapes=[
            pltpu.VMEM((parts, channels, square, quarter), x.dtype),
            pltpu.VMEM((channels, windows, stations, quarter), x.dtype),
            pltpu.VMEM((channels, windows, stations, quarter), jnp.float32),
            pltpu.VMEM((count, low, quarter), x.dtype),
            pltpu.VMEM((count, rounds, low, quarter), x.dtype),
            pltpu.VMEM((count, rounds, low, quarter), x.dtype),
            pltpu.VMEM((rounds - 1, channels, square, quarter), x.dtype),
            pltpu.VMEM((rounds - 1, chunk, square), x.dtype),
            pltpu.SemaphoreType.DMA((2 * parts,)),
            pltpu.SemaphoreType.DMA((2 * count,)),
            pltpu.SemaphoreType.DMA((2 * rounds * count,)),
            pltpu.SemaphoreType.DMA((2 * rounds,)),
            pltpu.SemaphoreType.DMA((rounds,)),
            pltpu.SemaphoreType.DMA((rounds,)),
        ],
        compiler_params=pltpu.CompilerParams(collective_id=2, has_side_effects=True),
    )(plan, weight, x, cos_table, sin_table)


def per_device(records, plan):
    stations_dev, windows, length = records.shape
    sta_devices = lax.axis_size("sta")
    seg_devices = lax.axis_size("seg")
    transform = 2 * length
    row_count = stations_dev * windows
    cos_table, sin_table = fourier_tables(length, NBIN, transform)
    signal = jnp.transpose(records, (1, 0, 2)).reshape(row_count, length)
    mean_level = band_mean(jnp.abs(signal).astype(jnp.bfloat16), HALF)
    flattened = (signal / (mean_level + 1e-05)).astype(jnp.bfloat16)
    spec_real = jnp.dot(flattened, cos_table, preferred_element_type=jnp.float32)
    spec_imag = jnp.dot(flattened, sin_table, preferred_element_type=jnp.float32)
    magnitude = jnp.sqrt(spec_real * spec_real + spec_imag * spec_imag).astype(jnp.bfloat16)
    smooth = band_mean(magnitude, HALF)
    whitened = jnp.stack(
        [spec_real / (smooth + 1e-06), spec_imag / (smooth + 1e-06)], axis=0
    ).astype(jnp.bfloat16)
    whitened = whitened.reshape(2, windows, stations_dev, NBIN)
    quarter = NBIN // seg_devices
    all_windows = windows * seg_devices
    first_bin = lax.axis_index("seg") * quarter
    bin_index = first_bin + jnp.arange(quarter, dtype=jnp.int32)
    weight = jnp.where(bin_index == 0, 1.0, 2.0).astype(jnp.float32).reshape(1, quarter)
    scaling = 1.0 / math.sqrt(4.0 * NBIN * all_windows)
    lagged = route_and_cross(
        scaling, plan, weight, whitened, cos_table, sin_table, sta_devices, seg_devices
    )
    return jnp.transpose(lagged, (1, 0, 2)).astype(jnp.float32)


def solution(mesh):
    in_specs = (P("sta", "seg", None), P())
    out_specs = P("seg", None, "sta")
    return jax.shard_map(
        per_device, mesh=mesh, in_specs=in_specs, out_specs=out_specs, check_vma=False
    )
```

```python
import functools
import math

import jax
import jax.numpy as jnp
from jax import lax
from jax.experimental import pallas as pl
from jax.experimental.pallas import tpu as pltpu
from jax.sharding import PartitionSpec as P

WLEN = 2048
NBIN = 1024
HALF = 64
ROUNDS = 4
LAGS = 2048


def band_mean(values, half_width):
    row_count, length = values.shape
    block_width = 2 * half_width
    blocks_count = length // block_width
    inside = jnp.arange(block_width, dtype=jnp.int32)
    source = inside[:, None]
    target = inside[None, :]
    inner_band = (jnp.abs(source - target) <= half_width).astype(jnp.bfloat16)
    before = (target + block_width - source <= half_width).astype(jnp.bfloat16)
    after_band = (source + block_width - target <= half_width).astype(jnp.bfloat16)
    blocks = values.reshape(row_count, blocks_count, block_width)
    earlier = jnp.pad(blocks[:, :-1], ((0, 0), (1, 0), (0, 0)))
    following = jnp.pad(blocks[:, 1:], ((0, 0), (0, 1), (0, 0)))
    flat_shape = (row_count * blocks_count, block_width)
    running = jnp.dot(blocks.reshape(flat_shape), inner_band, preferred_element_type=jnp.float32)
    running = running + jnp.dot(
        earlier.reshape(flat_shape), before, preferred_element_type=jnp.float32
    )
    running = running + jnp.dot(
        following.reshape(flat_shape), after_band, preferred_element_type=jnp.float32
    )
    position = jnp.arange(length, dtype=jnp.int32)
    counted = (
        jnp.minimum(position, half_width) + jnp.minimum(length - 1 - position, half_width) + 1
    ).astype(jnp.float32)
    return running.reshape(row_count, length) / counted


def angles_of(rows, step, bins, transform):
    phase_int = (rows[:, None] * step) * bins[None, :] % transform
    return phase_int.astype(jnp.float32) * (2.0 * math.pi / transform)


def fourier_tables(length, bin_count, transform):
    low_count = 64
    high_count = length // low_count
    bins = jnp.arange(bin_count, dtype=jnp.int32)
    high = angles_of(jnp.arange(high_count, dtype=jnp.int32), low_count, bins, transform)
    low = angles_of(jnp.arange(low_count, dtype=jnp.int32), 1, bins, transform)
    hc, hs = jnp.cos(high)[:, None], jnp.sin(high)[:, None]
    lc, ls = jnp.cos(low)[None], jnp.sin(low)[None]
    cos_part = (hc * lc - hs * ls).astype(jnp.bfloat16).reshape(length, bin_count)
    sin_part = (-(hs * lc + hc * ls)).astype(jnp.bfloat16).reshape(length, bin_count)
    return cos_part, sin_part


def cross_round(weight, own_ref, other_ref, r, dst):
    windows = own_ref.shape[1]
    stations = own_ref.shape[2]
    low = other_ref.shape[2]
    halves = stations // low
    group = 4

    def rows_of(c, w):
        first = (c * windows + w) * halves
        return jnp.concatenate(
            [other_ref[first + h, r].astype(jnp.float32) for h in range(halves)], axis=0
        )

    def body(index, carry):
        first = index * group
        acc_re = [None] * group
        acc_im = [None] * group
        for w in range(windows):
            pre = rows_of(0, w)
            pim = rows_of(1, w)
            for g in range(group):
                ore = own_ref[0, w, pl.ds(first + g, 1), :]
                oim = own_ref[1, w, pl.ds(first + g, 1), :]
                re = ore * pre + oim * pim
                im = oim * pre - ore * pim
                acc_re[g] = re if w == 0 else acc_re[g] + re
                acc_im[g] = im if w == 0 else acc_im[g] + im
        for g in range(group):
            rows = pl.ds(pl.multiple_of((first + g) * stations, stations), stations)
            dst[0, rows] = (acc_re[g] * weight).astype(dst.dtype)
            dst[1, rows] = (acc_im[g] * weight).astype(dst.dtype)
        return carry

    lax.fori_loop(0, stations // group, body, 0)


def peer_of(col, order, count):
    sibling = col + 1 - 2 * lax.rem(col, 2)
    if order == 0:
        return lax.rem(col + 2, count)
    if order == 1:
        return lax.rem(sibling + 2, count)
    if order == 2:
        return sibling
    return col


def lag_phase(scaling, cos_ref, sin_ref, y_ref, out_ref, staged, send_sems, recv_sems):
    count = out_ref.shape[0]
    chunk = out_ref.shape[1]
    quarter = y_ref.shape[3]
    rows = 256
    me = lax.axis_index("seg")
    row = lax.axis_index("sta")
    contract = (((1,), (1,)), ((), ()))

    def compute(target, dst):
        def body(index, carry):
            first = pl.multiple_of(target * chunk + index * rows, rows)
            acc = None
            for q in range(count):
                cols = pl.ds(q * quarter, quarter)
                for c, table in enumerate((cos_ref, sin_ref)):
                    part = lax.dot_general(
                        table[pl.ds(first, rows), cols], y_ref[q, c], contract,
                        preferred_element_type=jnp.float32,
                    )
                    acc = part if acc is None else acc + part
            local = pl.multiple_of(index * rows, rows)
            dst[pl.ds(local, rows), :] = (acc * scaling).astype(dst.dtype)
            return carry

        lax.fori_loop(0, chunk // rows, body, 0)

    copies = []
    for step in range(count - 1):
        target = peer_of(me, step, count)
        compute(target, staged.at[step])
        copy = pltpu.make_async_remote_copy(
            src_ref=staged.at[step],
            dst_ref=out_ref.at[me],
            send_sem=send_sems.at[step],
            recv_sem=recv_sems.at[step],
            device_id=(row, target),
            device_id_type=pl.DeviceIdType.MESH,
        )
        copy.start()
        copies.append(copy)
    compute(me, out_ref.at[me])
    for copy in copies:
        copy.wait()


def route_kernel(scaling, plan_ref, weight_ref, x_ref, cos_ref, sin_ref, lag_ref, out_ref, own,
                 own_f, spread, outgoing, partner, staged, lag_staged, zero_sems, first_sems,
                 second_sems, cross_sems, lag_sends, lag_recvs):
    count = spread.shape[0]
    low = spread.shape[1]
    rounds = plan_ref.shape[0]
    parts = own.shape[1] // x_ref.shape[1]
    windows_dev = x_ref.shape[1]
    quarter = own.shape[3]
    windows = own.shape[1]
    halves = own.shape[2] // low
    stations = own.shape[2]
    me = lax.axis_index("sta")
    col = lax.axis_index("seg")
    mesh_ids = pl.DeviceIdType.MESH
    barrier = pltpu.get_barrier_semaphore()

    def greet(step, carry):
        pl.semaphore_signal(
            barrier, inc=1, device_id=(lax.rem(me + step, count), col), device_id_type=mesh_ids
        )
        return carry

    lax.fori_loop(1, count, greet, 0)
    for step in range(1, parts):
        pl.semaphore_signal(
            barrier, inc=1, device_id=(me, lax.rem(col + step, parts)), device_id_type=mesh_ids
        )
    pl.semaphore_wait(barrier, count - 1 + parts - 1)

    def describe_zero(step):
        target = lax.rem(col + step, parts)
        return pltpu.make_async_remote_copy(
            src_ref=x_ref.at[:, :, :, pl.ds(pl.multiple_of(target * quarter, quarter), quarter)],
            dst_ref=own.at[:, pl.ds(col * windows_dev, windows_dev)],
            send_sem=zero_sems.at[step],
            recv_sem=zero_sems.at[parts + step],
            device_id=(me, target),
            device_id_type=mesh_ids,
        )

    for step in range(1, parts):
        describe_zero(step).start()
    local_zero = pltpu.make_async_copy(
        x_ref.at[:, :, :, pl.ds(pl.multiple_of(col * quarter, quarter), quarter)],
        own.at[:, pl.ds(col * windows_dev, windows_dev)],
        zero_sems.at[0],
    )
    local_zero.start()
    local_zero.wait()

    def chunk_of(j):
        c = j // (windows * halves)
        w = lax.rem(j // halves, windows)
        s_hi = lax.rem(j, halves)
        return own.at[c, w, pl.ds(s_hi * low, low)]

    def segment_of(j):
        return lax.rem(j // halves, windows) // windows_dev

    def describe_first(target, source):
        return pltpu.make_async_remote_copy(
            src_ref=chunk_of(target),
            dst_ref=spread.at[me],
            send_sem=first_sems.at[target],
            recv_sem=first_sems.at[count + source],
            device_id=(target, col),
            device_id_type=mesh_ids,
        )

    def send_local(step, carry):
        target = lax.rem(me + step, count)

        @pl.when(segment_of(target) == col)
        def _():
            describe_first(target, me).start()

        return carry

    def send_segment(segment):
        def body(step, carry):
            target = lax.rem(me + step, count)

            @pl.when(segment_of(target) == segment)
            def _():
                describe_first(target, me).start()

            return carry

        return body

    def finish_first(step, carry):
        target = lax.rem(me + step, count)
        source = lax.rem(me + count - step, count)
        describe_first(target, me).wait_send()
        describe_first(me, source).wait_recv()
        return carry

    lax.fori_loop(1, count, send_local, 0)
    for step in range(1, parts):
        describe_zero(step).wait_recv()
        lax.fori_loop(1, count, send_segment(lax.rem(col + parts - step, parts)), 0)
    for step in range(1, parts):
        describe_zero(step).wait_send()
    spread[me] = chunk_of(me)[...]
    lax.fori_loop(1, count, finish_first, 0)

    def pick(block, carry):
        for r in range(rounds):
            outgoing[block, r] = spread[plan_ref[r, block]]
        return carry

    lax.fori_loop(0, count, pick, 0)

    def round_of(order):
        return peer_of(col, order, rounds)

    def describe_second(order, step):
        target = lax.rem(me + step, count)
        r = round_of(order)
        return pltpu.make_async_remote_copy(
            src_ref=outgoing.at[target, r],
            dst_ref=partner.at[me, r],
            send_sem=second_sems.at[order * count + step],
            recv_sem=second_sems.at[(rounds + order) * count + step],
            device_id=(target, col),
            device_id_type=mesh_ids,
        )

    for order in range(rounds):
        def send_second(step, carry, order=order):
            describe_second(order, step).start()
            return carry

        lax.fori_loop(1, count, send_second, 0)
    for r in range(rounds):
        partner[me, r] = outgoing[me, r]
    own_f[...] = own[...].astype(jnp.float32)
    weight = weight_ref[...]

    def describe_cross(order):
        target = round_of(order)
        return pltpu.make_async_remote_copy(
            src_ref=staged.at[order],
            dst_ref=out_ref.at[col],
            send_sem=cross_sems.at[order],
            recv_sem=cross_sems.at[rounds + order],
            device_id=(me, target),
            device_id_type=mesh_ids,
        )

    for order in range(rounds):
        def arrived(step, carry, order=order):
            describe_second(order, step).wait_recv()
            return carry

        lax.fori_loop(1, count, arrived, 0)
        r = round_of(order)
        if order < rounds - 1:
            cross_round(weight, own_f, partner, r, staged.at[order])
            describe_cross(order).start()
        else:
            cross_round(weight, own_f, partner, r, out_ref.at[col])

    for order in range(rounds):
        def sent(step, carry, order=order):
            describe_second(order, step).wait_send()
            return carry

        lax.fori_loop(1, count, sent, 0)
    for order in range(rounds - 1):
        describe_cross(order).wait_recv()
    lag_phase(scaling, cos_ref, sin_ref, out_ref, lag_ref, lag_staged, lag_sends, lag_recvs)
    for order in range(rounds - 1):
        describe_cross(order).wait_send()


def route_and_cross(scaling, plan, weight, x, cos_table, sin_table, count, parts):
    channels, windows_dev, stations, bins = x.shape
    rounds = plan.shape[0]
    quarter = bins // parts
    windows = windows_dev * parts
    low = channels * windows * stations // count
    square = stations * stations
    chunk = LAGS // parts
    vmem = pl.BlockSpec(memory_space=pltpu.VMEM)
    return pl.pallas_call(
        functools.partial(route_kernel, scaling),
        in_specs=[pl.BlockSpec(memory_space=pltpu.SMEM), vmem, vmem, vmem, vmem],
        out_specs=vmem,
        out_shape=jax.ShapeDtypeStruct((rounds, chunk, square), x.dtype),
        scratch_shapes=[
            pltpu.VMEM((parts, channels, square, quarter), x.dtype),
            pltpu.VMEM((channels, windows, stations, quarter), x.dtype),
            pltpu.VMEM((channels, windows, stations, quarter), jnp.float32),
            pltpu.VMEM((count, low, quarter), x.dtype),
            pltpu.VMEM((count, rounds, low, quarter), x.dtype),
            pltpu.VMEM((count, rounds, low, quarter), x.dtype),
            pltpu.VMEM((rounds - 1, channels, square, quarter), x.dtype),
            pltpu.VMEM((rounds - 1, chunk, square), x.dtype),
            pltpu.SemaphoreType.DMA((2 * parts,)),
            pltpu.SemaphoreType.DMA((2 * count,)),
            pltpu.SemaphoreType.DMA((2 * rounds * count,)),
            pltpu.SemaphoreType.DMA((2 * rounds,)),
            pltpu.SemaphoreType.DMA((rounds,)),
            pltpu.SemaphoreType.DMA((rounds,)),
        ],
        compiler_params=pltpu.CompilerParams(collective_id=2, has_side_effects=True),
    )(plan, weight, x, cos_table, sin_table)


def per_device(records, plan):
    stations_dev, windows, length = records.shape
    sta_devices = lax.axis_size("sta")
    seg_devices = lax.axis_size("seg")
    transform = 2 * length
    row_count = stations_dev * windows
    cos_table, sin_table = fourier_tables(length, NBIN, transform)
    signal = jnp.transpose(records, (1, 0, 2)).reshape(row_count, length)
    mean_level = band_mean(jnp.abs(signal).astype(jnp.bfloat16), HALF)
    flattened = (signal / (mean_level + 1e-05)).astype(jnp.bfloat16)
    spec_real = jnp.dot(flattened, cos_table, preferred_element_type=jnp.float32)
    spec_imag = jnp.dot(flattened, sin_table, preferred_element_type=jnp.float32)
    magnitude = jnp.sqrt(spec_real * spec_real + spec_imag * spec_imag).astype(jnp.bfloat16)
    smooth = band_mean(magnitude, HALF)
    whitened = jnp.stack(
        [spec_real / (smooth + 1e-06), spec_imag / (smooth + 1e-06)], axis=0
    ).astype(jnp.bfloat16)
    whitened = whitened.reshape(2, windows, stations_dev, NBIN)
    quarter = NBIN // seg_devices
    all_windows = windows * seg_devices
    first_bin = lax.axis_index("seg") * quarter
    bin_index = first_bin + jnp.arange(quarter, dtype=jnp.int32)
    weight = jnp.where(bin_index == 0, 1.0, 2.0).astype(jnp.float32).reshape(1, quarter)
    scaling = 1.0 / math.sqrt(4.0 * NBIN * all_windows)
    lagged = route_and_cross(
        scaling, plan, weight, whitened, cos_table, sin_table, sta_devices, seg_devices
    )
    return jnp.transpose(lagged, (1, 0, 2)).astype(jnp.float32)


def solution(mesh):
    in_specs = (P("sta", "seg", None), P())
    out_specs = P("seg", None, "sta")
    return jax.shard_map(
        per_device, mesh=mesh, in_specs=in_specs, out_specs=out_specs, check_vma=False
    )
```

```python
import functools
import math

import jax
import jax.numpy as jnp
from jax import lax
from jax.experimental import pallas as pl
from jax.experimental.pallas import tpu as pltpu
from jax.sharding import PartitionSpec as P

WLEN = 2048
NBIN = 1024
HALF = 64
ROUNDS = 4
LAGS = 2048


def band_mean(values, half_width):
    row_count, length = values.shape
    block_width = 2 * half_width
    blocks_count = length // block_width
    inside = jnp.arange(block_width, dtype=jnp.int32)
    source = inside[:, None]
    target = inside[None, :]
    inner_band = (jnp.abs(source - target) <= half_width).astype(jnp.bfloat16)
    before = (target + block_width - source <= half_width).astype(jnp.bfloat16)
    after_band = (source + block_width - target <= half_width).astype(jnp.bfloat16)
    blocks = values.reshape(row_count, blocks_count, block_width)
    earlier = jnp.pad(blocks[:, :-1], ((0, 0), (1, 0), (0, 0)))
    following = jnp.pad(blocks[:, 1:], ((0, 0), (0, 1), (0, 0)))
    flat_shape = (row_count * blocks_count, block_width)
    running = jnp.dot(blocks.reshape(flat_shape), inner_band, preferred_element_type=jnp.float32)
    running = running + jnp.dot(
        earlier.reshape(flat_shape), before, preferred_element_type=jnp.float32
    )
    running = running + jnp.dot(
        following.reshape(flat_shape), after_band, preferred_element_type=jnp.float32
    )
    position = jnp.arange(length, dtype=jnp.int32)
    counted = (
        jnp.minimum(position, half_width) + jnp.minimum(length - 1 - position, half_width) + 1
    ).astype(jnp.float32)
    return running.reshape(row_count, length) / counted


def angles_of(rows, step, bins, transform):
    phase_int = (rows[:, None] * step) * bins[None, :] % transform
    return phase_int.astype(jnp.float32) * (2.0 * math.pi / transform)


def fourier_tables(length, bin_count, transform):
    low_count = 64
    high_count = length // low_count
    bins = jnp.arange(bin_count, dtype=jnp.int32)
    high = angles_of(jnp.arange(high_count, dtype=jnp.int32), low_count, bins, transform)
    low = angles_of(jnp.arange(low_count, dtype=jnp.int32), 1, bins, transform)
    hc, hs = jnp.cos(high)[:, None], jnp.sin(high)[:, None]
    lc, ls = jnp.cos(low)[None], jnp.sin(low)[None]
    cos_part = (hc * lc - hs * ls).astype(jnp.bfloat16).reshape(length, bin_count)
    sin_part = (-(hs * lc + hc * ls)).astype(jnp.bfloat16).reshape(length, bin_count)
    return cos_part, sin_part


def cross_round(weight, own_ref, other_ref, r, dst):
    windows = own_ref.shape[1]
    stations = own_ref.shape[2]
    low = other_ref.shape[2]
    halves = stations // low
    group = 4

    def rows_of(c, w):
        first = (c * windows + w) * halves
        return jnp.concatenate(
            [other_ref[first + h, r].astype(jnp.float32) for h in range(halves)], axis=0
        )

    def body(index, carry):
        first = index * group
        acc_re = [None] * group
        acc_im = [None] * group
        for w in range(windows):
            pre = rows_of(0, w)
            pim = rows_of(1, w)
            for g in range(group):
                ore = own_ref[0, w, pl.ds(first + g, 1), :]
                oim = own_ref[1, w, pl.ds(first + g, 1), :]
                re = ore * pre + oim * pim
                im = oim * pre - ore * pim
                acc_re[g] = re if w == 0 else acc_re[g] + re
                acc_im[g] = im if w == 0 else acc_im[g] + im
        for g in range(group):
            rows = pl.ds(pl.multiple_of((first + g) * stations, stations), stations)
            dst[0, rows] = (acc_re[g] * weight).astype(dst.dtype)
            dst[1, rows] = (acc_im[g] * weight).astype(dst.dtype)
        return carry

    lax.fori_loop(0, stations // group, body, 0)


def lag_phase(scaling, cos_ref, sin_ref, y_ref, out_ref, staged, send_sems, recv_sems,
              final_ref=None):
    count = out_ref.shape[0]
    chunk = out_ref.shape[1]
    quarter = y_ref.shape[3]
    rows = 256
    me = lax.axis_index("seg")
    row = lax.axis_index("sta")
    contract = (((1,), (1,)), ((), ()))

    def compute(target, dst):
        def body(index, carry):
            first = pl.multiple_of(target * chunk + index * rows, rows)
            acc = None
            for q in range(count):
                cols = pl.ds(q * quarter, quarter)
                for c, table in enumerate((cos_ref, sin_ref)):
                    part = lax.dot_general(
                        table[pl.ds(first, rows), cols], y_ref[q, c], contract,
                        preferred_element_type=jnp.float32,
                    )
                    acc = part if acc is None else acc + part
            local = pl.multiple_of(index * rows, rows)
            dst[pl.ds(local, rows), :] = (acc * scaling).astype(dst.dtype)
            return carry

        lax.fori_loop(0, chunk // rows, body, 0)

    copies = []
    for step in range(count - 1):
        target = lax.rem(me + 1 + step, count)
        compute(target, staged.at[step])
        copy = pltpu.make_async_remote_copy(
            src_ref=staged.at[step],
            dst_ref=out_ref.at[me],
            send_sem=send_sems.at[step],
            recv_sem=recv_sems.at[step],
            device_id=(row, target),
            device_id_type=pl.DeviceIdType.MESH,
        )
        copy.start()
        copies.append(copy)
    compute(me, out_ref.at[me])
    for copy in copies:
        copy.wait()
    if final_ref is not None:
        square = final_ref.shape[1] // count
        for r in range(count):
            final_ref[:, r * square:(r + 1) * square] = out_ref[r].astype(final_ref.dtype)


def route_kernel(scaling, plan_ref, weight_ref, x_ref, cos_ref, sin_ref, final_ref, lag_ref, out_ref, own,
                 own_f, spread, outgoing, partner, staged, lag_staged, zero_sems, first_sems,
                 second_sems, cross_sems, lag_sends, lag_recvs):
    count = spread.shape[0]
    low = spread.shape[1]
    rounds = plan_ref.shape[0]
    parts = own.shape[1] // x_ref.shape[1]
    windows_dev = x_ref.shape[1]
    quarter = own.shape[3]
    windows = own.shape[1]
    halves = own.shape[2] // low
    stations = own.shape[2]
    me = lax.axis_index("sta")
    col = lax.axis_index("seg")
    mesh_ids = pl.DeviceIdType.MESH
    barrier = pltpu.get_barrier_semaphore()

    def greet(step, carry):
        pl.semaphore_signal(
            barrier, inc=1, device_id=(lax.rem(me + step, count), col), device_id_type=mesh_ids
        )
        return carry

    lax.fori_loop(1, count, greet, 0)
    for step in range(1, parts):
        pl.semaphore_signal(
            barrier, inc=1, device_id=(me, lax.rem(col + step, parts)), device_id_type=mesh_ids
        )
    pl.semaphore_wait(barrier, count - 1 + parts - 1)

    def describe_zero(step):
        target = lax.rem(col + step, parts)
        return pltpu.make_async_remote_copy(
            src_ref=x_ref.at[:, :, :, pl.ds(pl.multiple_of(target * quarter, quarter), quarter)],
            dst_ref=own.at[:, pl.ds(col * windows_dev, windows_dev)],
            send_sem=zero_sems.at[step],
            recv_sem=zero_sems.at[parts + step],
            device_id=(me, target),
            device_id_type=mesh_ids,
        )

    for step in range(1, parts):
        describe_zero(step).start()
    local_zero = pltpu.make_async_copy(
        x_ref.at[:, :, :, pl.ds(pl.multiple_of(col * quarter, quarter), quarter)],
        own.at[:, pl.ds(col * windows_dev, windows_dev)],
        zero_sems.at[0],
    )
    local_zero.start()
    local_zero.wait()

    def chunk_of(j):
        c = j // (windows * halves)
        w = lax.rem(j // halves, windows)
        s_hi = lax.rem(j, halves)
        return own.at[c, w, pl.ds(s_hi * low, low)]

    def segment_of(j):
        return lax.rem(j // halves, windows) // windows_dev

    def describe_first(target, source):
        return pltpu.make_async_remote_copy(
            src_ref=chunk_of(target),
            dst_ref=spread.at[me],
            send_sem=first_sems.at[target],
            recv_sem=first_sems.at[count + source],
            device_id=(target, col),
            device_id_type=mesh_ids,
        )

    def send_local(step, carry):
        target = lax.rem(me + step, count)

        @pl.when(segment_of(target) == col)
        def _():
            describe_first(target, me).start()

        return carry

    def send_segment(segment):
        def body(step, carry):
            target = lax.rem(me + step, count)

            @pl.when(segment_of(target) == segment)
            def _():
                describe_first(target, me).start()

            return carry

        return body

    def finish_first(step, carry):
        target = lax.rem(me + step, count)
        source = lax.rem(me + count - step, count)
        describe_first(target, me).wait_send()
        describe_first(me, source).wait_recv()
        return carry

    lax.fori_loop(1, count, send_local, 0)
    for step in range(1, parts):
        describe_zero(step).wait_recv()
        lax.fori_loop(1, count, send_segment(lax.rem(col + parts - step, parts)), 0)
    for step in range(1, parts):
        describe_zero(step).wait_send()
    spread[me] = chunk_of(me)[...]
    lax.fori_loop(1, count, finish_first, 0)

    def pick(block, carry):
        for r in range(rounds):
            outgoing[block, r] = spread[plan_ref[r, block]]
        return carry

    lax.fori_loop(0, count, pick, 0)

    def round_of(order):
        return lax.rem(col + 1 + order, rounds)

    def describe_second(order, step):
        target = lax.rem(me + step, count)
        r = round_of(order)
        return pltpu.make_async_remote_copy(
            src_ref=outgoing.at[target, r],
            dst_ref=partner.at[me, r],
            send_sem=second_sems.at[order * count + step],
            recv_sem=second_sems.at[(rounds + order) * count + step],
            device_id=(target, col),
            device_id_type=mesh_ids,
        )

    for order in range(rounds):
        def send_second(step, carry, order=order):
            describe_second(order, step).start()
            return carry

        lax.fori_loop(1, count, send_second, 0)
    for r in range(rounds):
        partner[me, r] = outgoing[me, r]
    own_f[...] = own[...].astype(jnp.float32)
    weight = weight_ref[...]

    def describe_cross(order):
        target = round_of(order)
        return pltpu.make_async_remote_copy(
            src_ref=staged.at[order],
            dst_ref=out_ref.at[col],
            send_sem=cross_sems.at[order],
            recv_sem=cross_sems.at[rounds + order],
            device_id=(me, target),
            device_id_type=mesh_ids,
        )

    for order in range(rounds):
        def arrived(step, carry, order=order):
            describe_second(order, step).wait_recv()
            return carry

        lax.fori_loop(1, count, arrived, 0)
        r = round_of(order)
        if order < rounds - 1:
            cross_round(weight, own_f, partner, r, staged.at[order])
            describe_cross(order).start()
        else:
            cross_round(weight, own_f, partner, r, out_ref.at[col])

    for order in range(rounds):
        def sent(step, carry, order=order):
            describe_second(order, step).wait_send()
            return carry

        lax.fori_loop(1, count, sent, 0)
    for order in range(rounds - 1):
        describe_cross(order).wait_recv()
    lag_phase(
        scaling, cos_ref, sin_ref, out_ref, lag_ref, lag_staged, lag_sends, lag_recvs, final_ref
    )
    for order in range(rounds - 1):
        describe_cross(order).wait_send()


def route_and_cross(scaling, plan, weight, x, cos_table, sin_table, count, parts):
    channels, windows_dev, stations, bins = x.shape
    rounds = plan.shape[0]
    quarter = bins // parts
    windows = windows_dev * parts
    low = channels * windows * stations // count
    square = stations * stations
    chunk = LAGS // parts
    vmem = pl.BlockSpec(memory_space=pltpu.VMEM)
    return pl.pallas_call(
        functools.partial(route_kernel, scaling),
        in_specs=[pl.BlockSpec(memory_space=pltpu.SMEM), vmem, vmem, vmem, vmem],
        out_specs=vmem,
        out_shape=jax.ShapeDtypeStruct((chunk, rounds * square), jnp.float32),
        scratch_shapes=[
            pltpu.VMEM((rounds, chunk, square), x.dtype),
            pltpu.VMEM((parts, channels, square, quarter), x.dtype),
            pltpu.VMEM((channels, windows, stations, quarter), x.dtype),
            pltpu.VMEM((channels, windows, stations, quarter), jnp.float32),
            pltpu.VMEM((count, low, quarter), x.dtype),
            pltpu.VMEM((count, rounds, low, quarter), x.dtype),
            pltpu.VMEM((count, rounds, low, quarter), x.dtype),
            pltpu.VMEM((rounds - 1, channels, square, quarter), x.dtype),
            pltpu.VMEM((rounds - 1, chunk, square), x.dtype),
            pltpu.SemaphoreType.DMA((2 * parts,)),
            pltpu.SemaphoreType.DMA((2 * count,)),
            pltpu.SemaphoreType.DMA((2 * rounds * count,)),
            pltpu.SemaphoreType.DMA((2 * rounds,)),
            pltpu.SemaphoreType.DMA((rounds,)),
            pltpu.SemaphoreType.DMA((rounds,)),
        ],
        compiler_params=pltpu.CompilerParams(collective_id=2, has_side_effects=True),
    )(plan, weight, x, cos_table, sin_table)


def per_device(records, plan):
    stations_dev, windows, length = records.shape
    sta_devices = lax.axis_size("sta")
    seg_devices = lax.axis_size("seg")
    transform = 2 * length
    row_count = stations_dev * windows
    cos_table, sin_table = fourier_tables(length, NBIN, transform)
    signal = jnp.transpose(records, (1, 0, 2)).reshape(row_count, length)
    mean_level = band_mean(jnp.abs(signal).astype(jnp.bfloat16), HALF)
    flattened = (signal / (mean_level + 1e-05)).astype(jnp.bfloat16)
    spec_real = jnp.dot(flattened, cos_table, preferred_element_type=jnp.float32)
    spec_imag = jnp.dot(flattened, sin_table, preferred_element_type=jnp.float32)
    magnitude = jnp.sqrt(spec_real * spec_real + spec_imag * spec_imag).astype(jnp.bfloat16)
    smooth = band_mean(magnitude, HALF)
    whitened = jnp.stack(
        [spec_real / (smooth + 1e-06), spec_imag / (smooth + 1e-06)], axis=0
    ).astype(jnp.bfloat16)
    whitened = whitened.reshape(2, windows, stations_dev, NBIN)
    quarter = NBIN // seg_devices
    all_windows = windows * seg_devices
    first_bin = lax.axis_index("seg") * quarter
    bin_index = first_bin + jnp.arange(quarter, dtype=jnp.int32)
    weight = jnp.where(bin_index == 0, 1.0, 2.0).astype(jnp.float32).reshape(1, quarter)
    scaling = 1.0 / math.sqrt(4.0 * NBIN * all_windows)
    lagged = route_and_cross(
        scaling, plan, weight, whitened, cos_table, sin_table, sta_devices, seg_devices
    )
    return lagged.reshape(lagged.shape[0], ROUNDS, lagged.shape[1] // ROUNDS)


def solution(mesh):
    in_specs = (P("sta", "seg", None), P())
    out_specs = P("seg", None, "sta")
    return jax.shard_map(
        per_device, mesh=mesh, in_specs=in_specs, out_specs=out_specs, check_vma=False
    )
```

```python
import functools
import math

import jax
import jax.numpy as jnp
from jax import lax
from jax.experimental import pallas as pl
from jax.experimental.pallas import tpu as pltpu
from jax.sharding import PartitionSpec as P

WLEN = 2048
NBIN = 1024
HALF = 64
ROUNDS = 4
LAGS = 2048


def band_mean(values, half_width):
    row_count, length = values.shape
    block_width = 2 * half_width
    blocks_count = length // block_width
    inside = jnp.arange(block_width, dtype=jnp.int32)
    source = inside[:, None]
    target = inside[None, :]
    inner_band = (jnp.abs(source - target) <= half_width).astype(jnp.bfloat16)
    before = (target + block_width - source <= half_width).astype(jnp.bfloat16)
    after_band = (source + block_width - target <= half_width).astype(jnp.bfloat16)
    blocks = values.reshape(row_count, blocks_count, block_width)
    earlier = jnp.pad(blocks[:, :-1], ((0, 0), (1, 0), (0, 0)))
    following = jnp.pad(blocks[:, 1:], ((0, 0), (0, 1), (0, 0)))
    flat_shape = (row_count * blocks_count, block_width)
    running = jnp.dot(blocks.reshape(flat_shape), inner_band, preferred_element_type=jnp.float32)
    running = running + jnp.dot(
        earlier.reshape(flat_shape), before, preferred_element_type=jnp.float32
    )
    running = running + jnp.dot(
        following.reshape(flat_shape), after_band, preferred_element_type=jnp.float32
    )
    position = jnp.arange(length, dtype=jnp.int32)
    counted = (
        jnp.minimum(position, half_width) + jnp.minimum(length - 1 - position, half_width) + 1
    ).astype(jnp.float32)
    return running.reshape(row_count, length) / counted


def angles_of(rows, step, bins, transform):
    phase_int = (rows[:, None] * step) * bins[None, :] % transform
    return phase_int.astype(jnp.float32) * (2.0 * math.pi / transform)


def fourier_tables(length, bin_count, transform):
    low_count = 64
    high_count = length // low_count
    bins = jnp.arange(bin_count, dtype=jnp.int32)
    high = angles_of(jnp.arange(high_count, dtype=jnp.int32), low_count, bins, transform)
    low = angles_of(jnp.arange(low_count, dtype=jnp.int32), 1, bins, transform)
    hc, hs = jnp.cos(high)[:, None], jnp.sin(high)[:, None]
    lc, ls = jnp.cos(low)[None], jnp.sin(low)[None]
    cos_part = (hc * lc - hs * ls).astype(jnp.bfloat16).reshape(length, bin_count)
    sin_part = (-(hs * lc + hc * ls)).astype(jnp.bfloat16).reshape(length, bin_count)
    return cos_part, sin_part


def cross_round(weight, own_ref, other_ref, r, dst):
    windows = own_ref.shape[1]
    stations = own_ref.shape[2]
    low = other_ref.shape[2]
    halves = stations // low
    group = 4

    def rows_of(c, w):
        first = (c * windows + w) * halves
        return jnp.concatenate(
            [other_ref[first + h, r].astype(jnp.float32) for h in range(halves)], axis=0
        )

    def body(index, carry):
        first = index * group
        acc_re = [None] * group
        acc_im = [None] * group
        for w in range(windows):
            pre = rows_of(0, w)
            pim = rows_of(1, w)
            for g in range(group):
                ore = own_ref[0, w, pl.ds(first + g, 1), :]
                oim = own_ref[1, w, pl.ds(first + g, 1), :]
                re = ore * pre + oim * pim
                im = oim * pre - ore * pim
                acc_re[g] = re if w == 0 else acc_re[g] + re
                acc_im[g] = im if w == 0 else acc_im[g] + im
        for g in range(group):
            rows = pl.ds(pl.multiple_of((first + g) * stations, stations), stations)
            dst[0, rows] = (acc_re[g] * weight).astype(dst.dtype)
            dst[1, rows] = (acc_im[g] * weight).astype(dst.dtype)
        return carry

    lax.fori_loop(0, stations // group, body, 0)


def lag_phase(scaling, cos_ref, sin_ref, y_ref, out_ref, staged, send_sems, recv_sems,
              final_ref=None):
    count = out_ref.shape[0]
    chunk = out_ref.shape[1]
    quarter = y_ref.shape[3]
    rows = 256
    me = lax.axis_index("seg")
    row = lax.axis_index("sta")
    contract = (((1,), (1,)), ((), ()))

    def compute(target, dst):
        def body(index, carry):
            first = pl.multiple_of(target * chunk + index * rows, rows)
            acc = None
            for q in range(count):
                cols = pl.ds(q * quarter, quarter)
                for c, table in enumerate((cos_ref, sin_ref)):
                    part = lax.dot_general(
                        table[pl.ds(first, rows), cols], y_ref[q, c], contract,
                        preferred_element_type=jnp.float32,
                    )
                    acc = part if acc is None else acc + part
            local = pl.multiple_of(index * rows, rows)
            dst[pl.ds(local, rows), :] = (acc * scaling).astype(dst.dtype)
            return carry

        lax.fori_loop(0, chunk // rows, body, 0)

    copies = []
    for step in range(count - 1):
        target = lax.rem(me + 1 + step, count)
        compute(target, staged.at[step])
        copy = pltpu.make_async_remote_copy(
            src_ref=staged.at[step],
            dst_ref=out_ref.at[me],
            send_sem=send_sems.at[step],
            recv_sem=recv_sems.at[step],
            device_id=(row, target),
            device_id_type=pl.DeviceIdType.MESH,
        )
        copy.start()
        copies.append(copy)
    compute(me, out_ref.at[me])
    for copy in copies:
        copy.wait()
    if final_ref is not None:
        square = final_ref.shape[1] // count
        for r in range(count):
            final_ref[:, r * square:(r + 1) * square] = out_ref[r].astype(final_ref.dtype)


def route_kernel(scaling, plan_ref, weight_ref, x_ref, cos_hbm, sin_hbm, final_ref, lag_ref, out_ref,
                 own, own_f, spread, outgoing, partner, staged, lag_staged, cos_ref, sin_ref,
                 table_sems, zero_sems, first_sems, second_sems, cross_sems, lag_sends, lag_recvs):
    count = spread.shape[0]
    low = spread.shape[1]
    rounds = plan_ref.shape[0]
    parts = own.shape[1] // x_ref.shape[1]
    windows_dev = x_ref.shape[1]
    quarter = own.shape[3]
    windows = own.shape[1]
    halves = own.shape[2] // low
    stations = own.shape[2]
    me = lax.axis_index("sta")
    col = lax.axis_index("seg")
    mesh_ids = pl.DeviceIdType.MESH
    tables = [
        pltpu.make_async_copy(cos_hbm, cos_ref, table_sems.at[0]),
        pltpu.make_async_copy(sin_hbm, sin_ref, table_sems.at[1]),
    ]
    for table in tables:
        table.start()
    barrier = pltpu.get_barrier_semaphore()

    def greet(step, carry):
        pl.semaphore_signal(
            barrier, inc=1, device_id=(lax.rem(me + step, count), col), device_id_type=mesh_ids
        )
        return carry

    lax.fori_loop(1, count, greet, 0)
    for step in range(1, parts):
        pl.semaphore_signal(
            barrier, inc=1, device_id=(me, lax.rem(col + step, parts)), device_id_type=mesh_ids
        )
    pl.semaphore_wait(barrier, count - 1 + parts - 1)

    def describe_zero(step):
        target = lax.rem(col + step, parts)
        return pltpu.make_async_remote_copy(
            src_ref=x_ref.at[:, :, :, pl.ds(pl.multiple_of(target * quarter, quarter), quarter)],
            dst_ref=own.at[:, pl.ds(col * windows_dev, windows_dev)],
            send_sem=zero_sems.at[step],
            recv_sem=zero_sems.at[parts + step],
            device_id=(me, target),
            device_id_type=mesh_ids,
        )

    for step in range(1, parts):
        describe_zero(step).start()
    local_zero = pltpu.make_async_copy(
        x_ref.at[:, :, :, pl.ds(pl.multiple_of(col * quarter, quarter), quarter)],
        own.at[:, pl.ds(col * windows_dev, windows_dev)],
        zero_sems.at[0],
    )
    local_zero.start()
    local_zero.wait()

    def chunk_of(j):
        c = j // (windows * halves)
        w = lax.rem(j // halves, windows)
        s_hi = lax.rem(j, halves)
        return own.at[c, w, pl.ds(s_hi * low, low)]

    def segment_of(j):
        return lax.rem(j // halves, windows) // windows_dev

    def describe_first(target, source):
        return pltpu.make_async_remote_copy(
            src_ref=chunk_of(target),
            dst_ref=spread.at[me],
            send_sem=first_sems.at[target],
            recv_sem=first_sems.at[count + source],
            device_id=(target, col),
            device_id_type=mesh_ids,
        )

    def send_local(step, carry):
        target = lax.rem(me + step, count)

        @pl.when(segment_of(target) == col)
        def _():
            describe_first(target, me).start()

        return carry

    def send_segment(segment):
        def body(step, carry):
            target = lax.rem(me + step, count)

            @pl.when(segment_of(target) == segment)
            def _():
                describe_first(target, me).start()

            return carry

        return body

    def finish_first(step, carry):
        target = lax.rem(me + step, count)
        source = lax.rem(me + count - step, count)
        describe_first(target, me).wait_send()
        describe_first(me, source).wait_recv()
        return carry

    lax.fori_loop(1, count, send_local, 0)
    for step in range(1, parts):
        describe_zero(step).wait_recv()
        lax.fori_loop(1, count, send_segment(lax.rem(col + parts - step, parts)), 0)
    for step in range(1, parts):
        describe_zero(step).wait_send()
    spread[me] = chunk_of(me)[...]
    lax.fori_loop(1, count, finish_first, 0)

    def pick(block, carry):
        for r in range(rounds):
            outgoing[block, r] = spread[plan_ref[r, block]]
        return carry

    lax.fori_loop(0, count, pick, 0)

    def round_of(order):
        return lax.rem(col + 1 + order, rounds)

    def describe_second(order, step):
        target = lax.rem(me + step, count)
        r = round_of(order)
        return pltpu.make_async_remote_copy(
            src_ref=outgoing.at[target, r],
            dst_ref=partner.at[me, r],
            send_sem=second_sems.at[order * count + step],
            recv_sem=second_sems.at[(rounds + order) * count + step],
            device_id=(target, col),
            device_id_type=mesh_ids,
        )

    for order in range(rounds):
        def send_second(step, carry, order=order):
            describe_second(order, step).start()
            return carry

        lax.fori_loop(1, count, send_second, 0)
    for r in range(rounds):
        partner[me, r] = outgoing[me, r]
    own_f[...] = own[...].astype(jnp.float32)
    weight = weight_ref[...]

    def describe_cross(order):
        target = round_of(order)
        return pltpu.make_async_remote_copy(
            src_ref=staged.at[order],
            dst_ref=out_ref.at[col],
            send_sem=cross_sems.at[order],
            recv_sem=cross_sems.at[rounds + order],
            device_id=(me, target),
            device_id_type=mesh_ids,
        )

    for order in range(rounds):
        def arrived(step, carry, order=order):
            describe_second(order, step).wait_recv()
            return carry

        lax.fori_loop(1, count, arrived, 0)
        r = round_of(order)
        if order < rounds - 1:
            cross_round(weight, own_f, partner, r, staged.at[order])
            describe_cross(order).start()
        else:
            cross_round(weight, own_f, partner, r, out_ref.at[col])

    for order in range(rounds):
        def sent(step, carry, order=order):
            describe_second(order, step).wait_send()
            return carry

        lax.fori_loop(1, count, sent, 0)
    for order in range(rounds - 1):
        describe_cross(order).wait_recv()
    for table in tables:
        table.wait()
    lag_phase(
        scaling, cos_ref, sin_ref, out_ref, lag_ref, lag_staged, lag_sends, lag_recvs, final_ref
    )
    for order in range(rounds - 1):
        describe_cross(order).wait_send()


def route_and_cross(scaling, plan, weight, x, cos_table, sin_table, count, parts):
    channels, windows_dev, stations, bins = x.shape
    rounds = plan.shape[0]
    quarter = bins // parts
    windows = windows_dev * parts
    low = channels * windows * stations // count
    square = stations * stations
    chunk = LAGS // parts
    vmem = pl.BlockSpec(memory_space=pltpu.VMEM)
    hbm = pl.BlockSpec(memory_space=pl.ANY)
    return pl.pallas_call(
        functools.partial(route_kernel, scaling),
        in_specs=[pl.BlockSpec(memory_space=pltpu.SMEM), vmem, vmem, hbm, hbm],
        out_specs=vmem,
        out_shape=jax.ShapeDtypeStruct((chunk, rounds * square), jnp.float32),
        scratch_shapes=[
            pltpu.VMEM((rounds, chunk, square), x.dtype),
            pltpu.VMEM((parts, channels, square, quarter), x.dtype),
            pltpu.VMEM((channels, windows, stations, quarter), x.dtype),
            pltpu.VMEM((channels, windows, stations, quarter), jnp.float32),
            pltpu.VMEM((count, low, quarter), x.dtype),
            pltpu.VMEM((count, rounds, low, quarter), x.dtype),
            pltpu.VMEM((count, rounds, low, quarter), x.dtype),
            pltpu.VMEM((rounds - 1, channels, square, quarter), x.dtype),
            pltpu.VMEM((rounds - 1, chunk, square), x.dtype),
            pltpu.VMEM(cos_table.shape, cos_table.dtype),
            pltpu.VMEM(sin_table.shape, sin_table.dtype),
            pltpu.SemaphoreType.DMA((2,)),
            pltpu.SemaphoreType.DMA((2 * parts,)),
            pltpu.SemaphoreType.DMA((2 * count,)),
            pltpu.SemaphoreType.DMA((2 * rounds * count,)),
            pltpu.SemaphoreType.DMA((2 * rounds,)),
            pltpu.SemaphoreType.DMA((rounds,)),
            pltpu.SemaphoreType.DMA((rounds,)),
        ],
        compiler_params=pltpu.CompilerParams(collective_id=2, has_side_effects=True),
    )(plan, weight, x, cos_table, sin_table)


def per_device(records, plan):
    stations_dev, windows, length = records.shape
    sta_devices = lax.axis_size("sta")
    seg_devices = lax.axis_size("seg")
    transform = 2 * length
    row_count = stations_dev * windows
    cos_table, sin_table = fourier_tables(length, NBIN, transform)
    signal = jnp.transpose(records, (1, 0, 2)).reshape(row_count, length)
    mean_level = band_mean(jnp.abs(signal).astype(jnp.bfloat16), HALF)
    flattened = (signal / (mean_level + 1e-05)).astype(jnp.bfloat16)
    spec_real = jnp.dot(flattened, cos_table, preferred_element_type=jnp.float32)
    spec_imag = jnp.dot(flattened, sin_table, preferred_element_type=jnp.float32)
    magnitude = jnp.sqrt(spec_real * spec_real + spec_imag * spec_imag).astype(jnp.bfloat16)
    smooth = band_mean(magnitude, HALF)
    whitened = jnp.stack(
        [spec_real / (smooth + 1e-06), spec_imag / (smooth + 1e-06)], axis=0
    ).astype(jnp.bfloat16)
    whitened = whitened.reshape(2, windows, stations_dev, NBIN)
    quarter = NBIN // seg_devices
    all_windows = windows * seg_devices
    first_bin = lax.axis_index("seg") * quarter
    bin_index = first_bin + jnp.arange(quarter, dtype=jnp.int32)
    weight = jnp.where(bin_index == 0, 1.0, 2.0).astype(jnp.float32).reshape(1, quarter)
    scaling = 1.0 / math.sqrt(4.0 * NBIN * all_windows)
    lagged = route_and_cross(
        scaling, plan, weight, whitened, cos_table, sin_table, sta_devices, seg_devices
    )
    return lagged.reshape(lagged.shape[0], ROUNDS, lagged.shape[1] // ROUNDS)


def solution(mesh):
    in_specs = (P("sta", "seg", None), P())
    out_specs = P("seg", None, "sta")
    return jax.shard_map(
        per_device, mesh=mesh, in_specs=in_specs, out_specs=out_specs, check_vma=False
    )
```

```python
import functools
import math

import jax
import jax.numpy as jnp
from jax import lax
from jax.experimental import pallas as pl
from jax.experimental.pallas import tpu as pltpu
from jax.sharding import PartitionSpec as P

WLEN = 2048
NBIN = 1024
HALF = 64
ROUNDS = 4
LAGS = 2048


def band_mean(values, half_width):
    row_count, length = values.shape
    block_width = 2 * half_width
    blocks_count = length // block_width
    inside = jnp.arange(block_width, dtype=jnp.int32)
    source = inside[:, None]
    target = inside[None, :]
    inner_band = (jnp.abs(source - target) <= half_width).astype(jnp.bfloat16)
    before = (target + block_width - source <= half_width).astype(jnp.bfloat16)
    after_band = (source + block_width - target <= half_width).astype(jnp.bfloat16)
    blocks = values.reshape(row_count, blocks_count, block_width)
    earlier = jnp.pad(blocks[:, :-1], ((0, 0), (1, 0), (0, 0)))
    following = jnp.pad(blocks[:, 1:], ((0, 0), (0, 1), (0, 0)))
    flat_shape = (row_count * blocks_count, block_width)
    running = jnp.dot(blocks.reshape(flat_shape), inner_band, preferred_element_type=jnp.float32)
    running = running + jnp.dot(
        earlier.reshape(flat_shape), before, preferred_element_type=jnp.float32
    )
    running = running + jnp.dot(
        following.reshape(flat_shape), after_band, preferred_element_type=jnp.float32
    )
    position = jnp.arange(length, dtype=jnp.int32)
    counted = (
        jnp.minimum(position, half_width) + jnp.minimum(length - 1 - position, half_width) + 1
    ).astype(jnp.float32)
    return running.reshape(row_count, length) / counted


def angles_of(rows, step, bins, transform):
    phase_int = (rows[:, None] * step) * bins[None, :] % transform
    return phase_int.astype(jnp.float32) * (2.0 * math.pi / transform)


def fourier_tables(length, bin_count, transform):
    low_count = 64
    high_count = length // low_count
    bins = jnp.arange(bin_count, dtype=jnp.int32)
    high = angles_of(jnp.arange(high_count, dtype=jnp.int32), low_count, bins, transform)
    low = angles_of(jnp.arange(low_count, dtype=jnp.int32), 1, bins, transform)
    hc, hs = jnp.cos(high)[:, None], jnp.sin(high)[:, None]
    lc, ls = jnp.cos(low)[None], jnp.sin(low)[None]
    cos_part = (hc * lc - hs * ls).astype(jnp.bfloat16).reshape(length, bin_count)
    sin_part = (-(hs * lc + hc * ls)).astype(jnp.bfloat16).reshape(length, bin_count)
    return cos_part, sin_part


def cross_round(weight, own_ref, other_ref, r, dst):
    windows = own_ref.shape[1]
    stations = own_ref.shape[2]
    low = other_ref.shape[2]
    halves = stations // low
    group = 4

    def rows_of(c, w):
        first = (c * windows + w) * halves
        return jnp.concatenate(
            [other_ref[first + h, r].astype(jnp.float32) for h in range(halves)], axis=0
        )

    def body(index, carry):
        first = index * group
        acc_re = [None] * group
        acc_im = [None] * group
        for w in range(windows):
            pre = rows_of(0, w)
            pim = rows_of(1, w)
            for g in range(group):
                ore = own_ref[0, w, pl.ds(first + g, 1), :]
                oim = own_ref[1, w, pl.ds(first + g, 1), :]
                re = ore * pre + oim * pim
                im = oim * pre - ore * pim
                acc_re[g] = re if w == 0 else acc_re[g] + re
                acc_im[g] = im if w == 0 else acc_im[g] + im
        for g in range(group):
            rows = pl.ds(pl.multiple_of((first + g) * stations, stations), stations)
            dst[0, rows] = (acc_re[g] * weight).astype(dst.dtype)
            dst[1, rows] = (acc_im[g] * weight).astype(dst.dtype)
        return carry

    lax.fori_loop(0, stations // group, body, 0)


def lag_phase(scaling, cos_ref, sin_ref, y_ref, out_ref, staged, send_sems, recv_sems,
              final_ref=None):
    count = out_ref.shape[0]
    chunk = out_ref.shape[1]
    quarter = y_ref.shape[3]
    rows = 256
    me = lax.axis_index("seg")
    row = lax.axis_index("sta")
    contract = (((1,), (1,)), ((), ()))

    def compute(target, dst):
        def body(index, carry):
            first = pl.multiple_of(target * chunk + index * rows, rows)
            acc = None
            for q in range(count):
                cols = pl.ds(q * quarter, quarter)
                for c, table in enumerate((cos_ref, sin_ref)):
                    part = lax.dot_general(
                        table[pl.ds(first, rows), cols], y_ref[q, c], contract,
                        preferred_element_type=jnp.float32,
                    )
                    acc = part if acc is None else acc + part
            local = pl.multiple_of(index * rows, rows)
            dst[pl.ds(local, rows), :] = (acc * scaling).astype(dst.dtype)
            return carry

        lax.fori_loop(0, chunk // rows, body, 0)

    copies = []
    for step in range(count - 1):
        target = lax.rem(me + 1 + step, count)
        compute(target, staged.at[step])
        copy = pltpu.make_async_remote_copy(
            src_ref=staged.at[step],
            dst_ref=out_ref.at[me],
            send_sem=send_sems.at[step],
            recv_sem=recv_sems.at[step],
            device_id=(row, target),
            device_id_type=pl.DeviceIdType.MESH,
        )
        copy.start()
        copies.append(copy)
    compute(me, out_ref.at[me])
    for copy in copies:
        copy.wait()
    if final_ref is not None:
        square = final_ref.shape[1] // count
        for r in range(count):
            final_ref[:, r * square:(r + 1) * square] = out_ref[r].astype(final_ref.dtype)


def route_kernel(scaling, plan_ref, weight_ref, x_ref, cos_hbm, sin_hbm, final_ref, lag_ref, out_ref,
                 own, own_f, spread, outgoing, partner, staged, lag_staged, cos_ref, sin_ref,
                 table_sems, zero_sems, first_sems, second_sems, cross_sems, lag_sends, lag_recvs):
    count = spread.shape[0]
    low = spread.shape[1]
    rounds = plan_ref.shape[0]
    parts = own.shape[1] // x_ref.shape[1]
    windows_dev = x_ref.shape[1]
    quarter = own.shape[3]
    windows = own.shape[1]
    halves = own.shape[2] // low
    stations = own.shape[2]
    me = lax.axis_index("sta")
    col = lax.axis_index("seg")
    mesh_ids = pl.DeviceIdType.MESH
    tables = [
        pltpu.make_async_copy(cos_hbm, cos_ref, table_sems.at[0]),
        pltpu.make_async_copy(sin_hbm, sin_ref, table_sems.at[1]),
    ]
    for table in tables:
        table.start()
    barrier = pltpu.get_barrier_semaphore()

    def greet(step, carry):
        pl.semaphore_signal(
            barrier, inc=1, device_id=(lax.rem(me + step, count), col), device_id_type=mesh_ids
        )
        return carry

    lax.fori_loop(1, count, greet, 0)
    for step in range(1, parts):
        pl.semaphore_signal(
            barrier, inc=1, device_id=(me, lax.rem(col + step, parts)), device_id_type=mesh_ids
        )
    pl.semaphore_wait(barrier, count - 1 + parts - 1)

    def describe_zero(step):
        target = lax.rem(col + step, parts)
        return pltpu.make_async_remote_copy(
            src_ref=x_ref.at[:, :, :, pl.ds(pl.multiple_of(target * quarter, quarter), quarter)],
            dst_ref=own.at[:, pl.ds(col * windows_dev, windows_dev)],
            send_sem=zero_sems.at[step],
            recv_sem=zero_sems.at[parts + step],
            device_id=(me, target),
            device_id_type=mesh_ids,
        )

    for step in range(1, parts):
        describe_zero(step).start()
    local_zero = pltpu.make_async_copy(
        x_ref.at[:, :, :, pl.ds(pl.multiple_of(col * quarter, quarter), quarter)],
        own.at[:, pl.ds(col * windows_dev, windows_dev)],
        zero_sems.at[0],
    )
    local_zero.start()
    local_zero.wait()

    def chunk_of(j):
        c = j // (windows * halves)
        w = lax.rem(j // halves, windows)
        s_hi = lax.rem(j, halves)
        return own.at[c, w, pl.ds(s_hi * low, low)]

    def segment_of(j):
        return lax.rem(j // halves, windows) // windows_dev

    def describe_first(target, source):
        return pltpu.make_async_remote_copy(
            src_ref=chunk_of(target),
            dst_ref=spread.at[me],
            send_sem=first_sems.at[target],
            recv_sem=first_sems.at[count + source],
            device_id=(target, col),
            device_id_type=mesh_ids,
        )

    def send_local(step, carry):
        target = lax.rem(me + step, count)

        @pl.when(segment_of(target) == col)
        def _():
            describe_first(target, me).start()

        return carry

    def send_segment(segment):
        def body(step, carry):
            target = lax.rem(me + step, count)

            @pl.when(segment_of(target) == segment)
            def _():
                describe_first(target, me).start()

            return carry

        return body

    def finish_first(step, carry):
        target = lax.rem(me + step, count)
        source = lax.rem(me + count - step, count)
        describe_first(target, me).wait_send()
        describe_first(me, source).wait_recv()
        return carry

    lax.fori_loop(1, count, send_local, 0)
    for step in range(1, parts):
        describe_zero(step).wait_recv()
        lax.fori_loop(1, count, send_segment(lax.rem(col + parts - step, parts)), 0)
    for step in range(1, parts):
        describe_zero(step).wait_send()
    spread[me] = chunk_of(me)[...]
    lax.fori_loop(1, count, finish_first, 0)

    def pick(block, carry):
        for r in range(rounds):
            outgoing[block, r] = spread[plan_ref[r, block]]
        return carry

    lax.fori_loop(0, count, pick, 0)

    def round_of(order):
        return lax.rem(col + 1 + order, rounds)

    def describe_second(order, step):
        target = lax.rem(me + step, count)
        r = round_of(order)
        return pltpu.make_async_remote_copy(
            src_ref=outgoing.at[target, r],
            dst_ref=partner.at[me, r],
            send_sem=second_sems.at[order * count + step],
            recv_sem=second_sems.at[(rounds + order) * count + step],
            device_id=(target, col),
            device_id_type=mesh_ids,
        )

    for order in range(rounds):
        def send_second(step, carry, order=order):
            describe_second(order, step).start()
            return carry

        lax.fori_loop(1, count, send_second, 0)
    for r in range(rounds):
        partner[me, r] = outgoing[me, r]
    own_f[...] = own[...].astype(jnp.float32)
    weight = weight_ref[...]

    def describe_cross(order):
        target = round_of(order)
        return pltpu.make_async_remote_copy(
            src_ref=staged.at[order],
            dst_ref=out_ref.at[col],
            send_sem=cross_sems.at[order],
            recv_sem=cross_sems.at[rounds + order],
            device_id=(me, target),
            device_id_type=mesh_ids,
        )

    for order in range(rounds):
        def arrived(step, carry, order=order):
            describe_second(order, step).wait_recv()
            return carry

        lax.fori_loop(1, count, arrived, 0)
        r = round_of(order)
        if order < rounds - 1:
            cross_round(weight, own_f, partner, r, staged.at[order])
            describe_cross(order).start()
        else:
            cross_round(weight, own_f, partner, r, out_ref.at[col])

    for order in range(rounds - 1):
        describe_cross(order).wait_recv()
    for table in tables:
        table.wait()
    lag_phase(
        scaling, cos_ref, sin_ref, out_ref, lag_ref, lag_staged, lag_sends, lag_recvs, final_ref
    )
    for order in range(rounds - 1):
        describe_cross(order).wait_send()
    for order in range(rounds):
        def sent(step, carry, order=order):
            describe_second(order, step).wait_send()
            return carry

        lax.fori_loop(1, count, sent, 0)


def route_and_cross(scaling, plan, weight, x, cos_table, sin_table, count, parts):
    channels, windows_dev, stations, bins = x.shape
    rounds = plan.shape[0]
    quarter = bins // parts
    windows = windows_dev * parts
    low = channels * windows * stations // count
    square = stations * stations
    chunk = LAGS // parts
    vmem = pl.BlockSpec(memory_space=pltpu.VMEM)
    hbm = pl.BlockSpec(memory_space=pl.ANY)
    return pl.pallas_call(
        functools.partial(route_kernel, scaling),
        in_specs=[pl.BlockSpec(memory_space=pltpu.SMEM), vmem, vmem, hbm, hbm],
        out_specs=vmem,
        out_shape=jax.ShapeDtypeStruct((chunk, rounds * square), jnp.float32),
        scratch_shapes=[
            pltpu.VMEM((rounds, chunk, square), x.dtype),
            pltpu.VMEM((parts, channels, square, quarter), x.dtype),
            pltpu.VMEM((channels, windows, stations, quarter), x.dtype),
            pltpu.VMEM((channels, windows, stations, quarter), jnp.float32),
            pltpu.VMEM((count, low, quarter), x.dtype),
            pltpu.VMEM((count, rounds, low, quarter), x.dtype),
            pltpu.VMEM((count, rounds, low, quarter), x.dtype),
            pltpu.VMEM((rounds - 1, channels, square, quarter), x.dtype),
            pltpu.VMEM((rounds - 1, chunk, square), x.dtype),
            pltpu.VMEM(cos_table.shape, cos_table.dtype),
            pltpu.VMEM(sin_table.shape, sin_table.dtype),
            pltpu.SemaphoreType.DMA((2,)),
            pltpu.SemaphoreType.DMA((2 * parts,)),
            pltpu.SemaphoreType.DMA((2 * count,)),
            pltpu.SemaphoreType.DMA((2 * rounds * count,)),
            pltpu.SemaphoreType.DMA((2 * rounds,)),
            pltpu.SemaphoreType.DMA((rounds,)),
            pltpu.SemaphoreType.DMA((rounds,)),
        ],
        compiler_params=pltpu.CompilerParams(collective_id=2, has_side_effects=True),
    )(plan, weight, x, cos_table, sin_table)


def per_device(records, plan):
    stations_dev, windows, length = records.shape
    sta_devices = lax.axis_size("sta")
    seg_devices = lax.axis_size("seg")
    transform = 2 * length
    row_count = stations_dev * windows
    cos_table, sin_table = fourier_tables(length, NBIN, transform)
    signal = jnp.transpose(records, (1, 0, 2)).reshape(row_count, length)
    mean_level = band_mean(jnp.abs(signal).astype(jnp.bfloat16), HALF)
    flattened = (signal / (mean_level + 1e-05)).astype(jnp.bfloat16)
    spec_real = jnp.dot(flattened, cos_table, preferred_element_type=jnp.float32)
    spec_imag = jnp.dot(flattened, sin_table, preferred_element_type=jnp.float32)
    magnitude = jnp.sqrt(spec_real * spec_real + spec_imag * spec_imag).astype(jnp.bfloat16)
    smooth = band_mean(magnitude, HALF)
    whitened = jnp.stack(
        [spec_real / (smooth + 1e-06), spec_imag / (smooth + 1e-06)], axis=0
    ).astype(jnp.bfloat16)
    whitened = whitened.reshape(2, windows, stations_dev, NBIN)
    quarter = NBIN // seg_devices
    all_windows = windows * seg_devices
    first_bin = lax.axis_index("seg") * quarter
    bin_index = first_bin + jnp.arange(quarter, dtype=jnp.int32)
    weight = jnp.where(bin_index == 0, 1.0, 2.0).astype(jnp.float32).reshape(1, quarter)
    scaling = 1.0 / math.sqrt(4.0 * NBIN * all_windows)
    lagged = route_and_cross(
        scaling, plan, weight, whitened, cos_table, sin_table, sta_devices, seg_devices
    )
    return lagged.reshape(lagged.shape[0], ROUNDS, lagged.shape[1] // ROUNDS)


def solution(mesh):
    in_specs = (P("sta", "seg", None), P())
    out_specs = P("seg", None, "sta")
    return jax.shard_map(
        per_device, mesh=mesh, in_specs=in_specs, out_specs=out_specs, check_vma=False
    )
```

```python
import functools
import math

import jax
import jax.numpy as jnp
from jax import lax
from jax.experimental import pallas as pl
from jax.experimental.pallas import tpu as pltpu
from jax.sharding import PartitionSpec as P

WLEN = 2048
NBIN = 1024
HALF = 64
ROUNDS = 4
LAGS = 2048


def band_mean(values, half_width):
    row_count, length = values.shape
    block_width = 2 * half_width
    blocks_count = length // block_width
    inside = jnp.arange(block_width, dtype=jnp.int32)
    source = inside[:, None]
    target = inside[None, :]
    inner_band = (jnp.abs(source - target) <= half_width).astype(jnp.bfloat16)
    before = (target + block_width - source <= half_width).astype(jnp.bfloat16)
    after_band = (source + block_width - target <= half_width).astype(jnp.bfloat16)
    blocks = values.reshape(row_count, blocks_count, block_width)
    earlier = jnp.pad(blocks[:, :-1], ((0, 0), (1, 0), (0, 0)))
    following = jnp.pad(blocks[:, 1:], ((0, 0), (0, 1), (0, 0)))
    flat_shape = (row_count * blocks_count, block_width)
    running = jnp.dot(blocks.reshape(flat_shape), inner_band, preferred_element_type=jnp.float32)
    running = running + jnp.dot(
        earlier.reshape(flat_shape), before, preferred_element_type=jnp.float32
    )
    running = running + jnp.dot(
        following.reshape(flat_shape), after_band, preferred_element_type=jnp.float32
    )
    position = jnp.arange(length, dtype=jnp.int32)
    counted = (
        jnp.minimum(position, half_width) + jnp.minimum(length - 1 - position, half_width) + 1
    ).astype(jnp.float32)
    return running.reshape(row_count, length) / counted


def angles_of(rows, step, bins, transform):
    phase_int = (rows[:, None] * step) * bins[None, :] % transform
    return phase_int.astype(jnp.float32) * (2.0 * math.pi / transform)


def fourier_tables(length, bin_count, transform):
    low_count = 64
    high_count = length // low_count
    bins = jnp.arange(bin_count, dtype=jnp.int32)
    high = angles_of(jnp.arange(high_count, dtype=jnp.int32), low_count, bins, transform)
    low = angles_of(jnp.arange(low_count, dtype=jnp.int32), 1, bins, transform)
    hc, hs = jnp.cos(high)[:, None], jnp.sin(high)[:, None]
    lc, ls = jnp.cos(low)[None], jnp.sin(low)[None]
    cos_part = (hc * lc - hs * ls).astype(jnp.bfloat16).reshape(length, bin_count)
    sin_part = (-(hs * lc + hc * ls)).astype(jnp.bfloat16).reshape(length, bin_count)
    return cos_part, sin_part


def cross_round(weight, own_ref, other_ref, r, dst):
    windows = own_ref.shape[1]
    stations = own_ref.shape[2]
    low = other_ref.shape[2]
    halves = stations // low
    group = 4

    def rows_of(c, w):
        first = (c * windows + w) * halves
        return jnp.concatenate(
            [other_ref[first + h, r].astype(jnp.float32) for h in range(halves)], axis=0
        )

    def body(index, carry):
        first = index * group
        acc_re = [None] * group
        acc_im = [None] * group
        for w in range(windows):
            pre = rows_of(0, w)
            pim = rows_of(1, w)
            for g in range(group):
                ore = own_ref[0, w, pl.ds(first + g, 1), :]
                oim = own_ref[1, w, pl.ds(first + g, 1), :]
                re = ore * pre + oim * pim
                im = oim * pre - ore * pim
                acc_re[g] = re if w == 0 else acc_re[g] + re
                acc_im[g] = im if w == 0 else acc_im[g] + im
        for g in range(group):
            rows = pl.ds(pl.multiple_of((first + g) * stations, stations), stations)
            dst[0, rows] = (acc_re[g] * weight).astype(dst.dtype)
            dst[1, rows] = (acc_im[g] * weight).astype(dst.dtype)
        return carry

    lax.fori_loop(0, stations // group, body, 0)


def lag_phase(scaling, cos_ref, sin_ref, y_ref, out_ref, staged, send_sems, recv_sems,
              final_ref=None):
    count = out_ref.shape[0]
    chunk = out_ref.shape[1]
    quarter = y_ref.shape[3]
    rows = 512
    me = lax.axis_index("seg")
    row = lax.axis_index("sta")
    contract = (((1,), (1,)), ((), ()))

    def compute(target, dst):
        def body(index, carry):
            first = pl.multiple_of(target * chunk + index * rows, rows)
            acc = None
            for q in range(count):
                cols = pl.ds(q * quarter, quarter)
                for c, table in enumerate((cos_ref, sin_ref)):
                    part = lax.dot_general(
                        table[pl.ds(first, rows), cols], y_ref[q, c], contract,
                        preferred_element_type=jnp.float32,
                    )
                    acc = part if acc is None else acc + part
            local = pl.multiple_of(index * rows, rows)
            dst[pl.ds(local, rows), :] = (acc * scaling).astype(dst.dtype)
            return carry

        lax.fori_loop(0, chunk // rows, body, 0)

    copies = []
    for step in range(count - 1):
        target = lax.rem(me + 1 + step, count)
        compute(target, staged.at[step])
        copy = pltpu.make_async_remote_copy(
            src_ref=staged.at[step],
            dst_ref=out_ref.at[me],
            send_sem=send_sems.at[step],
            recv_sem=recv_sems.at[step],
            device_id=(row, target),
            device_id_type=pl.DeviceIdType.MESH,
        )
        copy.start()
        copies.append(copy)
    compute(me, out_ref.at[me])
    for copy in copies:
        copy.wait()
    if final_ref is not None:
        square = final_ref.shape[1] // count
        for r in range(count):
            final_ref[:, r * square:(r + 1) * square] = out_ref[r].astype(final_ref.dtype)


def route_kernel(scaling, plan_ref, weight_ref, x_ref, cos_hbm, sin_hbm, final_ref, lag_ref, out_ref,
                 own, own_f, spread, outgoing, partner, staged, lag_staged, cos_ref, sin_ref,
                 table_sems, zero_sems, first_sems, second_sems, cross_sems, lag_sends, lag_recvs):
    count = spread.shape[0]
    low = spread.shape[1]
    rounds = plan_ref.shape[0]
    parts = own.shape[1] // x_ref.shape[1]
    windows_dev = x_ref.shape[1]
    quarter = own.shape[3]
    windows = own.shape[1]
    halves = own.shape[2] // low
    stations = own.shape[2]
    me = lax.axis_index("sta")
    col = lax.axis_index("seg")
    mesh_ids = pl.DeviceIdType.MESH
    tables = [
        pltpu.make_async_copy(cos_hbm, cos_ref, table_sems.at[0]),
        pltpu.make_async_copy(sin_hbm, sin_ref, table_sems.at[1]),
    ]
    for table in tables:
        table.start()
    barrier = pltpu.get_barrier_semaphore()

    def greet(step, carry):
        pl.semaphore_signal(
            barrier, inc=1, device_id=(lax.rem(me + step, count), col), device_id_type=mesh_ids
        )
        return carry

    lax.fori_loop(1, count, greet, 0)
    for step in range(1, parts):
        pl.semaphore_signal(
            barrier, inc=1, device_id=(me, lax.rem(col + step, parts)), device_id_type=mesh_ids
        )
    pl.semaphore_wait(barrier, count - 1 + parts - 1)

    def describe_zero(step):
        target = lax.rem(col + step, parts)
        return pltpu.make_async_remote_copy(
            src_ref=x_ref.at[:, :, :, pl.ds(pl.multiple_of(target * quarter, quarter), quarter)],
            dst_ref=own.at[:, pl.ds(col * windows_dev, windows_dev)],
            send_sem=zero_sems.at[step],
            recv_sem=zero_sems.at[parts + step],
            device_id=(me, target),
            device_id_type=mesh_ids,
        )

    for step in range(1, parts):
        describe_zero(step).start()
    local_zero = pltpu.make_async_copy(
        x_ref.at[:, :, :, pl.ds(pl.multiple_of(col * quarter, quarter), quarter)],
        own.at[:, pl.ds(col * windows_dev, windows_dev)],
        zero_sems.at[0],
    )
    local_zero.start()
    local_zero.wait()

    def chunk_of(j):
        c = j // (windows * halves)
        w = lax.rem(j // halves, windows)
        s_hi = lax.rem(j, halves)
        return own.at[c, w, pl.ds(s_hi * low, low)]

    def segment_of(j):
        return lax.rem(j // halves, windows) // windows_dev

    def describe_first(target, source):
        return pltpu.make_async_remote_copy(
            src_ref=chunk_of(target),
            dst_ref=spread.at[me],
            send_sem=first_sems.at[target],
            recv_sem=first_sems.at[count + source],
            device_id=(target, col),
            device_id_type=mesh_ids,
        )

    def send_local(step, carry):
        target = lax.rem(me + step, count)

        @pl.when(segment_of(target) == col)
        def _():
            describe_first(target, me).start()

        return carry

    def send_segment(segment):
        def body(step, carry):
            target = lax.rem(me + step, count)

            @pl.when(segment_of(target) == segment)
            def _():
                describe_first(target, me).start()

            return carry

        return body

    def finish_first(step, carry):
        target = lax.rem(me + step, count)
        source = lax.rem(me + count - step, count)
        describe_first(target, me).wait_send()
        describe_first(me, source).wait_recv()
        return carry

    lax.fori_loop(1, count, send_local, 0)
    for step in range(1, parts):
        describe_zero(step).wait_recv()
        lax.fori_loop(1, count, send_segment(lax.rem(col + parts - step, parts)), 0)
    for step in range(1, parts):
        describe_zero(step).wait_send()
    spread[me] = chunk_of(me)[...]
    lax.fori_loop(1, count, finish_first, 0)

    def pick(block, carry):
        for r in range(rounds):
            outgoing[block, r] = spread[plan_ref[r, block]]
        return carry

    lax.fori_loop(0, count, pick, 0)

    def round_of(order):
        return lax.rem(col + 1 + order, rounds)

    def describe_second(order, step):
        target = lax.rem(me + step, count)
        r = round_of(order)
        return pltpu.make_async_remote_copy(
            src_ref=outgoing.at[target, r],
            dst_ref=partner.at[me, r],
            send_sem=second_sems.at[order * count + step],
            recv_sem=second_sems.at[(rounds + order) * count + step],
            device_id=(target, col),
            device_id_type=mesh_ids,
        )

    for order in range(rounds):
        def send_second(step, carry, order=order):
            describe_second(order, step).start()
            return carry

        lax.fori_loop(1, count, send_second, 0)
    for r in range(rounds):
        partner[me, r] = outgoing[me, r]
    own_f[...] = own[...].astype(jnp.float32)
    weight = weight_ref[...]

    def describe_cross(order):
        target = round_of(order)
        return pltpu.make_async_remote_copy(
            src_ref=staged.at[order],
            dst_ref=out_ref.at[col],
            send_sem=cross_sems.at[order],
            recv_sem=cross_sems.at[rounds + order],
            device_id=(me, target),
            device_id_type=mesh_ids,
        )

    for order in range(rounds):
        def arrived(step, carry, order=order):
            describe_second(order, step).wait_recv()
            return carry

        lax.fori_loop(1, count, arrived, 0)
        r = round_of(order)
        if order < rounds - 1:
            cross_round(weight, own_f, partner, r, staged.at[order])
            describe_cross(order).start()
        else:
            cross_round(weight, own_f, partner, r, out_ref.at[col])

    for order in range(rounds):
        def sent(step, carry, order=order):
            describe_second(order, step).wait_send()
            return carry

        lax.fori_loop(1, count, sent, 0)
    for order in range(rounds - 1):
        describe_cross(order).wait_recv()
    for table in tables:
        table.wait()
    lag_phase(
        scaling, cos_ref, sin_ref, out_ref, lag_ref, lag_staged, lag_sends, lag_recvs, final_ref
    )
    for order in range(rounds - 1):
        describe_cross(order).wait_send()


def route_and_cross(scaling, plan, weight, x, cos_table, sin_table, count, parts):
    channels, windows_dev, stations, bins = x.shape
    rounds = plan.shape[0]
    quarter = bins // parts
    windows = windows_dev * parts
    low = channels * windows * stations // count
    square = stations * stations
    chunk = LAGS // parts
    vmem = pl.BlockSpec(memory_space=pltpu.VMEM)
    hbm = pl.BlockSpec(memory_space=pl.ANY)
    return pl.pallas_call(
        functools.partial(route_kernel, scaling),
        in_specs=[pl.BlockSpec(memory_space=pltpu.SMEM), vmem, vmem, hbm, hbm],
        out_specs=vmem,
        out_shape=jax.ShapeDtypeStruct((chunk, rounds * square), jnp.float32),
        scratch_shapes=[
            pltpu.VMEM((rounds, chunk, square), x.dtype),
            pltpu.VMEM((parts, channels, square, quarter), x.dtype),
            pltpu.VMEM((channels, windows, stations, quarter), x.dtype),
            pltpu.VMEM((channels, windows, stations, quarter), jnp.float32),
            pltpu.VMEM((count, low, quarter), x.dtype),
            pltpu.VMEM((count, rounds, low, quarter), x.dtype),
            pltpu.VMEM((count, rounds, low, quarter), x.dtype),
            pltpu.VMEM((rounds - 1, channels, square, quarter), x.dtype),
            pltpu.VMEM((rounds - 1, chunk, square), x.dtype),
            pltpu.VMEM(cos_table.shape, cos_table.dtype),
            pltpu.VMEM(sin_table.shape, sin_table.dtype),
            pltpu.SemaphoreType.DMA((2,)),
            pltpu.SemaphoreType.DMA((2 * parts,)),
            pltpu.SemaphoreType.DMA((2 * count,)),
            pltpu.SemaphoreType.DMA((2 * rounds * count,)),
            pltpu.SemaphoreType.DMA((2 * rounds,)),
            pltpu.SemaphoreType.DMA((rounds,)),
            pltpu.SemaphoreType.DMA((rounds,)),
        ],
        compiler_params=pltpu.CompilerParams(collective_id=2, has_side_effects=True),
    )(plan, weight, x, cos_table, sin_table)


def per_device(records, plan):
    stations_dev, windows, length = records.shape
    sta_devices = lax.axis_size("sta")
    seg_devices = lax.axis_size("seg")
    transform = 2 * length
    row_count = stations_dev * windows
    cos_table, sin_table = fourier_tables(length, NBIN, transform)
    signal = jnp.transpose(records, (1, 0, 2)).reshape(row_count, length)
    mean_level = band_mean(jnp.abs(signal).astype(jnp.bfloat16), HALF)
    flattened = (signal / (mean_level + 1e-05)).astype(jnp.bfloat16)
    spec_real = jnp.dot(flattened, cos_table, preferred_element_type=jnp.float32)
    spec_imag = jnp.dot(flattened, sin_table, preferred_element_type=jnp.float32)
    magnitude = jnp.sqrt(spec_real * spec_real + spec_imag * spec_imag).astype(jnp.bfloat16)
    smooth = band_mean(magnitude, HALF)
    whitened = jnp.stack(
        [spec_real / (smooth + 1e-06), spec_imag / (smooth + 1e-06)], axis=0
    ).astype(jnp.bfloat16)
    whitened = whitened.reshape(2, windows, stations_dev, NBIN)
    quarter = NBIN // seg_devices
    all_windows = windows * seg_devices
    first_bin = lax.axis_index("seg") * quarter
    bin_index = first_bin + jnp.arange(quarter, dtype=jnp.int32)
    weight = jnp.where(bin_index == 0, 1.0, 2.0).astype(jnp.float32).reshape(1, quarter)
    scaling = 1.0 / math.sqrt(4.0 * NBIN * all_windows)
    lagged = route_and_cross(
        scaling, plan, weight, whitened, cos_table, sin_table, sta_devices, seg_devices
    )
    return lagged.reshape(lagged.shape[0], ROUNDS, lagged.shape[1] // ROUNDS)


def solution(mesh):
    in_specs = (P("sta", "seg", None), P())
    out_specs = P("seg", None, "sta")
    return jax.shard_map(
        per_device, mesh=mesh, in_specs=in_specs, out_specs=out_specs, check_vma=False
    )
```

```python
import functools
import math

import jax
import jax.numpy as jnp
from jax import lax
from jax.experimental import pallas as pl
from jax.experimental.pallas import tpu as pltpu
from jax.sharding import PartitionSpec as P

WLEN = 2048
NBIN = 1024
HALF = 64
ROUNDS = 4
LAGS = 2048


def band_mean(values, half_width):
    row_count, length = values.shape
    block_width = 2 * half_width
    blocks_count = length // block_width
    inside = jnp.arange(block_width, dtype=jnp.int32)
    source = inside[:, None]
    target = inside[None, :]
    inner_band = (jnp.abs(source - target) <= half_width).astype(jnp.bfloat16)
    before = (target + block_width - source <= half_width).astype(jnp.bfloat16)
    after_band = (source + block_width - target <= half_width).astype(jnp.bfloat16)
    blocks = values.reshape(row_count, blocks_count, block_width)
    earlier = jnp.pad(blocks[:, :-1], ((0, 0), (1, 0), (0, 0)))
    following = jnp.pad(blocks[:, 1:], ((0, 0), (0, 1), (0, 0)))
    flat_shape = (row_count * blocks_count, block_width)
    running = jnp.dot(blocks.reshape(flat_shape), inner_band, preferred_element_type=jnp.float32)
    running = running + jnp.dot(
        earlier.reshape(flat_shape), before, preferred_element_type=jnp.float32
    )
    running = running + jnp.dot(
        following.reshape(flat_shape), after_band, preferred_element_type=jnp.float32
    )
    position = jnp.arange(length, dtype=jnp.int32)
    counted = (
        jnp.minimum(position, half_width) + jnp.minimum(length - 1 - position, half_width) + 1
    ).astype(jnp.float32)
    return running.reshape(row_count, length) / counted


def angles_of(rows, step, bins, transform):
    phase_int = (rows[:, None] * step) * bins[None, :] % transform
    return phase_int.astype(jnp.float32) * (2.0 * math.pi / transform)


def fourier_tables(length, bin_count, transform):
    low_count = 64
    high_count = length // low_count
    bins = jnp.arange(bin_count, dtype=jnp.int32)
    high = angles_of(jnp.arange(high_count, dtype=jnp.int32), low_count, bins, transform)
    low = angles_of(jnp.arange(low_count, dtype=jnp.int32), 1, bins, transform)
    hc, hs = jnp.cos(high)[:, None], jnp.sin(high)[:, None]
    lc, ls = jnp.cos(low)[None], jnp.sin(low)[None]
    cos_part = (hc * lc - hs * ls).astype(jnp.bfloat16).reshape(length, bin_count)
    sin_part = (-(hs * lc + hc * ls)).astype(jnp.bfloat16).reshape(length, bin_count)
    return cos_part, sin_part


def cross_round(weight, own_ref, other_ref, r, dst):
    windows = own_ref.shape[1]
    stations = own_ref.shape[2]
    low = other_ref.shape[2]
    halves = stations // low
    group = 4

    def rows_of(c, w):
        first = (c * windows + w) * halves
        return jnp.concatenate(
            [other_ref[first + h, r].astype(jnp.float32) for h in range(halves)], axis=0
        )

    def body(index, carry):
        first = index * group
        acc_re = [None] * group
        acc_im = [None] * group
        for w in range(windows):
            pre = rows_of(0, w)
            pim = rows_of(1, w)
            for g in range(group):
                ore = own_ref[0, w, pl.ds(first + g, 1), :]
                oim = own_ref[1, w, pl.ds(first + g, 1), :]
                re = ore * pre + oim * pim
                im = oim * pre - ore * pim
                acc_re[g] = re if w == 0 else acc_re[g] + re
                acc_im[g] = im if w == 0 else acc_im[g] + im
        for g in range(group):
            rows = pl.ds(pl.multiple_of((first + g) * stations, stations), stations)
            dst[0, rows] = (acc_re[g] * weight).astype(dst.dtype)
            dst[1, rows] = (acc_im[g] * weight).astype(dst.dtype)
        return carry

    lax.fori_loop(0, stations // group, body, 0)


def lag_phase(scaling, cos_ref, sin_ref, y_ref, out_ref, staged, send_sems, recv_sems,
              final_ref=None):
    count = out_ref.shape[0]
    chunk = out_ref.shape[1]
    quarter = y_ref.shape[3]
    rows = 256
    me = lax.axis_index("seg")
    row = lax.axis_index("sta")
    contract = (((1,), (1,)), ((), ()))

    def compute(target, dst):
        def body(index, carry):
            first = pl.multiple_of(target * chunk + index * rows, rows)
            acc = None
            for q in range(count):
                cols = pl.ds(q * quarter, quarter)
                for c, table in enumerate((cos_ref, sin_ref)):
                    part = lax.dot_general(
                        table[pl.ds(first, rows), cols], y_ref[q, c], contract,
                        preferred_element_type=jnp.float32,
                    )
                    acc = part if acc is None else acc + part
            local = pl.multiple_of(index * rows, rows)
            dst[pl.ds(local, rows), :] = (acc * scaling).astype(dst.dtype)
            return carry

        lax.fori_loop(0, chunk // rows, body, 0)

    copies = []
    for step in range(count - 1):
        target = lax.rem(me + 1 + step, count)
        compute(target, staged.at[step])
        copy = pltpu.make_async_remote_copy(
            src_ref=staged.at[step],
            dst_ref=out_ref.at[me],
            send_sem=send_sems.at[step],
            recv_sem=recv_sems.at[step],
            device_id=(row, target),
            device_id_type=pl.DeviceIdType.MESH,
        )
        copy.start()
        copies.append(copy)
    compute(me, out_ref.at[me])
    for copy in copies:
        copy.wait()
    if final_ref is not None:
        square = final_ref.shape[1] // count
        for r in range(count):
            final_ref[:, r * square:(r + 1) * square] = out_ref[r].astype(final_ref.dtype)


def route_kernel(scaling, plan_ref, x_ref, cos_hbm, sin_hbm, final_ref, lag_ref, out_ref,
                 own, own_f, spread, outgoing, partner, staged, lag_staged, cos_ref, sin_ref,
                 table_sems, zero_sems, first_sems, second_sems, cross_sems, lag_sends, lag_recvs):
    count = spread.shape[0]
    low = spread.shape[1]
    rounds = plan_ref.shape[0]
    parts = own.shape[1] // x_ref.shape[1]
    windows_dev = x_ref.shape[1]
    quarter = own.shape[3]
    windows = own.shape[1]
    halves = own.shape[2] // low
    stations = own.shape[2]
    me = lax.axis_index("sta")
    col = lax.axis_index("seg")
    mesh_ids = pl.DeviceIdType.MESH
    tables = [
        pltpu.make_async_copy(cos_hbm, cos_ref, table_sems.at[0]),
        pltpu.make_async_copy(sin_hbm, sin_ref, table_sems.at[1]),
    ]
    for table in tables:
        table.start()
    barrier = pltpu.get_barrier_semaphore()

    def greet(step, carry):
        pl.semaphore_signal(
            barrier, inc=1, device_id=(lax.rem(me + step, count), col), device_id_type=mesh_ids
        )
        return carry

    lax.fori_loop(1, count, greet, 0)
    for step in range(1, parts):
        pl.semaphore_signal(
            barrier, inc=1, device_id=(me, lax.rem(col + step, parts)), device_id_type=mesh_ids
        )
    pl.semaphore_wait(barrier, count - 1 + parts - 1)

    def describe_zero(step):
        target = lax.rem(col + step, parts)
        return pltpu.make_async_remote_copy(
            src_ref=x_ref.at[:, :, :, pl.ds(pl.multiple_of(target * quarter, quarter), quarter)],
            dst_ref=own.at[:, pl.ds(col * windows_dev, windows_dev)],
            send_sem=zero_sems.at[step],
            recv_sem=zero_sems.at[parts + step],
            device_id=(me, target),
            device_id_type=mesh_ids,
        )

    for step in range(1, parts):
        describe_zero(step).start()
    local_zero = pltpu.make_async_copy(
        x_ref.at[:, :, :, pl.ds(pl.multiple_of(col * quarter, quarter), quarter)],
        own.at[:, pl.ds(col * windows_dev, windows_dev)],
        zero_sems.at[0],
    )
    local_zero.start()
    local_zero.wait()

    def chunk_of(j):
        c = j // (windows * halves)
        w = lax.rem(j // halves, windows)
        s_hi = lax.rem(j, halves)
        return own.at[c, w, pl.ds(s_hi * low, low)]

    def segment_of(j):
        return lax.rem(j // halves, windows) // windows_dev

    def describe_first(target, source):
        return pltpu.make_async_remote_copy(
            src_ref=chunk_of(target),
            dst_ref=spread.at[me],
            send_sem=first_sems.at[target],
            recv_sem=first_sems.at[count + source],
            device_id=(target, col),
            device_id_type=mesh_ids,
        )

    def send_local(step, carry):
        target = lax.rem(me + step, count)

        @pl.when(segment_of(target) == col)
        def _():
            describe_first(target, me).start()

        return carry

    def send_segment(segment):
        def body(step, carry):
            target = lax.rem(me + step, count)

            @pl.when(segment_of(target) == segment)
            def _():
                describe_first(target, me).start()

            return carry

        return body

    def finish_first(step, carry):
        target = lax.rem(me + step, count)
        source = lax.rem(me + count - step, count)
        describe_first(target, me).wait_send()
        describe_first(me, source).wait_recv()
        return carry

    lax.fori_loop(1, count, send_local, 0)
    for step in range(1, parts):
        describe_zero(step).wait_recv()
        lax.fori_loop(1, count, send_segment(lax.rem(col + parts - step, parts)), 0)
    for step in range(1, parts):
        describe_zero(step).wait_send()
    spread[me] = chunk_of(me)[...]
    lax.fori_loop(1, count, finish_first, 0)

    def pick(block, carry):
        for r in range(rounds):
            outgoing[block, r] = spread[plan_ref[r, block]]
        return carry

    lax.fori_loop(0, count, pick, 0)

    def round_of(order):
        return lax.rem(col + 1 + order, rounds)

    def describe_second(order, step):
        target = lax.rem(me + step, count)
        r = round_of(order)
        return pltpu.make_async_remote_copy(
            src_ref=outgoing.at[target, r],
            dst_ref=partner.at[me, r],
            send_sem=second_sems.at[order * count + step],
            recv_sem=second_sems.at[(rounds + order) * count + step],
            device_id=(target, col),
            device_id_type=mesh_ids,
        )

    for order in range(rounds):
        def send_second(step, carry, order=order):
            describe_second(order, step).start()
            return carry

        lax.fori_loop(1, count, send_second, 0)
    for r in range(rounds):
        partner[me, r] = outgoing[me, r]
    own_f[...] = own[...].astype(jnp.float32)
    bin_index = col * quarter + lax.broadcasted_iota(jnp.int32, (1, quarter), 1)
    weight = jnp.where(bin_index == 0, 1.0, 2.0).astype(jnp.float32)

    def describe_cross(order):
        target = round_of(order)
        return pltpu.make_async_remote_copy(
            src_ref=staged.at[order],
            dst_ref=out_ref.at[col],
            send_sem=cross_sems.at[order],
            recv_sem=cross_sems.at[rounds + order],
            device_id=(me, target),
            device_id_type=mesh_ids,
        )

    for order in range(rounds):
        def arrived(step, carry, order=order):
            describe_second(order, step).wait_recv()
            return carry

        lax.fori_loop(1, count, arrived, 0)
        r = round_of(order)
        if order < rounds - 1:
            cross_round(weight, own_f, partner, r, staged.at[order])
            describe_cross(order).start()
        else:
            cross_round(weight, own_f, partner, r, out_ref.at[col])

    for order in range(rounds):
        def sent(step, carry, order=order):
            describe_second(order, step).wait_send()
            return carry

        lax.fori_loop(1, count, sent, 0)
    for order in range(rounds - 1):
        describe_cross(order).wait_recv()
    for table in tables:
        table.wait()
    lag_phase(
        scaling, cos_ref, sin_ref, out_ref, lag_ref, lag_staged, lag_sends, lag_recvs, final_ref
    )
    for order in range(rounds - 1):
        describe_cross(order).wait_send()


def route_and_cross(scaling, plan, x, cos_table, sin_table, count, parts):
    channels, windows_dev, stations, bins = x.shape
    rounds = plan.shape[0]
    quarter = bins // parts
    windows = windows_dev * parts
    low = channels * windows * stations // count
    square = stations * stations
    chunk = LAGS // parts
    vmem = pl.BlockSpec(memory_space=pltpu.VMEM)
    hbm = pl.BlockSpec(memory_space=pl.ANY)
    return pl.pallas_call(
        functools.partial(route_kernel, scaling),
        in_specs=[pl.BlockSpec(memory_space=pltpu.SMEM), vmem, hbm, hbm],
        out_specs=vmem,
        out_shape=jax.ShapeDtypeStruct((chunk, rounds * square), jnp.float32),
        scratch_shapes=[
            pltpu.VMEM((rounds, chunk, square), x.dtype),
            pltpu.VMEM((parts, channels, square, quarter), x.dtype),
            pltpu.VMEM((channels, windows, stations, quarter), x.dtype),
            pltpu.VMEM((channels, windows, stations, quarter), jnp.float32),
            pltpu.VMEM((count, low, quarter), x.dtype),
            pltpu.VMEM((count, rounds, low, quarter), x.dtype),
            pltpu.VMEM((count, rounds, low, quarter), x.dtype),
            pltpu.VMEM((rounds - 1, channels, square, quarter), x.dtype),
            pltpu.VMEM((rounds - 1, chunk, square), x.dtype),
            pltpu.VMEM(cos_table.shape, cos_table.dtype),
            pltpu.VMEM(sin_table.shape, sin_table.dtype),
            pltpu.SemaphoreType.DMA((2,)),
            pltpu.SemaphoreType.DMA((2 * parts,)),
            pltpu.SemaphoreType.DMA((2 * count,)),
            pltpu.SemaphoreType.DMA((2 * rounds * count,)),
            pltpu.SemaphoreType.DMA((2 * rounds,)),
            pltpu.SemaphoreType.DMA((rounds,)),
            pltpu.SemaphoreType.DMA((rounds,)),
        ],
        compiler_params=pltpu.CompilerParams(collective_id=2, has_side_effects=True),
    )(plan, x, cos_table, sin_table)


def per_device(records, plan):
    stations_dev, windows, length = records.shape
    sta_devices = lax.axis_size("sta")
    seg_devices = lax.axis_size("seg")
    transform = 2 * length
    row_count = stations_dev * windows
    cos_table, sin_table = fourier_tables(length, NBIN, transform)
    signal = jnp.transpose(records, (1, 0, 2)).reshape(row_count, length)
    mean_level = band_mean(jnp.abs(signal).astype(jnp.bfloat16), HALF)
    flattened = (signal / (mean_level + 1e-05)).astype(jnp.bfloat16)
    spec_real = jnp.dot(flattened, cos_table, preferred_element_type=jnp.float32)
    spec_imag = jnp.dot(flattened, sin_table, preferred_element_type=jnp.float32)
    magnitude = jnp.sqrt(spec_real * spec_real + spec_imag * spec_imag).astype(jnp.bfloat16)
    smooth = band_mean(magnitude, HALF)
    whitened = jnp.stack(
        [spec_real / (smooth + 1e-06), spec_imag / (smooth + 1e-06)], axis=0
    ).astype(jnp.bfloat16)
    whitened = whitened.reshape(2, windows, stations_dev, NBIN)
    quarter = NBIN // seg_devices
    all_windows = windows * seg_devices
    first_bin = lax.axis_index("seg") * quarter
    bin_index = first_bin + jnp.arange(quarter, dtype=jnp.int32)
    scaling = 1.0 / math.sqrt(4.0 * NBIN * all_windows)
    lagged = route_and_cross(
        scaling, plan, whitened, cos_table, sin_table, sta_devices, seg_devices
    )
    return lagged.reshape(lagged.shape[0], ROUNDS, lagged.shape[1] // ROUNDS)


def solution(mesh):
    in_specs = (P("sta", "seg", None), P())
    out_specs = P("seg", None, "sta")
    return jax.shard_map(
        per_device, mesh=mesh, in_specs=in_specs, out_specs=out_specs, check_vma=False
    )
```
